32 devices in a mesh: fsdp: 4 (over z), ctx: 2 (over x), tp: 4 (over y, core).
Axes of the slice: x: 2, y: 2, z: 4, core: 2. Of those that a mesh axis runs over, the one named last changes fastest.
Arguments:
- tokens: bfloat16 [12288, 1024], P(('fsdp', 'ctx')), may hold values from -6 to 6
- out_grad: bfloat16 [12288, 1024], P(('fsdp', 'ctx')), may hold values from -6 to 6
- doc_ids: int32 [12288], P('fsdp'), may hold values from 0 to 23, never falling along the last dimension, each value on 1 to 1024 neighbouring positions
- block_ids: int32 [12288], P('fsdp'), may hold values from 0 to 63, never falling along the last dimension, each value on 1 to 256 neighbouring positions
- expert_ids: int32 [12288, 8], P(('fsdp', 'ctx')), may hold values from 0 to 31, all different within a row; in each aligned block of 1536 rows (0 to 1535, 1536 to 3071, ...) at most 576 rows name the same one
- norm1_gain: bfloat16 [1024], P('fsdp'), may hold values from 0.5 to 1.5
- w_query: bfloat16 [1024, 1024], P('fsdp', 'tp'), may hold values from -0.1875 to 0.1875
- w_key: bfloat16 [1024, 512], P('fsdp', 'tp'), may hold values from -0.1875 to 0.1875
- w_value: bfloat16 [1024, 512], P('fsdp', 'tp'), may hold values from -0.1875 to 0.1875
- w_out: bfloat16 [1024, 1024], P('tp', 'fsdp'), may hold values from -2 to 2
- norm2_gain: bfloat16 [1024], P('fsdp'), may hold values from 0.5 to 1.5
- w_router: bfloat16 [1024, 32], P('fsdp'), may hold values from -0.09375 to 0.09375
- w_gate: bfloat16 [32, 1024, 512], P(None, 'fsdp', 'tp'), may hold values from -0.1875 to 0.1875
- w_up: bfloat16 [32, 1024, 512], P(None, 'fsdp', 'tp'), may hold values from -0.1875 to 0.1875
- w_down: bfloat16 [32, 512, 1024], P(None, 'tp', 'fsdp'), may hold values from -1 to 1
Outputs:
- block_out: bfloat16 [12288, 1024], P(('fsdp', 'ctx'))
- input_grad: bfloat16 [12288, 1024], P(('fsdp', 'ctx'))
- grad_norm1: float32 [1024], P('fsdp')
- grad_query: float32 [1024, 1024], P('fsdp', 'tp')
- grad_key: float32 [1024, 512], P('fsdp', 'tp')
- grad_value: float32 [1024, 512], P('fsdp', 'tp')
- grad_out: float32 [1024, 1024], P('tp', 'fsdp')
- grad_norm2: float32 [1024], P('fsdp')
- grad_router: float32 [1024, 32], P('fsdp')
- grad_gate: float32 [32, 1024, 512], P(None, 'fsdp', 'tp')
- grad_up: float32 [32, 1024, 512], P(None, 'fsdp', 'tp')
- grad_down: float32 [32, 512, 1024], P(None, 'tp', 'fsdp')
The draws below stay inside these ranges and needn't reach their ends.
Inputs may be any that keep to these rules, and one draw needn't show every extreme that they name: `doc_ids`: never falls along the tokens; each document holds 1 to 1024 consecutive tokens. `block_ids`: never falls along the tokens; each block holds 1 to 256 consecutive tokens. `expert_ids`: the 8 experts of a token differ; in each aligned block of 1536 tokens (the tokens of one device) no expert is named more than 576 times, a bound that some block reaches.
All inputs are finite; a program needn't handle non-finite values.
Results may differ from the reference program's by a relative error of at most 0.017.
Values may be sent and summed in bfloat16 or wider, within the bound.
A program may use at most 448 MiB of HBM per device.

```python
import math
import jax
import jax.numpy as jnp
import numpy as np
from jax import lax

D = 1024
H = 16
KVH = 8
HD = 64
E = 32
TOP = 8
FF = 512
CT = 1536
BLK = 256
DOC = 1024
CAP = 576
LEN = 3072
TOKENS = 12288
N_FSDP = 4


def steps_of(key, dims, shards, smallest, high):
    def one(dim, parts):
        heights = jax.random.uniform(jax.random.fold_in(jax.random.fold_in(key, 6), dim), (parts,), jnp.float32, smallest / len(shards), high / len(shards))
        return jnp.repeat(jnp.exp(heights), dims[dim] // parts).reshape((-1,) + (1,) * (len(dims) - dim - 1))

    factor_of = one(*shards[0])
    for cut in shards[1:]:
        factor_of = factor_of * one(*cut)
    return factor_of


def length_profile(amount, total, reach, skew):
    loads = [(1 << 20) // math.isqrt(rank ** skew) + 1 for rank in range(2, amount + 1)]
    spare, holding = total - reach - (amount - 1), [1] * (amount - 1)
    while spare > 0:
        candidates = [i for i in range(amount - 1) if holding[i] < reach]
        whole, remaining = sum([loads[i] for i in candidates]), spare
        for i in candidates:
            extra = min(reach - holding[i], max(1, remaining * loads[i] // whole), spare)
            holding[i] = holding[i] + extra
            spare = spare - extra
    return np.array([reach] + holding)


def ragged_sizes(own_key, amount, total, reach, slope):
    if amount == 2:
        one = jax.random.randint(own_key, (), max(1, total - reach), min(reach, total - 1) + 1)
        return jnp.stack([one, total - one])
    sizes = jnp.asarray(length_profile(amount, total, reach, slope), jnp.int32)
    couples = (amount - 1) // 2
    donor, taker = sizes[1:1 + 2 * couples:2], sizes[2:2 + 2 * couples:2]
    room = jnp.minimum(donor - 1, reach - taker)
    moved = jax.random.randint(jax.random.fold_in(own_key, 1), (couples,), 0, 1 << 20) % (room + 1)
    sizes = sizes.at[1:1 + 2 * couples:2].set(donor - moved).at[2:2 + 2 * couples:2].set(taker + moved)
    return sizes[jax.random.permutation(jax.random.fold_in(own_key, 2), amount)]


def routed_block(rng, own, number, rows, count, top, reach, slope):
    order = jax.random.permutation(rng, count)
    packed, common = shares(count, rows * top, reach, slope, True), shares(count, rows * top, reach, slope, False)
    places = jnp.arange(count)

    def named(tallies, rotation):
        used = int((tallies > 0).sum())
        fixed = max(1, used // 4)
        shifted = fixed + (places - fixed + rotation * (used - fixed)) % max(1, count - fixed)
        return jnp.zeros((count,), jnp.int32).at[order[jnp.where(places < fixed, places, shifted)]].set(jnp.asarray(tallies, jnp.int32))

    tallies = jnp.where(number % 4 == 0, named(packed, number // 4), named(common, number - number // 4 - 1))
    mixed = jax.random.permutation(jax.random.fold_in(own, 3), count)
    donor, receiver = mixed[0:count // 2 * 2:2], mixed[1:count // 2 * 2:2]
    slack = jnp.minimum(tallies[donor] - 1, reach - tallies[receiver]) // 2
    slack = jnp.where((donor == order[0]) | (receiver == order[0]) | (tallies[receiver] == 0), 0, jnp.maximum(slack, 0))
    shifted = jax.random.randint(jax.random.fold_in(own, 4), (count // 2,), 0, 1 << 20) % (slack + 1)
    tallies = tallies.at[donor].add(-shifted).at[receiver].add(shifted)
    members = jnp.searchsorted(jnp.cumsum(tallies), jnp.arange(rows * top), side="right").astype(jnp.int32)
    grid = members.reshape(top, rows).T
    grid = grid[jax.random.permutation(jax.random.fold_in(own, 1), rows)]
    rotation = jax.random.randint(jax.random.fold_in(own, 2), (rows, 1), 0, top)
    return jnp.take_along_axis(grid, (jnp.arange(top)[None, :] + rotation) % top, axis=1)


def shares(count, total, limit, lean, full):
    portions = [(1 << 20) // math.isqrt(grade ** lean) + 1 for grade in range(1, count + 1)]
    largest = limit if full else min(limit, max(-(-total // count), total * portions[0] // sum(portions)))
    least = 1 if total - largest >= count - 1 else 0
    holding, spare = [largest] + [least] * (count - 1), total - largest - least * (count - 1)
    while spare > 0:
        free = [i for i in range(1, count) if holding[i] < largest] or [i for i in range(1, count) if holding[i] < limit]
        whole, remaining = sum([portions[i] for i in free]), spare
        for i in free:
            more = min(limit - holding[i], max(1, remaining * portions[i] // whole), spare)
            holding[i] = holding[i] + more
            spare = spare - more
    return np.array(holding)


def scatter_about(key, shape, scale, reach, shards=(), kind=jnp.bfloat16):
    gain = steps_of(key, shape, shards, -0.22, 0.18) if shards else 1.0
    values = jax.random.normal(key, shape, jnp.float32) * scale * gain
    return jnp.minimum(jnp.maximum(values, -reach), reach).astype(kind)


def setup_inputs(seed: int = 0) -> dict:
    key_of = jax.random.split(jax.random.key(seed), 16)
    tokens = scatter_about(key_of[0], (TOKENS, D), 1.0, 6.0, ((0, 8),))
    out_grad = scatter_about(key_of[1], (TOKENS, D), 1.0, 6.0, ((0, 8),))
    doc_ids = jnp.searchsorted(jnp.cumsum(ragged_sizes(key_of[2], TOKENS // (DOC // 2), TOKENS, DOC, 0)), jnp.arange(TOKENS), side="right").astype(jnp.int32)
    block_ids = jnp.searchsorted(jnp.cumsum(ragged_sizes(key_of[3], TOKENS // (BLK * 3 // 4), TOKENS, BLK, 0)), jnp.arange(TOKENS), side="right").astype(jnp.int32)
    expert_ids_keys = jax.random.split(jax.random.fold_in(key_of[4], 1), TOKENS // CT)
    expert_ids_turns = jax.random.permutation(jax.random.fold_in(key_of[4], 3), TOKENS // CT)
    expert_ids = jax.vmap(lambda own, number: routed_block(jax.random.fold_in(key_of[4], 2), own, number, CT, E, TOP, CAP, 1))(expert_ids_keys, expert_ids_turns).reshape((TOKENS, TOP))
    norm1_gain = jnp.clip(1.0 + 0.1 * jax.random.normal(key_of[5], (D,), jnp.float32), 0.5, 1.5).astype(jnp.bfloat16)
    w_query = scatter_about(key_of[6], (D, H * HD), D ** -0.5, 0.1875, ((0, 4), (1, 4)))
    w_key = scatter_about(key_of[7], (D, KVH * HD), D ** -0.5, 0.1875, ((0, 4), (1, 4)))
    w_value = scatter_about(key_of[8], (D, KVH * HD), D ** -0.5, 0.1875, ((0, 4), (1, 4)))
    w_out = scatter_about(key_of[9], (H * HD, D), (max(H * HD // 128, 1)) ** -0.5, 2.0, ((0, 4), (1, 4)))
    norm2_gain = jnp.clip(1.0 + 0.1 * jax.random.normal(key_of[10], (D,), jnp.float32), 0.5, 1.5).astype(jnp.bfloat16)
    w_router = scatter_about(key_of[11], (D, E), (4 * D) ** -0.5, 0.09375, ((0, 4),))
    w_gate = scatter_about(key_of[12], (E, D, FF), D ** -0.5, 0.1875, ((1, 4), (2, 4)))
    w_up = scatter_about(key_of[13], (E, D, FF), D ** -0.5, 0.1875, ((1, 4), (2, 4)))
    w_down = scatter_about(key_of[14], (E, FF, D), (max(FF // 16, 1)) ** -0.5, 1.0, ((1, 4), (2, 4)))
    return {"tokens": tokens, "out_grad": out_grad, "doc_ids": doc_ids, "block_ids": block_ids, "expert_ids": expert_ids, "norm1_gain": norm1_gain, "w_query": w_query, "w_key": w_key, "w_value": w_value, "w_out": w_out, "norm2_gain": norm2_gain, "w_router": w_router, "w_gate": w_gate, "w_up": w_up, "w_down": w_down}


epsilon = 1e-06
rope_base = 10000.0
masked_score = -1e+30
highest = lax.Precision.HIGHEST

@jax.custom_vjp
def low(v):
    return lax.optimization_barrier(v.astype(jnp.bfloat16)).astype(jnp.float32)

@jax.custom_vjp
def low_back(v):
    return v

def low_keep(v):
    return (low(v), None)

def low_pass(kept, grad):
    return (grad,)

def back_keep(v):
    return (v, None)

def back_low(kept, grad):
    return (low(grad),)
low.defvjp(low_keep, low_pass)
low_back.defvjp(back_keep, back_low)

def rope_angles(positions, head_size):
    half_size = head_size // 2
    frequency = rope_base ** (-2.0 * jnp.arange(half_size, dtype=jnp.float32) / head_size)
    angles = positions.astype(jnp.float32)[:, None] * frequency[None, :]
    return (jnp.cos(angles), jnp.sin(angles))

def rotate(values, cosine, sine_table, head_size):
    row_count = values.shape[0]
    shaped = values.reshape(row_count, -1, head_size)
    half_size = head_size // 2
    first_half = shaped[:, :, :half_size]
    second_half = shaped[:, :, half_size:]
    cos_rows = cosine[:, None, :]
    sin_rows = sine_table[:, None, :]
    turned = jnp.concatenate([first_half * cos_rows - second_half * sin_rows, second_half * cos_rows + first_half * sin_rows], axis=2)
    return turned.reshape(row_count, -1)

def matmul(left_mat, right_mat):
    return jnp.dot(left_mat, right_mat, precision=highest, preferred_element_type=jnp.float32)

def slot_numbers(block_experts):
    flat_ids = block_experts.reshape(-1)
    flat_hot = (flat_ids[:, None] == jnp.arange(E, dtype=jnp.int32)[None, :]).astype(jnp.int32)
    running = jnp.cumsum(flat_hot, axis=0)
    return (flat_ids * CAP + lax.optimization_barrier(jnp.sum(running * flat_hot, axis=1)) - 1).astype(jnp.int32)

def reference(tokens, out_grad, doc_ids, block_ids, expert_ids, norm1_gain, w_query, w_key, w_value, w_out, norm2_gain, w_router, w_gate, w_up, w_down):
    doc_seq = doc_ids.reshape(N_FSDP, LEN)
    block_seq = block_ids.reshape(N_FSDP, LEN)
    expert_blocks = expert_ids.reshape(TOKENS // CT, CT, TOP)
    slot_blocks = lax.map(slot_numbers, expert_blocks)
    cosine, sine_table = rope_angles(jnp.arange(LEN, dtype=jnp.int32), HD)
    score_scale = HD ** (-0.5)

    def forward(inputs, gain_first, query_w, key_w, value_w, out_w, gain_second, router_w, gate_w, up_w, down_w):

        def attend(pieces):
            seq_in, seq_doc, seq_block = pieces
            rms_row = lax.rsqrt(lax.optimization_barrier(jnp.mean(seq_in * seq_in, axis=1, keepdims=True)) + epsilon)
            normed = low(seq_in * rms_row * gain_first)
            queries = low(rotate(low_back(matmul(normed, query_w)), cosine, sine_table, HD))
            keys = low(rotate(low_back(matmul(normed, key_w)), cosine, sine_table, HD))
            values = low(low_back(matmul(normed, value_w)))
            grouped = queries.reshape(LEN, KVH, H // KVH, HD)
            keyed = keys.reshape(LEN, KVH, HD)
            scores = low_back(jnp.einsum('qgrd,kgd->grqk', grouped, keyed, precision=highest) * score_scale)
            allowed = (seq_doc[:, None] == seq_doc[None, :]) & (seq_block[None, :] <= seq_block[:, None])
            scores = jnp.where(allowed[None, None], scores, masked_score)
            prob_table = low(jax.nn.softmax(scores, axis=-1))
            mixed = jnp.einsum('grqk,kgd->qgrd', prob_table, values.reshape(LEN, KVH, HD), precision=highest).reshape(LEN, H * HD)
            mixed = low(low_back(mixed))
            return seq_in + low_back(matmul(mixed, out_w))
        hidden = lax.map(jax.checkpoint(attend), (inputs.reshape(N_FSDP, LEN, D), doc_seq, block_seq)).reshape(TOKENS, D)

        def experts(pieces):
            block_in, block_experts, block_slots = pieces
            rms_row = lax.rsqrt(lax.optimization_barrier(jnp.mean(block_in * block_in, axis=1, keepdims=True)) + epsilon)
            normed = low(block_in * rms_row * gain_second)
            logits = low_back(matmul(normed, router_w))
            chosen = jnp.take_along_axis(logits, block_experts, axis=1)
            gate_probs = jax.nn.softmax(chosen, axis=1)
            buffer = jnp.zeros((E * CAP, D), jnp.float32).at[block_slots].set(jnp.repeat(normed, TOP, axis=0)).reshape(E, CAP, D)
            gate_val = low_back(jnp.einsum('ecd,edf->ecf', buffer, gate_w, precision=highest))
            up_val = low_back(jnp.einsum('ecd,edf->ecf', buffer, up_w, precision=highest))
            inner_act = low(jax.nn.silu(gate_val) * up_val)
            result = low_back(jnp.einsum('ecf,efd->ecd', inner_act, down_w, precision=highest)).reshape(E * CAP, D)
            picked = result[block_slots].reshape(CT, TOP, D)
            return block_in + lax.optimization_barrier(jnp.sum(picked * gate_probs[:, :, None], axis=1))
        outputs = lax.map(jax.checkpoint(experts), (hidden.reshape(TOKENS // CT, CT, D), expert_blocks, slot_blocks))
        return outputs.reshape(TOKENS, D)
    block_result, pullback = jax.vjp(forward, tokens.astype(jnp.float32), norm1_gain.astype(jnp.float32), w_query.astype(jnp.float32), w_key.astype(jnp.float32), w_value.astype(jnp.float32), w_out.astype(jnp.float32), norm2_gain.astype(jnp.float32), w_router.astype(jnp.float32), w_gate.astype(jnp.float32), w_up.astype(jnp.float32), w_down.astype(jnp.float32))
    gradients = pullback(out_grad.astype(jnp.float32))
    return (block_result.astype(jnp.bfloat16), gradients[0].astype(jnp.bfloat16), gradients[1], gradients[2], gradients[3], gradients[4], gradients[5], gradients[6], gradients[7], gradients[8], gradients[9], gradients[10])
```

```python
import functools
import jax
import jax.numpy as jnp
from jax import lax
from jax.experimental import pallas as pl
from jax.experimental.pallas import tpu as pltpu

HD = 64
DOC = 1024
BLK = 256
QB = 256
BAND = DOC + 2 * BLK
masked_score = -1e30
epsilon = 1e-06
VL = 60 * 1024 * 1024

def nt(a, b):
    return lax.dot_general(a, b, (((1,), (1,)), ((), ())), preferred_element_type=jnp.float32)

def tn(a, b):
    return lax.dot_general(a, b, (((0,), (0,)), ((), ())), preferred_element_type=jnp.float32)

def nn(a, b):
    return jnp.dot(a, b, preferred_element_type=jnp.float32)

def band_start(row, length):
    return pl.multiple_of(jnp.clip(row - DOC, 0, length - BAND), QB)

def flash_fwd_body(base_ref, q_ref, k_ref, v_ref, docq_ref, blkq_ref, dock_ref, blkk_ref, o_ref, *, share, length):
    step = pl.program_id(0)
    start = band_start(base_ref[0] + step * QB, length)
    keys = pl.ds(start, BAND)
    dock = dock_ref[:, keys]
    blkk = blkk_ref[:, keys]
    ok = (docq_ref[...] == dock) & (blkk <= blkq_ref[...])
    bias = jnp.where(ok, 0.0, masked_score)
    for head in range(q_ref.shape[0]):
        s = nt(q_ref[head], k_ref[head // share, keys, :]) + bias
        top = jnp.max(s, axis=1, keepdims=True)
        e = jnp.exp(s - top)
        p = e * (1.0 / jnp.sum(e, axis=1, keepdims=True))
        o_ref[head] = nn(p.astype(jnp.bfloat16), v_ref[head // share, keys, :]).astype(jnp.bfloat16)

def flash_fwd(base, q, k, v, docq, blkq, dock, blkk):
    heads, rows, _ = q.shape
    kv, length, _ = k.shape
    full = lambda shape: pl.BlockSpec(shape, lambda i, b: (0,) * len(shape))
    return pl.pallas_call(
        functools.partial(flash_fwd_body, share=heads // kv, length=length),
        grid_spec=pltpu.PrefetchScalarGridSpec(
            num_scalar_prefetch=1, grid=(rows // QB,),
            in_specs=[
                pl.BlockSpec((heads, QB, HD), lambda i, b: (0, i, 0)),
                full(k.shape), full(v.shape),
                pl.BlockSpec((QB, 1), lambda i, b: (i, 0)),
                pl.BlockSpec((QB, 1), lambda i, b: (i, 0)),
                full((1, length)), full((1, length)),
            ],
            out_specs=pl.BlockSpec((heads, QB, HD), lambda i, b: (0, i, 0)),
        ),
        out_shape=jax.ShapeDtypeStruct(q.shape, jnp.bfloat16),
        compiler_params=pltpu.CompilerParams(vmem_limit_bytes=VL),
        name="flash_fwd",
    )(base, q, k, v, docq, blkq, dock, blkk)

def flash_bwd_body(base_ref, q_ref, g_ref, k_ref, v_ref, docq_ref, blkq_ref, dock_ref, blkk_ref, dq_ref, dk_ref, dv_ref, *, share, length):
    step = pl.program_id(0)
    start = band_start(base_ref[0] + step * QB, length)
    keys = pl.ds(start, BAND)

    @pl.when(step == 0)
    def _():
        dk_ref[...] = jnp.zeros_like(dk_ref)
        dv_ref[...] = jnp.zeros_like(dv_ref)

    ok = (docq_ref[...] == dock_ref[keys, :]) & (blkk_ref[keys, :] <= blkq_ref[...])
    bias = jnp.where(ok, 0.0, masked_score)
    for head in range(q_ref.shape[0]):
        kvh = head // share
        q = q_ref[head]
        g = g_ref[head]
        k = k_ref[kvh, keys, :]
        s = nt(k, q) + bias
        e = jnp.exp(s - jnp.max(s, axis=0, keepdims=True))
        p = e * (1.0 / jnp.sum(e, axis=0, keepdims=True))
        dp = nt(v_ref[kvh, keys, :], g)
        delta = jnp.sum(dp * p, axis=0, keepdims=True)
        ds = (p * (dp - delta)).astype(jnp.bfloat16)
        dq_ref[head] = tn(ds, k)
        dk_ref[kvh, keys, :] += nn(ds, q)
        dv_ref[kvh, keys, :] += nn(p.astype(jnp.bfloat16), g)

def flash_bwd(base, q, g, k, v, docq, blkq, dock, blkk):
    heads, rows, _ = q.shape
    kv, length, _ = k.shape
    full = lambda shape: pl.BlockSpec(shape, lambda i, b: (0,) * len(shape))
    return pl.pallas_call(
        functools.partial(flash_bwd_body, share=heads // kv, length=length),
        grid_spec=pltpu.PrefetchScalarGridSpec(
            num_scalar_prefetch=1, grid=(rows // QB,),
            in_specs=[
                pl.BlockSpec((heads, QB, HD), lambda i, b: (0, i, 0)),
                pl.BlockSpec((heads, QB, HD), lambda i, b: (0, i, 0)),
                full(k.shape), full(v.shape),
                pl.BlockSpec((1, QB), lambda i, b: (0, i)),
                pl.BlockSpec((1, QB), lambda i, b: (0, i)),
                full((length, 1)), full((length, 1)),
            ],
            out_specs=[
                pl.BlockSpec((heads, QB, HD), lambda i, b: (0, i, 0)),
                full(k.shape), full(v.shape),
            ],
        ),
        out_shape=[
            jax.ShapeDtypeStruct(q.shape, jnp.float32),
            jax.ShapeDtypeStruct(k.shape, jnp.float32),
            jax.ShapeDtypeStruct(v.shape, jnp.float32),
        ],
        compiler_params=pltpu.CompilerParams(vmem_limit_bytes=VL),
        name="flash_bwd",
    )(base, q, g, k, v, docq, blkq, dock, blkk)

PAIR = 2
TM = 512

def moe_body(x_ref, g_ref, xt_ref, gt_ref, gates_ref, w_ref, a_ref, gu_ref, grads_ref, dots_ref):
    rows, width = x_ref.shape
    shards, _, pair, part, ff = w_ref.shape
    step = pl.program_id(0)

    def weights(which):
        return jnp.concatenate(
            [jnp.concatenate([w_ref[z, which, e] for z in range(shards)], axis=0) for e in range(pair)], axis=1
        )

    gate_w = weights(0)
    up_w = weights(1)
    down_w = weights(2)
    experts = gates_ref.shape[1]

    def tile(i, carry):
        here = pl.ds(pl.multiple_of(i * TM, TM), TM)
        x = x_ref[here, :]
        gate_val = nn(x, gate_w)
        up_val = nn(x, up_w)
        back = nn(g_ref[here, :], down_w)
        lanes = lax.broadcasted_iota(jnp.int32, (TM, experts), 1)
        gates = gates_ref[here, :]
        gate = jnp.concatenate(
            [
                jnp.broadcast_to(
                    jnp.sum(jnp.where(lanes == step * pair + e, gates, 0.0), axis=1, keepdims=True), (TM, ff)
                )
                for e in range(pair)
            ],
            axis=1,
        )
        sig = 1.0 / (1.0 + jnp.exp(-gate_val))
        silu = gate_val * sig
        inner = silu * up_val
        a_ref[here, :] = (inner * gate).astype(jnp.bfloat16)
        prod = inner * back
        for e in range(pair):
            dots_ref[0, here, e : e + 1] = jnp.sum(prod[:, e * ff : (e + 1) * ff], axis=1, keepdims=True)
        back = back * gate
        gu_ref[here, : pair * ff] = (back * up_val * sig * (1.0 + gate_val * (1.0 - sig))).astype(jnp.bfloat16)
        gu_ref[here, pair * ff :] = (back * silu).astype(jnp.bfloat16)
        return carry

    lax.fori_loop(0, rows // TM, tile, 0)
    for z in range(shards):
        part_rows = pl.ds(z * part, part)
        both = nn(xt_ref[part_rows, :], gu_ref[...])
        down = nn(gt_ref[part_rows, :], a_ref[...])
        for e in range(pair):
            grads_ref[z, 0, e] = both[:, e * ff : (e + 1) * ff].astype(jnp.bfloat16)
            grads_ref[z, 1, e] = both[:, (pair + e) * ff : (pair + e + 1) * ff].astype(jnp.bfloat16)
            grads_ref[z, 2, e] = down[:, e * ff : (e + 1) * ff].astype(jnp.bfloat16)

def moe_main(x, g, xt, gt, gates, w):
    rows, width = x.shape
    shards, three, count, part, ff = w.shape
    one = lambda shape: pl.BlockSpec(shape, lambda i: (0,) * len(shape), pipeline_mode=pl.Buffered(1))
    return pl.pallas_call(
        moe_body,
        grid=(count // PAIR,),
        in_specs=[
            one(x.shape), one(g.shape), one(xt.shape), one(gt.shape), one(gates.shape),
            pl.BlockSpec((shards, 3, PAIR, part, ff), lambda i: (0, 0, i, 0, 0)),
        ],
        out_specs=[
            pl.BlockSpec((rows, PAIR * ff), lambda i: (0, i)),
            pl.BlockSpec((rows, 2 * PAIR * ff), lambda i: (0, i)),
            pl.BlockSpec((shards, 3, PAIR, part, ff), lambda i: (0, 0, i, 0, 0)),
            pl.BlockSpec((1, rows, PAIR), lambda i: (i, 0, 0)),
        ],
        out_shape=[
            jax.ShapeDtypeStruct((rows, count * ff), jnp.bfloat16),
            jax.ShapeDtypeStruct((rows, 2 * count * ff), jnp.bfloat16),
            jax.ShapeDtypeStruct(w.shape, jnp.bfloat16),
            jax.ShapeDtypeStruct((count // PAIR, rows, PAIR), jnp.float32),
        ],
        compiler_params=pltpu.CompilerParams(vmem_limit_bytes=VL),
        cost_estimate=pl.CostEstimate(flops=2 * rows * width * count * ff * 6, bytes_accessed=8 * rows * width + 12 * count * ff * width, transcendentals=0),
        name="moe_main",
    )(x, g, xt, gt, gates, w)

def back_body(*refs, count, first, kinds):
    gu_refs, w_refs, o_ref = refs[:count], refs[count : 2 * count], refs[2 * count]
    shards, _, experts, part, ff = w_refs[0].shape
    for z in range(shards):
        total = None
        for gu_ref, w_ref in zip(gu_refs, w_refs):
            w = jnp.concatenate(
                [
                    w_ref[z, kind, p * PAIR + e]
                    for p in range(experts // PAIR)
                    for kind in range(kinds)
                    for e in range(PAIR)
                ],
                axis=1,
            )
            piece = nt(gu_ref[...], w)
            total = piece if total is None else total + piece
        o_ref[:, z * part : (z + 1) * part] = total.astype(o_ref.dtype)


def moe_back(gus, ws, first, kinds):
    shards, three, experts, part, ff = ws[0].shape
    rows = gus[0].shape[0]
    width = shards * part
    count = len(gus)
    return pl.pallas_call(
        functools.partial(back_body, count=count, first=first, kinds=kinds),
        grid=(rows // TM,),
        in_specs=[pl.BlockSpec((TM, kinds * experts * ff), lambda i: (i, 0)) for _ in gus]
        + [
            pl.BlockSpec(
                (shards, kinds, experts, part, ff),
                lambda i: (0, first // kinds, 0, 0, 0),
                pipeline_mode=pl.Buffered(1),
            )
            for _ in ws
        ],
        out_specs=pl.BlockSpec((TM, width), lambda i: (i, 0)),
        out_shape=jax.ShapeDtypeStruct((rows, width), jnp.bfloat16),
        compiler_params=pltpu.CompilerParams(vmem_limit_bytes=VL),
        cost_estimate=pl.CostEstimate(
            flops=2 * rows * width * count * experts * ff * kinds,
            bytes_accessed=2 * rows * kinds * count * experts * ff,
            transcendentals=0,
        ),
        name="moe_back" if kinds == 2 else "moe_out",
    )(*gus, *ws)


MESH = pl.DeviceIdType.MESH


class Place:
    def __init__(self):
        self.ctx = lax.axis_index("ctx")
        self.tp = lax.axis_index("tp")
        self.core = lax.rem(self.tp, 2)
        self.high = self.tp // 2
        self.pair_tp = self.high * 2 + 1 - self.core
        self.far_tp = (1 - self.high) * 2 + self.core
        self.cross_tp = (1 - self.high) * 2 + 1 - self.core
        self.pair = {"tp": self.pair_tp}
        self.far = {"tp": self.far_tp}
        self.side = {"ctx": 1 - self.ctx}

    def meet(self, who):
        barrier = pltpu.get_barrier_semaphore()
        for device in who:
            pl.semaphore_signal(barrier, inc=1, device_id=device, device_id_type=MESH)
        pl.semaphore_wait(barrier, len(who))


def push(src, dst, sems, slot, device):
    return pltpu.make_async_remote_copy(
        src_ref=src, dst_ref=dst, send_sem=sems.at[0, slot], recv_sem=sems.at[1, slot],
        device_id=device, device_id_type=MESH,
    )


def gather_four(place, all_ref, sems, at):
    here, far = all_ref.at[place.tp], all_ref.at[place.far_tp]
    to_far = push(here, here, sems, at, place.far)
    to_pair = push(here, here, sems, at + 1, place.pair)
    to_far.start()
    to_pair.start()
    to_far.wait_recv()
    on = push(far, far, sems, at + 2, place.pair)
    on.start()
    to_pair.wait_recv()
    on.wait_recv()
    to_far.wait_send()
    to_pair.wait_send()
    on.wait_send()


def gather_eight(place, all_ref, sems, at):
    rows = all_ref.shape[1]
    top, low = pl.ds(0, rows // 2), pl.ds(rows // 2, rows // 2)
    part = lambda ctx, tp: all_ref.at[ctx * 4 + tp]
    other = 1 - place.ctx
    here = part(place.ctx, place.tp)
    side = part(other, place.tp)
    far = part(place.ctx, place.far_tp)
    cross = part(other, place.far_tp)
    side_top, far_low = side.at[top], far.at[low]
    cross_top, cross_low = cross.at[top], cross.at[low]
    to_side = push(here, here, sems, at, place.side)
    to_far = push(here, here, sems, at + 1, place.far)
    to_pair = push(here, here, sems, at + 2, place.pair)
    for copy in (to_side, to_far, to_pair):
        copy.start()
    to_side.wait_recv()
    turn_far = push(side_top, side_top, sems, at + 3, place.far)
    pair_side = push(side, side, sems, at + 5, place.pair)
    turn_far.start()
    pair_side.start()
    to_far.wait_recv()
    turn_side = push(far_low, far_low, sems, at + 4, place.side)
    pair_far = push(far, far, sems, at + 6, place.pair)
    turn_side.start()
    pair_far.start()
    turn_far.wait_recv()
    pair_top = push(cross_top, cross_top, sems, at + 7, place.pair)
    pair_top.start()
    turn_side.wait_recv()
    pair_low = push(cross_low, cross_low, sems, at + 8, place.pair)
    pair_low.start()
    for copy in (to_pair, pair_side, pair_far, pair_top, pair_low):
        copy.wait_recv()
    for copy in (to_side, to_far, to_pair, turn_far, turn_side, pair_side, pair_far, pair_top, pair_low):
        copy.wait_send()


def reduce_four(place, produce, send_ref, pair_in, far_in, own_ref, sems, at):
    def fold(j):
        slot = j // 2

        @pl.when(lax.rem(j, 2) == place.core)
        def _():
            push(send_ref.at[j], pair_in.at[slot], sems, at + slot, place.pair).wait_recv()
            total = send_ref[j].astype(jnp.float32) + pair_in[slot].astype(jnp.float32)

            @pl.when(slot == place.high)
            def _():
                own_ref[...] = total

            @pl.when(slot != place.high)
            def _():
                send_ref[j] = total.astype(jnp.bfloat16)
                push(send_ref.at[j], far_in, sems, at + 2, place.far).start()

    def step(j, carry):
        produce(j)

        @pl.when(lax.rem(j, 2) != place.core)
        def _():
            slot = j // 2
            push(send_ref.at[j], pair_in.at[slot], sems, at + slot, place.pair).start()

        @pl.when(j > 0)
        def _():
            fold(j - 1)

        return carry

    lax.fori_loop(0, 4, step, 0)
    fold(3)
    last = push(send_ref.at[place.far_tp], far_in, sems, at + 2, place.far)
    last.wait_recv()
    own_ref[...] += far_in[...].astype(jnp.float32)
    last.wait_send()
    for slot in range(2):
        push(send_ref.at[place.pair_tp], pair_in.at[slot], sems, at + slot, place.pair).wait_send()


SMEMS = pl.BlockSpec(memory_space=pltpu.SMEM)
WHOLE = pl.BlockSpec(memory_space=pltpu.VMEM)


def normalize(x):
    r = lax.rsqrt(jnp.mean(x * x, axis=1, keepdims=True) + epsilon)
    return r, x * r


def mid_body(tok_ref, q_ref, k_ref, v_ref, docq_ref, blkq_ref, dock_ref, blkk_ref, w_ref, gain_ref,
             mix_ref, hid_ref, all_ref, send, pair_in, far_in, own, sems, *, share, length):
    place = Place()
    place.meet((place.pair, place.far, place.side))
    heads, rows, _ = q_ref.shape
    block = rows // 4
    band = min(DOC + block + BLK, length)

    def produce(j):
        at = pl.multiple_of(j * block, block)
        here = pl.ds(at, block)
        start = pl.multiple_of(jnp.clip(place.ctx * rows + at - DOC, 0, length - band), 128)
        keys = pl.ds(start, band)
        ok = (docq_ref[here, :] == dock_ref[:, keys]) & (blkk_ref[:, keys] <= blkq_ref[here, :])
        bias = jnp.where(ok, 0.0, masked_score)
        outs = []
        for head in range(heads):
            s = nt(q_ref[head, here, :], k_ref[head // share, keys, :]) + bias
            e = jnp.exp(s - jnp.max(s, axis=1, keepdims=True))
            p = e * (1.0 / jnp.sum(e, axis=1, keepdims=True))
            outs.append(nn(p.astype(jnp.bfloat16), v_ref[head // share, keys, :]).astype(jnp.bfloat16))
        mix = jnp.concatenate(outs, axis=1)
        mix_ref[here, :] = mix
        send[j] = nt(mix, w_ref[...]).astype(jnp.bfloat16)

    reduce_four(place, produce, send, pair_in, far_in, own, sems, 0)
    hidden = tok_ref[...].astype(jnp.float32) + own[...]
    hid_ref[...] = hidden
    all_ref[place.ctx * 4 + place.tp] = (normalize(hidden)[1] * gain_ref[...]).astype(jnp.bfloat16)
    gather_eight(place, all_ref, sems, 3)


def mid(tok, q, k, v, docq, blkq, dock, blkk, out_w, gain):
    heads, rows, _ = q.shape
    kv, length, _ = k.shape
    own, width = tok.shape
    return pl.pallas_call(
        functools.partial(mid_body, share=heads // kv, length=length),
        in_specs=[WHOLE] * 10,
        out_specs=[WHOLE] * 3,
        out_shape=[
            jax.ShapeDtypeStruct((rows, heads * HD), jnp.bfloat16),
            jax.ShapeDtypeStruct((own, width), jnp.float32),
            jax.ShapeDtypeStruct((8, own, width), jnp.bfloat16),
        ],
        scratch_shapes=[
            pltpu.VMEM((4, own, width), jnp.bfloat16),
            pltpu.VMEM((2, own, width), jnp.bfloat16),
            pltpu.VMEM((own, width), jnp.bfloat16),
            pltpu.VMEM((own, width), jnp.float32),
            pltpu.SemaphoreType.DMA((2, 12)),
        ],
        compiler_params=pltpu.CompilerParams(vmem_limit_bytes=VL, collective_id=0, has_side_effects=True),
        name="mid",
    )(tok, q, k, v, docq, blkq, dock, blkk, out_w, gain)


def tail_body(tok_ref, hg_ref, lin_ref, w_ref, gain_ref, all_ref, gg_ref, send, pair_in, far_in, own, sems):
    place = Place()
    place.meet((place.pair, place.far))
    block = lin_ref.shape[0] // 4

    def produce(j):
        here = pl.ds(pl.multiple_of(j * block, block), block)
        send[j] = nt(lin_ref[here, :], w_ref[...]).astype(jnp.bfloat16)

    reduce_four(place, produce, send, pair_in, far_in, own, sems, 0)
    one_grad = own[...]
    r, xhat = normalize(tok_ref[...].astype(jnp.float32))
    gg_ref[...] = jnp.sum(one_grad * xhat, axis=0, keepdims=True)
    n = one_grad * gain_ref[...]
    grad = hg_ref[...] + r * (n - xhat * jnp.mean(n * xhat, axis=1, keepdims=True))
    all_ref[place.tp] = grad.astype(jnp.bfloat16)
    gather_four(place, all_ref, sems, 3)


def tail(tok, hidden_grad, lin_grad, qkv_w, gain):
    own, width = tok.shape
    return pl.pallas_call(
        tail_body,
        in_specs=[WHOLE] * 5,
        out_specs=[WHOLE] * 2,
        out_shape=[
            jax.ShapeDtypeStruct((4, own, width), jnp.bfloat16),
            jax.ShapeDtypeStruct((1, width), jnp.float32),
        ],
        scratch_shapes=[
            pltpu.VMEM((4, own, width), jnp.bfloat16),
            pltpu.VMEM((2, own, width), jnp.bfloat16),
            pltpu.VMEM((own, width), jnp.bfloat16),
            pltpu.VMEM((own, width), jnp.float32),
            pltpu.SemaphoreType.DMA((2, 6)),
        ],
        compiler_params=pltpu.CompilerParams(vmem_limit_bytes=VL, collective_id=1, has_side_effects=True),
        name="tail",
    )(tok, hidden_grad, lin_grad, qkv_w, gain)


def turn_body(*refs, count, kinds, first, finish):
    gu_refs, w_refs = refs[:count], refs[count : 2 * count]
    lg_ref, router_ref, hid_ref, extra_ref, gain_ref = refs[2 * count : 2 * count + 5]
    outs = refs[2 * count + 5 : 2 * count + 8]
    gu_buf, gu_sem, give, keep, pair_in, cut, own, sems = refs[2 * count + 8 :]
    all_ref = outs[0]
    place = Place()
    place.meet((place.pair, place.far, place.side))
    block = hid_ref.shape[0]
    shards, _, experts, part, ff = w_refs[0].shape
    half = block // 2
    top, low = pl.ds(0, half), pl.ds(half, half)
    bf = jnp.bfloat16
    f = jnp.float32
    order = [(1, 1), (1, 0), (0, 1), (0, 0)]

    def tile_of(step):
        dx, dy = order[step // 2]
        ctx = place.ctx + dx * (1 - 2 * place.ctx)
        high = place.high + dy * (1 - 2 * place.high)
        core = 1 - place.core if step % 2 == 0 else place.core
        return ctx * 4 + high * 2 + core

    def fetch(step):
        at = pl.ds(pl.multiple_of(tile_of(step) * block, block), block)
        return [
            pltpu.make_async_copy(gu.at[at, :], gu_buf.at[step % 2, n], gu_sem.at[step % 2, n])
            for n, gu in enumerate(gu_refs)
        ]

    for copy in fetch(0):
        copy.start()

    def compute(step, dst):
        for copy in fetch(step):
            copy.wait()
        if step + 1 < 8:
            for copy in fetch(step + 1):
                copy.start()
        at = pl.ds(pl.multiple_of(tile_of(step) * block, block), block)
        for z in range(shards):
            cols = slice(z * part, (z + 1) * part)
            total = None
            if lg_ref is not None:
                total = nt(lg_ref[at, :], router_ref[cols, :])
            for n, w_ref in enumerate(w_refs):
                w = jnp.concatenate(
                    [
                        w_ref[z, kind, p * PAIR + e]
                        for p in range(experts // PAIR)
                        for kind in range(kinds)
                        for e in range(PAIR)
                    ],
                    axis=1,
                )
                piece = nt(gu_buf[step % 2, n], w)
                total = piece if total is None else total + piece
            dst[:, cols] = total.astype(bf)

    copies = []

    def send(src, dst, slot, device):
        copy = push(src, dst, sems, slot, device)
        copy.start()
        copies.append(copy)
        return copy

    for k in range(4):
        compute(2 * k, give.at[k])
        got = send(give.at[k], pair_in.at[k], k, place.pair)
        compute(2 * k + 1, keep.at[k])
        got.wait_recv()
        total = keep[k].astype(f) + pair_in[k].astype(f)
        if k == 0:
            keep[k] = total.astype(bf)
            a_cross = send(keep.at[k, top], cut.at[0], 4, place.side)
            b_cross = send(keep.at[k, low], cut.at[1], 5, place.far)
        elif k == 1:
            b_cross.wait_recv()
            keep[k, top] = total[:half].astype(bf)
            keep[k, low] = (total[half:] + cut[1].astype(f)).astype(bf)
            a_first = send(keep.at[k, top], cut.at[2], 6, place.side)
            b_last = send(keep.at[k, low], cut.at[5], 9, place.side)
        elif k == 2:
            a_cross.wait_recv()
            keep[k, low] = total[half:].astype(bf)
            keep[k, top] = (total[:half] + cut[0].astype(f)).astype(bf)
            b_first = send(keep.at[k, low], cut.at[4], 8, place.far)
            a_last = send(keep.at[k, top], cut.at[3], 7, place.far)
        else:
            for copy in (a_first, a_last, b_first, b_last):
                copy.wait_recv()
            own[top, :] = total[:half] + cut[2].astype(f) + cut[3].astype(f)
            own[low, :] = total[half:] + cut[4].astype(f) + cut[5].astype(f)
    finish(place, own, hid_ref, extra_ref, gain_ref, outs)
    gather_four(place, all_ref, sems, 10)
    for copy in copies:
        copy.wait_send()


def turn_back(place, own, hid_ref, grad_ref, gain_ref, outs):
    all_ref, hg_ref, gg_ref = outs
    two_grad = own[...]
    r, hhat = normalize(hid_ref[...])
    gg_ref[...] = jnp.sum(two_grad * hhat, axis=0, keepdims=True)
    m = two_grad * gain_ref[...]
    grad = grad_ref[...].astype(jnp.float32) + r * (m - hhat * jnp.mean(m * hhat, axis=1, keepdims=True))
    hg_ref[...] = grad
    all_ref[place.tp] = grad.astype(jnp.bfloat16)


def turn(gus, ws, logit_grad, router_w, hidden, grad_own, gain):
    shards, _, experts, part, ff = ws[0].shape
    own, width = hidden.shape
    count = len(gus)
    kinds = 2
    cols = gus[0].shape[1]
    anys = pl.BlockSpec(memory_space=pl.ANY)
    return pl.pallas_call(
        functools.partial(turn_body, count=count, kinds=kinds, first=0, finish=turn_back),
        grid=(1,),
        in_specs=[anys] * count
        + [
            pl.BlockSpec((shards, kinds, experts, part, ff), lambda i: (0, 0, 0, 0, 0), pipeline_mode=pl.Buffered(1))
            for _ in ws
        ]
        + [WHOLE] * 5,
        out_specs=[WHOLE] * 3,
        out_shape=[
            jax.ShapeDtypeStruct((4, own, width), jnp.bfloat16),
            jax.ShapeDtypeStruct((own, width), jnp.float32),
            jax.ShapeDtypeStruct((1, width), jnp.float32),
        ],
        scratch_shapes=[
            pltpu.VMEM((2, count, own, cols), jnp.bfloat16),
            pltpu.SemaphoreType.DMA((2, count)),
            pltpu.VMEM((4, own, width), jnp.bfloat16),
            pltpu.VMEM((4, own, width), jnp.bfloat16),
            pltpu.VMEM((4, own, width), jnp.bfloat16),
            pltpu.VMEM((6, own // 2, width), jnp.bfloat16),
            pltpu.VMEM((own, width), jnp.float32),
            pltpu.SemaphoreType.DMA((2, 13)),
        ],
        compiler_params=pltpu.CompilerParams(vmem_limit_bytes=VL, collective_id=2, has_side_effects=True),
        name="turn",
    )(*gus, *ws, logit_grad, router_w, hidden, grad_own, gain)


from jax.sharding import PartitionSpec as P

rope_base = 10000.0
CHUNKS = 4
bf16 = jnp.bfloat16
f32 = jnp.float32


def rope_tables(positions):
    half = HD // 2
    frequency = rope_base ** (-2.0 * jnp.arange(half, dtype=f32) / HD)
    angles = positions.astype(f32)[:, None] * frequency[None, :]
    return jnp.cos(angles)[:, None, :], jnp.sin(angles)[:, None, :]


def rotate(values, cosine, sine):
    shaped = values.reshape(values.shape[0], -1, HD)
    a, b = shaped[:, :, : HD // 2], shaped[:, :, HD // 2 :]
    return jnp.concatenate([a * cosine - b * sine, b * cosine + a * sine], axis=2)


def per_device(
    tokens, out_grad, doc_ids, block_ids, expert_ids, norm1_gain, w_query, w_key, w_value, w_out,
    norm2_gain, w_router, w_gate, w_up, w_down,
):
    shards = lax.axis_size("fsdp")
    ctx_size = lax.axis_size("ctx")
    tp_size = lax.axis_size("tp")
    ctx = lax.axis_index("ctx")
    tp = lax.axis_index("tp")
    rows, width = tokens.shape
    part = width // shards
    own = rows // tp_size
    length = doc_ids.shape[0]
    q_width, kv_width = w_query.shape[1], w_key.shape[1]
    heads, kv_heads = q_width // HD, kv_width // HD
    experts = w_gate.shape[0]
    mine = experts // ctx_size
    each = mine // CHUNKS
    ff = w_gate.shape[2]

    small = jnp.concatenate([w_router, norm1_gain[:, None], norm2_gain[:, None]], axis=1)
    spare = -small.shape[1] % 128
    packed = jnp.concatenate(
        [w_query, w_key, w_value, w_out.T, small, jnp.zeros((part, spare), bf16)], axis=1
    )
    packed = lax.all_gather(packed, "fsdp", axis=0, tiled=True)
    qkv_w = packed[:, : q_width + 2 * kv_width]
    at = q_width + 2 * kv_width
    out_w = packed[:, at : at + q_width]
    at += q_width
    router_w = packed[:, at : at + experts]
    gain_one = packed[:, at + experts].astype(f32)
    gain_two = packed[:, at + experts + 1].astype(f32)

    stacked = []
    for chunk in range(CHUNKS):
        first = ctx * mine + chunk * each
        pick = lambda w: lax.dynamic_slice_in_dim(w, first, each, 0)
        shard = jnp.stack([pick(w_gate), pick(w_up), pick(w_down).transpose(0, 2, 1)])
        stacked.append(lax.all_gather(shard, "fsdp", axis=0))
    grad_all = lax.all_gather(out_grad, "ctx", axis=0, tiled=True)
    ids_all = lax.all_gather(expert_ids, "ctx", axis=0, tiled=True)

    inputs = tokens.astype(f32)
    rms_one = lax.rsqrt(jnp.mean(inputs * inputs, axis=1, keepdims=True) + epsilon)
    normed = (inputs * rms_one * gain_one).astype(bf16)
    start = ctx * rows
    cosine, sine = rope_tables(start + jnp.arange(rows, dtype=jnp.int32))
    lin = jnp.dot(normed, qkv_w, preferred_element_type=f32)
    turned = rotate(lin[:, : q_width + kv_width], cosine, sine).astype(bf16)
    queries = turned[:, :heads].transpose(1, 0, 2) * bf16(HD**-0.5)
    keys_values = jnp.concatenate(
        [turned[:, heads:], lin[:, q_width + kv_width :].astype(bf16).reshape(rows, kv_heads, HD)], axis=1
    ).reshape(rows, 2 * kv_width)
    keys_values = lax.all_gather(keys_values, "ctx", axis=0, tiled=True)
    keys_values = keys_values.reshape(length, 2 * kv_heads, HD).transpose(1, 0, 2)
    keys, values = keys_values[:kv_heads], keys_values[kv_heads:]
    query_doc = lax.dynamic_slice_in_dim(doc_ids, start, rows)
    query_block = lax.dynamic_slice_in_dim(block_ids, start, rows)
    base = start.astype(jnp.int32).reshape(1)
    tokens_own = lax.dynamic_slice_in_dim(tokens, tp * own, own)
    grad_own = lax.dynamic_slice_in_dim(out_grad, tp * own, own)
    attn_mix, hidden, normed_two = mid(
        tokens_own, queries, keys, values, query_doc[:, None], query_block[:, None], doc_ids[None],
        block_ids[None], out_w, gain_two[None],
    )
    normed_two = normed_two.reshape(ctx_size * rows, width)

    logits = jnp.dot(normed_two, router_w, preferred_element_type=f32)
    chosen = jnp.any(ids_all[:, :, None] == jnp.arange(experts, dtype=jnp.int32)[None, None, :], axis=1)
    masked = jnp.where(chosen, logits, masked_score)
    powers = jnp.exp(masked - jnp.max(masked, axis=1, keepdims=True))
    gates = powers / jnp.sum(powers, axis=1, keepdims=True)
    gates_mine = lax.dynamic_slice_in_dim(gates, ctx * mine, mine, 1)

    normed_t, grad_t = normed_two.T, grad_all.T
    inner_all, outer_all, dots_all, shard_grads = [], [], [], []
    for chunk in range(CHUNKS):
        inner, outer, grads, dots = moe_main(
            normed_two, grad_all, normed_t, grad_t,
            gates_mine[:, chunk * each : (chunk + 1) * each], stacked[chunk],
        )
        inner_all.append(inner)
        outer_all.append(outer)
        dots_all.append(dots)
        scattered = lax.psum_scatter(grads, "fsdp", scatter_dimension=0, tiled=False)
        shard_grads.append(lax.all_gather(scattered, "ctx", axis=0))
    combined = moe_back(inner_all, stacked, 2, 1)

    dots = jnp.concatenate(dots_all, axis=0).transpose(1, 0, 2).reshape(ctx_size * rows, mine)
    weighted = gates_mine * dots
    dots_sum = jnp.sum(weighted, axis=1, keepdims=True)
    spread = lax.dynamic_update_slice_in_dim(jnp.zeros_like(gates), weighted, ctx * mine, 1)
    logit_grad = (spread - gates * dots_sum).astype(bf16)
    router_grad = lax.dot_general(
        normed_two, logit_grad, (((0,), (0,)), ((), ())), preferred_element_type=f32
    )
    branch_grad, hidden_grad, gain_two_grad = turn(
        outer_all, stacked, logit_grad, router_w, hidden, grad_own, gain_two[None]
    )
    branch_grad = branch_grad.reshape(rows, width)
    mixed = lax.psum_scatter(combined, ("ctx", "tp"), scatter_dimension=0, tiled=True)
    block_out = lax.all_gather((hidden + mixed.astype(f32)).astype(bf16), "tp", axis=0, tiled=True)

    out_w_grad = lax.dot_general(
        branch_grad, attn_mix, (((0,), (0,)), ((), ())), preferred_element_type=f32
    )
    mix_grad = jnp.dot(branch_grad, out_w, preferred_element_type=f32).astype(bf16)
    query_grad, key_grad, value_grad = flash_bwd(
        base, queries, mix_grad.reshape(rows, heads, HD).transpose(1, 0, 2), keys, values,
        query_doc[None], query_block[None], doc_ids[:, None], block_ids[:, None],
    )
    kv_grad = jnp.concatenate([key_grad, value_grad], axis=0).transpose(1, 0, 2).reshape(length, 2 * kv_width)
    kv_grad = lax.psum_scatter(kv_grad.astype(bf16), "ctx", scatter_dimension=0, tiled=True).astype(f32)
    query_grad = (query_grad * HD**-0.5).transpose(1, 0, 2).reshape(rows, q_width)
    turned_grad = rotate(
        jnp.concatenate([query_grad, kv_grad[:, :kv_width]], axis=1), cosine, -sine
    ).reshape(rows, q_width + kv_width)
    lin_grad = jnp.concatenate([turned_grad, kv_grad[:, kv_width:]], axis=1).astype(bf16)
    qkv_grad = lax.dot_general(normed, lin_grad, (((0,), (0,)), ((), ())), preferred_element_type=f32)

    input_grad, gain_one_grad = tail(tokens_own, hidden_grad, lin_grad, qkv_w, gain_one[None])
    input_grad = input_grad.reshape(rows, width)

    big = jnp.concatenate([qkv_grad, out_w_grad], axis=1).astype(bf16)
    big = lax.psum_scatter(big, "fsdp", scatter_dimension=0, tiled=True)
    big = lax.psum(big, "ctx").astype(f32)
    tiny = jnp.concatenate(
        [router_grad, gain_one_grad[0][:, None], gain_two_grad[0][:, None]], axis=1
    )
    tiny = lax.psum(lax.psum_scatter(tiny, "fsdp", scatter_dimension=0, tiled=True), ("ctx", "tp"))

    sums = jnp.stack(shard_grads, axis=1).astype(f32)
    gate_s, up_s, down_s = [sums[:, :, kind].reshape(experts, part, ff) for kind in range(3)]
    at = q_width + 2 * kv_width
    return (
        block_out,
        input_grad,
        tiny[:, experts],
        big[:, :q_width],
        big[:, q_width : q_width + kv_width],
        big[:, q_width + kv_width : at],
        big[:, at : at + q_width].T,
        tiny[:, experts + 1],
        tiny[:, :experts],
        gate_s,
        up_s,
        down_s.transpose(0, 2, 1),
    )


def solution(mesh):
    rows = P(("fsdp", "ctx"), None)
    return jax.shard_map(
        per_device,
        mesh=mesh,
        in_specs=(
            rows, rows, P("fsdp"), P("fsdp"), rows, P("fsdp"), P("fsdp", "tp"), P("fsdp", "tp"),
            P("fsdp", "tp"), P("tp", "fsdp"), P("fsdp"), P("fsdp", None), P(None, "fsdp", "tp"),
            P(None, "fsdp", "tp"), P(None, "tp", "fsdp"),
        ),
        out_specs=(
            rows, rows, P("fsdp"), P("fsdp", "tp"), P("fsdp", "tp"), P("fsdp", "tp"), P("tp", "fsdp"),
            P("fsdp"), P("fsdp", None), P(None, "fsdp", "tp"), P(None, "fsdp", "tp"), P(None, "tp", "fsdp"),
        ),
        check_vma=False,
    )
```

```python
import functools
import jax
import jax.numpy as jnp
from jax import lax
from jax.experimental import pallas as pl
from jax.experimental.pallas import tpu as pltpu

HD = 64
DOC = 1024
BLK = 256
QB = 256
BAND = DOC + 2 * BLK
masked_score = -1e30
epsilon = 1e-06
VL = 60 * 1024 * 1024

def nt(a, b):
    return lax.dot_general(a, b, (((1,), (1,)), ((), ())), preferred_element_type=jnp.float32)

def tn(a, b):
    return lax.dot_general(a, b, (((0,), (0,)), ((), ())), preferred_element_type=jnp.float32)

def nn(a, b):
    return jnp.dot(a, b, preferred_element_type=jnp.float32)

def band_start(row, length):
    return pl.multiple_of(jnp.clip(row - DOC, 0, length - BAND), QB)

def flash_fwd_body(base_ref, q_ref, k_ref, v_ref, docq_ref, blkq_ref, dock_ref, blkk_ref, o_ref, *, share, length):
    step = pl.program_id(0)
    start = band_start(base_ref[0] + step * QB, length)
    keys = pl.ds(start, BAND)
    dock = dock_ref[:, keys]
    blkk = blkk_ref[:, keys]
    ok = (docq_ref[...] == dock) & (blkk <= blkq_ref[...])
    bias = jnp.where(ok, 0.0, masked_score)
    for head in range(q_ref.shape[0]):
        s = nt(q_ref[head], k_ref[head // share, keys, :]) + bias
        top = jnp.max(s, axis=1, keepdims=True)
        e = jnp.exp(s - top)
        p = e * (1.0 / jnp.sum(e, axis=1, keepdims=True))
        o_ref[head] = nn(p.astype(jnp.bfloat16), v_ref[head // share, keys, :]).astype(jnp.bfloat16)

def flash_fwd(base, q, k, v, docq, blkq, dock, blkk):
    heads, rows, _ = q.shape
    kv, length, _ = k.shape
    full = lambda shape: pl.BlockSpec(shape, lambda i, b: (0,) * len(shape))
    return pl.pallas_call(
        functools.partial(flash_fwd_body, share=heads // kv, length=length),
        grid_spec=pltpu.PrefetchScalarGridSpec(
            num_scalar_prefetch=1, grid=(rows // QB,),
            in_specs=[
                pl.BlockSpec((heads, QB, HD), lambda i, b: (0, i, 0)),
                full(k.shape), full(v.shape),
                pl.BlockSpec((QB, 1), lambda i, b: (i, 0)),
                pl.BlockSpec((QB, 1), lambda i, b: (i, 0)),
                full((1, length)), full((1, length)),
            ],
            out_specs=pl.BlockSpec((heads, QB, HD), lambda i, b: (0, i, 0)),
        ),
        out_shape=jax.ShapeDtypeStruct(q.shape, jnp.bfloat16),
        compiler_params=pltpu.CompilerParams(vmem_limit_bytes=VL),
        name="flash_fwd",
    )(base, q, k, v, docq, blkq, dock, blkk)

def flash_bwd_body(base_ref, q_ref, g_ref, k_ref, v_ref, docq_ref, blkq_ref, dock_ref, blkk_ref, dq_ref, dk_ref, dv_ref, *, share, length):
    step = pl.program_id(0)
    start = band_start(base_ref[0] + step * QB, length)
    keys = pl.ds(start, BAND)

    @pl.when(step == 0)
    def _():
        dk_ref[...] = jnp.zeros_like(dk_ref)
        dv_ref[...] = jnp.zeros_like(dv_ref)

    ok = (docq_ref[...] == dock_ref[keys, :]) & (blkk_ref[keys, :] <= blkq_ref[...])
    bias = jnp.where(ok, 0.0, masked_score)
    for head in range(q_ref.shape[0]):
        kvh = head // share
        q = q_ref[head]
        g = g_ref[head]
        k = k_ref[kvh, keys, :]
        s = nt(k, q) + bias
        e = jnp.exp(s - jnp.max(s, axis=0, keepdims=True))
        p = e * (1.0 / jnp.sum(e, axis=0, keepdims=True))
        dp = nt(v_ref[kvh, keys, :], g)
        delta = jnp.sum(dp * p, axis=0, keepdims=True)
        ds = (p * (dp - delta)).astype(jnp.bfloat16)
        dq_ref[head] = tn(ds, k)
        dk_ref[kvh, keys, :] += nn(ds, q)
        dv_ref[kvh, keys, :] += nn(p.astype(jnp.bfloat16), g)

def flash_bwd(base, q, g, k, v, docq, blkq, dock, blkk):
    heads, rows, _ = q.shape
    kv, length, _ = k.shape
    full = lambda shape: pl.BlockSpec(shape, lambda i, b: (0,) * len(shape))
    return pl.pallas_call(
        functools.partial(flash_bwd_body, share=heads // kv, length=length),
        grid_spec=pltpu.PrefetchScalarGridSpec(
            num_scalar_prefetch=1, grid=(rows // QB,),
            in_specs=[
                pl.BlockSpec((heads, QB, HD), lambda i, b: (0, i, 0)),
                pl.BlockSpec((heads, QB, HD), lambda i, b: (0, i, 0)),
                full(k.shape), full(v.shape),
                pl.BlockSpec((1, QB), lambda i, b: (0, i)),
                pl.BlockSpec((1, QB), lambda i, b: (0, i)),
                full((length, 1)), full((length, 1)),
            ],
            out_specs=[
                pl.BlockSpec((heads, QB, HD), lambda i, b: (0, i, 0)),
                full(k.shape), full(v.shape),
            ],
        ),
        out_shape=[
            jax.ShapeDtypeStruct(q.shape, jnp.float32),
            jax.ShapeDtypeStruct(k.shape, jnp.float32),
            jax.ShapeDtypeStruct(v.shape, jnp.float32),
        ],
        compiler_params=pltpu.CompilerParams(vmem_limit_bytes=VL),
        cost_estimate=busy(55),
        name="flash_bwd",
    )(base, q, g, k, v, docq, blkq, dock, blkk)

PAIR = 2
TM = 512

def moe_body(x_ref, g_ref, xt_ref, gt_ref, gates_ref, w_ref, a_ref, gu_ref, grads_ref, dots_ref):
    rows, width = x_ref.shape
    shards, _, pair, part, ff = w_ref.shape
    step = pl.program_id(0)

    def weights(which):
        return jnp.concatenate(
            [jnp.concatenate([w_ref[z, which, e] for z in range(shards)], axis=0) for e in range(pair)], axis=1
        )

    gate_w = weights(0)
    up_w = weights(1)
    down_w = weights(2)
    experts = gates_ref.shape[1]

    def tile(i, carry):
        here = pl.ds(pl.multiple_of(i * TM, TM), TM)
        x = x_ref[here, :]
        gate_val = nn(x, gate_w)
        up_val = nn(x, up_w)
        back = nn(g_ref[here, :], down_w)
        lanes = lax.broadcasted_iota(jnp.int32, (TM, experts), 1)
        gates = gates_ref[here, :]
        gate = jnp.concatenate(
            [
                jnp.broadcast_to(
                    jnp.sum(jnp.where(lanes == step * pair + e, gates, 0.0), axis=1, keepdims=True), (TM, ff)
                )
                for e in range(pair)
            ],
            axis=1,
        )
        sig = 1.0 / (1.0 + jnp.exp(-gate_val))
        silu = gate_val * sig
        inner = silu * up_val
        a_ref[here, :] = (inner * gate).astype(jnp.bfloat16)
        prod = inner * back
        for e in range(pair):
            dots_ref[0, here, e : e + 1] = jnp.sum(prod[:, e * ff : (e + 1) * ff], axis=1, keepdims=True)
        back = back * gate
        gu_ref[here, : pair * ff] = (back * up_val * sig * (1.0 + gate_val * (1.0 - sig))).astype(jnp.bfloat16)
        gu_ref[here, pair * ff :] = (back * silu).astype(jnp.bfloat16)
        return carry

    lax.fori_loop(0, rows // TM, tile, 0)
    for z in range(shards):
        part_rows = pl.ds(z * part, part)
        both = nn(xt_ref[part_rows, :], gu_ref[...])
        down = nn(gt_ref[part_rows, :], a_ref[...])
        for e in range(pair):
            grads_ref[z, 0, e] = both[:, e * ff : (e + 1) * ff].astype(jnp.bfloat16)
            grads_ref[z, 1, e] = both[:, (pair + e) * ff : (pair + e + 1) * ff].astype(jnp.bfloat16)
            grads_ref[z, 2, e] = down[:, e * ff : (e + 1) * ff].astype(jnp.bfloat16)

def moe_main(x, g, xt, gt, gates, w):
    rows, width = x.shape
    shards, three, count, part, ff = w.shape
    one = lambda shape: pl.BlockSpec(shape, lambda i: (0,) * len(shape), pipeline_mode=pl.Buffered(1))
    return pl.pallas_call(
        moe_body,
        grid=(count // PAIR,),
        in_specs=[
            one(x.shape), one(g.shape), one(xt.shape), one(gt.shape), one(gates.shape),
            pl.BlockSpec((shards, 3, PAIR, part, ff), lambda i: (0, 0, i, 0, 0)),
        ],
        out_specs=[
            pl.BlockSpec((rows, PAIR * ff), lambda i: (0, i)),
            pl.BlockSpec((rows, 2 * PAIR * ff), lambda i: (0, i)),
            pl.BlockSpec((shards, 3, PAIR, part, ff), lambda i: (0, 0, i, 0, 0)),
            pl.BlockSpec((1, rows, PAIR), lambda i: (i, 0, 0)),
        ],
        out_shape=[
            jax.ShapeDtypeStruct((rows, count * ff), jnp.bfloat16),
            jax.ShapeDtypeStruct((rows, 2 * count * ff), jnp.bfloat16),
            jax.ShapeDtypeStruct(w.shape, jnp.bfloat16),
            jax.ShapeDtypeStruct((count // PAIR, rows, PAIR), jnp.float32),
        ],
        compiler_params=pltpu.CompilerParams(vmem_limit_bytes=VL),
        cost_estimate=pl.CostEstimate(flops=2 * rows * width * count * ff * 6, bytes_accessed=8 * rows * width + 12 * count * ff * width, transcendentals=0),
        name="moe_main",
    )(x, g, xt, gt, gates, w)

def back_body(*refs, count, first, kinds):
    gu_refs, w_refs, o_ref = refs[:count], refs[count : 2 * count], refs[2 * count]
    shards, _, experts, part, ff = w_refs[0].shape
    for z in range(shards):
        total = None
        for gu_ref, w_ref in zip(gu_refs, w_refs):
            w = jnp.concatenate(
                [
                    w_ref[z, kind, p * PAIR + e]
                    for p in range(experts // PAIR)
                    for kind in range(kinds)
                    for e in range(PAIR)
                ],
                axis=1,
            )
            piece = nt(gu_ref[...], w)
            total = piece if total is None else total + piece
        o_ref[:, z * part : (z + 1) * part] = total.astype(o_ref.dtype)


def moe_back(gus, ws, first, kinds):
    shards, three, experts, part, ff = ws[0].shape
    rows = gus[0].shape[0]
    width = shards * part
    count = len(gus)
    return pl.pallas_call(
        functools.partial(back_body, count=count, first=first, kinds=kinds),
        grid=(rows // TM,),
        in_specs=[pl.BlockSpec((TM, kinds * experts * ff), lambda i: (i, 0)) for _ in gus]
        + [
            pl.BlockSpec(
                (shards, kinds, experts, part, ff),
                lambda i: (0, first // kinds, 0, 0, 0),
                pipeline_mode=pl.Buffered(1),
            )
            for _ in ws
        ],
        out_specs=pl.BlockSpec((TM, width), lambda i: (i, 0)),
        out_shape=jax.ShapeDtypeStruct((rows, width), jnp.bfloat16),
        compiler_params=pltpu.CompilerParams(vmem_limit_bytes=VL),
        cost_estimate=pl.CostEstimate(
            flops=2 * rows * width * count * experts * ff * kinds,
            bytes_accessed=2 * rows * kinds * count * experts * ff,
            transcendentals=0,
        ),
        name="moe_back" if kinds == 2 else "moe_out",
    )(*gus, *ws)


MESH = pl.DeviceIdType.MESH


class Place:
    def __init__(self):
        self.ctx = lax.axis_index("ctx")
        self.tp = lax.axis_index("tp")
        self.core = lax.rem(self.tp, 2)
        self.high = self.tp // 2
        self.pair_tp = self.high * 2 + 1 - self.core
        self.far_tp = (1 - self.high) * 2 + self.core
        self.cross_tp = (1 - self.high) * 2 + 1 - self.core
        self.pair = {"tp": self.pair_tp}
        self.far = {"tp": self.far_tp}
        self.side = {"ctx": 1 - self.ctx}

    def meet(self, who):
        barrier = pltpu.get_barrier_semaphore()
        for device in who:
            pl.semaphore_signal(barrier, inc=1, device_id=device, device_id_type=MESH)
        pl.semaphore_wait(barrier, len(who))


def push(src, dst, sems, slot, device):
    return pltpu.make_async_remote_copy(
        src_ref=src, dst_ref=dst, send_sem=sems.at[0, slot], recv_sem=sems.at[1, slot],
        device_id=device, device_id_type=MESH,
    )


def gather_four(place, all_ref, sems, at):
    here, far = all_ref.at[place.tp], all_ref.at[place.far_tp]
    to_far = push(here, here, sems, at, place.far)
    to_pair = push(here, here, sems, at + 1, place.pair)
    to_far.start()
    to_pair.start()
    to_far.wait_recv()
    on = push(far, far, sems, at + 2, place.pair)
    on.start()
    to_pair.wait_recv()
    on.wait_recv()
    to_far.wait_send()
    to_pair.wait_send()
    on.wait_send()


def gather_eight(place, all_ref, sems, at):
    rows = all_ref.shape[1]
    top, low = pl.ds(0, rows // 2), pl.ds(rows // 2, rows // 2)
    part = lambda ctx, tp: all_ref.at[ctx * 4 + tp]
    other = 1 - place.ctx
    here = part(place.ctx, place.tp)
    side = part(other, place.tp)
    far = part(place.ctx, place.far_tp)
    cross = part(other, place.far_tp)
    side_top, far_low = side.at[top], far.at[low]
    cross_top, cross_low = cross.at[top], cross.at[low]
    to_side = push(here, here, sems, at, place.side)
    to_far = push(here, here, sems, at + 1, place.far)
    to_pair = push(here, here, sems, at + 2, place.pair)
    for copy in (to_side, to_far, to_pair):
        copy.start()
    to_side.wait_recv()
    turn_far = push(side_top, side_top, sems, at + 3, place.far)
    pair_side = push(side, side, sems, at + 5, place.pair)
    turn_far.start()
    pair_side.start()
    to_far.wait_recv()
    turn_side = push(far_low, far_low, sems, at + 4, place.side)
    pair_far = push(far, far, sems, at + 6, place.pair)
    turn_side.start()
    pair_far.start()
    turn_far.wait_recv()
    pair_top = push(cross_top, cross_top, sems, at + 7, place.pair)
    pair_top.start()
    turn_side.wait_recv()
    pair_low = push(cross_low, cross_low, sems, at + 8, place.pair)
    pair_low.start()
    for copy in (to_pair, pair_side, pair_far, pair_top, pair_low):
        copy.wait_recv()
    for copy in (to_side, to_far, to_pair, turn_far, turn_side, pair_side, pair_far, pair_top, pair_low):
        copy.wait_send()


def reduce_four(place, produce, send_ref, pair_in, far_in, own_ref, sems, at):
    def fold(j):
        slot = j // 2

        @pl.when(lax.rem(j, 2) == place.core)
        def _():
            push(send_ref.at[j], pair_in.at[slot], sems, at + slot, place.pair).wait_recv()
            total = send_ref[j].astype(jnp.float32) + pair_in[slot].astype(jnp.float32)

            @pl.when(slot == place.high)
            def _():
                own_ref[...] = total

            @pl.when(slot != place.high)
            def _():
                send_ref[j] = total.astype(jnp.bfloat16)
                push(send_ref.at[j], far_in, sems, at + 2, place.far).start()

    def step(j, carry):
        produce(j)

        @pl.when(lax.rem(j, 2) != place.core)
        def _():
            slot = j // 2
            push(send_ref.at[j], pair_in.at[slot], sems, at + slot, place.pair).start()

        @pl.when(j > 0)
        def _():
            fold(j - 1)

        return carry

    lax.fori_loop(0, 4, step, 0)
    fold(3)
    last = push(send_ref.at[place.far_tp], far_in, sems, at + 2, place.far)
    last.wait_recv()
    own_ref[...] += far_in[...].astype(jnp.float32)
    last.wait_send()
    for slot in range(2):
        push(send_ref.at[place.pair_tp], pair_in.at[slot], sems, at + slot, place.pair).wait_send()


SMEMS = pl.BlockSpec(memory_space=pltpu.SMEM)
WHOLE = pl.BlockSpec(memory_space=pltpu.VMEM)


def normalize(x):
    r = lax.rsqrt(jnp.mean(x * x, axis=1, keepdims=True) + epsilon)
    return r, x * r


def mid_body(tok_ref, q_ref, k_ref, v_ref, docq_ref, blkq_ref, dock_ref, blkk_ref, w_ref, gain_ref,
             mix_ref, hid_ref, all_ref, send, pair_in, far_in, own, sems, *, share, length):
    place = Place()
    place.meet((place.pair, place.far, place.side))
    heads, rows, _ = q_ref.shape
    block = rows // 4
    band = min(DOC + block + BLK, length)

    def produce(j):
        at = pl.multiple_of(j * block, block)
        here = pl.ds(at, block)
        start = pl.multiple_of(jnp.clip(place.ctx * rows + at - DOC, 0, length - band), 128)
        keys = pl.ds(start, band)
        ok = (docq_ref[here, :] == dock_ref[:, keys]) & (blkk_ref[:, keys] <= blkq_ref[here, :])
        bias = jnp.where(ok, 0.0, masked_score)
        outs = []
        for head in range(heads):
            s = nt(q_ref[head, here, :], k_ref[head // share, keys, :]) + bias
            e = jnp.exp(s - jnp.max(s, axis=1, keepdims=True))
            p = e * (1.0 / jnp.sum(e, axis=1, keepdims=True))
            outs.append(nn(p.astype(jnp.bfloat16), v_ref[head // share, keys, :]).astype(jnp.bfloat16))
        mix = jnp.concatenate(outs, axis=1)
        mix_ref[here, :] = mix
        send[j] = nt(mix, w_ref[...]).astype(jnp.bfloat16)

    reduce_four(place, produce, send, pair_in, far_in, own, sems, 0)
    hidden = tok_ref[...].astype(jnp.float32) + own[...]
    hid_ref[...] = hidden
    all_ref[place.ctx * 4 + place.tp] = (normalize(hidden)[1] * gain_ref[...]).astype(jnp.bfloat16)
    gather_eight(place, all_ref, sems, 3)


def mid(tok, q, k, v, docq, blkq, dock, blkk, out_w, gain):
    heads, rows, _ = q.shape
    kv, length, _ = k.shape
    own, width = tok.shape
    return pl.pallas_call(
        functools.partial(mid_body, share=heads // kv, length=length),
        in_specs=[WHOLE] * 10,
        out_specs=[WHOLE] * 3,
        out_shape=[
            jax.ShapeDtypeStruct((rows, heads * HD), jnp.bfloat16),
            jax.ShapeDtypeStruct((own, width), jnp.float32),
            jax.ShapeDtypeStruct((8, own, width), jnp.bfloat16),
        ],
        scratch_shapes=[
            pltpu.VMEM((4, own, width), jnp.bfloat16),
            pltpu.VMEM((2, own, width), jnp.bfloat16),
            pltpu.VMEM((own, width), jnp.bfloat16),
            pltpu.VMEM((own, width), jnp.float32),
            pltpu.SemaphoreType.DMA((2, 12)),
        ],
        compiler_params=pltpu.CompilerParams(vmem_limit_bytes=VL, collective_id=0, has_side_effects=True),
        cost_estimate=busy(100),
        name="mid",
    )(tok, q, k, v, docq, blkq, dock, blkk, out_w, gain)


def tail_body(tok_ref, hg_ref, lin_ref, w_ref, gain_ref, all_ref, gg_ref, send, pair_in, far_in, own, sems):
    place = Place()
    place.meet((place.pair, place.far))
    block = lin_ref.shape[0] // 4

    def produce(j):
        here = pl.ds(pl.multiple_of(j * block, block), block)
        send[j] = nt(lin_ref[here, :], w_ref[...]).astype(jnp.bfloat16)

    reduce_four(place, produce, send, pair_in, far_in, own, sems, 0)
    one_grad = own[...]
    r, xhat = normalize(tok_ref[...].astype(jnp.float32))
    gg_ref[...] = jnp.sum(one_grad * xhat, axis=0, keepdims=True)
    n = one_grad * gain_ref[...]
    grad = hg_ref[...] + r * (n - xhat * jnp.mean(n * xhat, axis=1, keepdims=True))
    all_ref[place.tp] = grad.astype(jnp.bfloat16)
    gather_four(place, all_ref, sems, 3)


def tail(tok, hidden_grad, lin_grad, qkv_w, gain):
    own, width = tok.shape
    return pl.pallas_call(
        tail_body,
        in_specs=[WHOLE] * 5,
        out_specs=[WHOLE] * 2,
        out_shape=[
            jax.ShapeDtypeStruct((4, own, width), jnp.bfloat16),
            jax.ShapeDtypeStruct((1, width), jnp.float32),
        ],
        scratch_shapes=[
            pltpu.VMEM((4, own, width), jnp.bfloat16),
            pltpu.VMEM((2, own, width), jnp.bfloat16),
            pltpu.VMEM((own, width), jnp.bfloat16),
            pltpu.VMEM((own, width), jnp.float32),
            pltpu.SemaphoreType.DMA((2, 6)),
        ],
        compiler_params=pltpu.CompilerParams(vmem_limit_bytes=VL, collective_id=1, has_side_effects=True),
        cost_estimate=busy(50),
        name="tail",
    )(tok, hidden_grad, lin_grad, qkv_w, gain)


def turn_body(*refs, count, kinds, first, finish):
    gu_refs, w_refs = refs[:count], refs[count : 2 * count]
    lg_ref, router_ref, hid_ref, extra_ref, gain_ref = refs[2 * count : 2 * count + 5]
    outs = refs[2 * count + 5 : 2 * count + 8]
    gu_buf, gu_sem, give, keep, pair_in, cut, own, sems = refs[2 * count + 8 :]
    all_ref = outs[0]
    place = Place()
    place.meet((place.pair, place.far, place.side))
    block = hid_ref.shape[0]
    shards, _, experts, part, ff = w_refs[0].shape
    half = block // 2
    top, low = pl.ds(0, half), pl.ds(half, half)
    bf = jnp.bfloat16
    f = jnp.float32
    order = [(1, 1), (1, 0), (0, 1), (0, 0)]

    def tile_of(step):
        dx, dy = order[step // 2]
        ctx = place.ctx + dx * (1 - 2 * place.ctx)
        high = place.high + dy * (1 - 2 * place.high)
        core = 1 - place.core if step % 2 == 0 else place.core
        return ctx * 4 + high * 2 + core

    def fetch(step):
        at = pl.ds(pl.multiple_of(tile_of(step) * block, block), block)
        return [
            pltpu.make_async_copy(gu.at[at, :], gu_buf.at[step % 2, n], gu_sem.at[step % 2, n])
            for n, gu in enumerate(gu_refs)
        ]

    for copy in fetch(0):
        copy.start()

    def compute(step, dst):
        for copy in fetch(step):
            copy.wait()
        if step + 1 < 8:
            for copy in fetch(step + 1):
                copy.start()
        at = pl.ds(pl.multiple_of(tile_of(step) * block, block), block)
        for z in range(shards):
            cols = slice(z * part, (z + 1) * part)
            total = None
            if lg_ref is not None:
                total = nt(lg_ref[at, :], router_ref[cols, :])
            for n, w_ref in enumerate(w_refs):
                w = jnp.concatenate(
                    [
                        w_ref[z, kind, p * PAIR + e]
                        for p in range(experts // PAIR)
                        for kind in range(kinds)
                        for e in range(PAIR)
                    ],
                    axis=1,
                )
                piece = nt(gu_buf[step % 2, n], w)
                total = piece if total is None else total + piece
            dst[:, cols] = total.astype(bf)

    copies = []

    def send(src, dst, slot, device):
        copy = push(src, dst, sems, slot, device)
        copy.start()
        copies.append(copy)
        return copy

    for k in range(4):
        compute(2 * k, give.at[k])
        got = send(give.at[k], pair_in.at[k], k, place.pair)
        compute(2 * k + 1, keep.at[k])
        got.wait_recv()
        total = keep[k].astype(f) + pair_in[k].astype(f)
        if k == 0:
            keep[k] = total.astype(bf)
            a_cross = send(keep.at[k, top], cut.at[0], 4, place.side)
            b_cross = send(keep.at[k, low], cut.at[1], 5, place.far)
        elif k == 1:
            b_cross.wait_recv()
            keep[k, top] = total[:half].astype(bf)
            keep[k, low] = (total[half:] + cut[1].astype(f)).astype(bf)
            a_first = send(keep.at[k, top], cut.at[2], 6, place.side)
            b_last = send(keep.at[k, low], cut.at[5], 9, place.side)
        elif k == 2:
            a_cross.wait_recv()
            keep[k, low] = total[half:].astype(bf)
            keep[k, top] = (total[:half] + cut[0].astype(f)).astype(bf)
            b_first = send(keep.at[k, low], cut.at[4], 8, place.far)
            a_last = send(keep.at[k, top], cut.at[3], 7, place.far)
        else:
            for copy in (a_first, a_last, b_first, b_last):
                copy.wait_recv()
            own[top, :] = total[:half] + cut[2].astype(f) + cut[3].astype(f)
            own[low, :] = total[half:] + cut[4].astype(f) + cut[5].astype(f)
    finish(place, own, hid_ref, extra_ref, gain_ref, outs)
    gather_four(place, all_ref, sems, 10)
    for copy in copies:
        copy.wait_send()


def turn_back(place, own, hid_ref, grad_ref, gain_ref, outs):
    all_ref, hg_ref, gg_ref = outs
    two_grad = own[...]
    r, hhat = normalize(hid_ref[...])
    gg_ref[...] = jnp.sum(two_grad * hhat, axis=0, keepdims=True)
    m = two_grad * gain_ref[...]
    grad = grad_ref[...].astype(jnp.float32) + r * (m - hhat * jnp.mean(m * hhat, axis=1, keepdims=True))
    hg_ref[...] = grad
    all_ref[place.tp] = grad.astype(jnp.bfloat16)


def turn(gus, ws, logit_grad, router_w, hidden, grad_own, gain):
    shards, _, experts, part, ff = ws[0].shape
    own, width = hidden.shape
    count = len(gus)
    kinds = 2
    cols = gus[0].shape[1]
    anys = pl.BlockSpec(memory_space=pl.ANY)
    return pl.pallas_call(
        functools.partial(turn_body, count=count, kinds=kinds, first=0, finish=turn_back),
        grid=(1,),
        in_specs=[anys] * count
        + [
            pl.BlockSpec((shards, kinds, experts, part, ff), lambda i: (0, 0, 0, 0, 0), pipeline_mode=pl.Buffered(1))
            for _ in ws
        ]
        + [WHOLE] * 5,
        out_specs=[WHOLE] * 3,
        out_shape=[
            jax.ShapeDtypeStruct((4, own, width), jnp.bfloat16),
            jax.ShapeDtypeStruct((own, width), jnp.float32),
            jax.ShapeDtypeStruct((1, width), jnp.float32),
        ],
        scratch_shapes=[
            pltpu.VMEM((2, count, own, cols), jnp.bfloat16),
            pltpu.SemaphoreType.DMA((2, count)),
            pltpu.VMEM((4, own, width), jnp.bfloat16),
            pltpu.VMEM((4, own, width), jnp.bfloat16),
            pltpu.VMEM((4, own, width), jnp.bfloat16),
            pltpu.VMEM((6, own // 2, width), jnp.bfloat16),
            pltpu.VMEM((own, width), jnp.float32),
            pltpu.SemaphoreType.DMA((2, 13)),
        ],
        compiler_params=pltpu.CompilerParams(vmem_limit_bytes=VL, collective_id=2, has_side_effects=True),
        cost_estimate=busy(75),
        name="turn",
    )(*gus, *ws, logit_grad, router_w, hidden, grad_own, gain)


from jax.sharding import PartitionSpec as P

rope_base = 10000.0
CHUNKS = 4
bf16 = jnp.bfloat16
f32 = jnp.float32


def rope_tables(positions):
    half = HD // 2
    frequency = rope_base ** (-2.0 * jnp.arange(half, dtype=f32) / HD)
    angles = positions.astype(f32)[:, None] * frequency[None, :]
    return jnp.cos(angles)[:, None, :], jnp.sin(angles)[:, None, :]


def busy(us):
    return pl.CostEstimate(flops=int(us * 1e9), bytes_accessed=1 << 20, transcendentals=0)


def swap(x):
    return lax.ppermute(x, "ctx", [(0, 1), (1, 0)])


def after(x, *done):
    return lax.optimization_barrier((x, *done))


def rotate(values, cosine, sine):
    shaped = values.reshape(values.shape[0], -1, HD)
    a, b = shaped[:, :, : HD // 2], shaped[:, :, HD // 2 :]
    return jnp.concatenate([a * cosine - b * sine, b * cosine + a * sine], axis=2)


def per_device(
    tokens, out_grad, doc_ids, block_ids, expert_ids, norm1_gain, w_query, w_key, w_value, w_out,
    norm2_gain, w_router, w_gate, w_up, w_down,
):
    shards = lax.axis_size("fsdp")
    ctx_size = lax.axis_size("ctx")
    tp_size = lax.axis_size("tp")
    ctx = lax.axis_index("ctx")
    tp = lax.axis_index("tp")
    rows, width = tokens.shape
    part = width // shards
    own = rows // tp_size
    length = doc_ids.shape[0]
    q_width, kv_width = w_query.shape[1], w_key.shape[1]
    heads, kv_heads = q_width // HD, kv_width // HD
    experts = w_gate.shape[0]
    mine = experts // ctx_size
    each = mine // CHUNKS
    ff = w_gate.shape[2]

    small = jnp.concatenate([w_router, norm1_gain[:, None], norm2_gain[:, None]], axis=1)
    ordered = lambda here, there, axis=0: jnp.concatenate(
        [jnp.where(ctx == 0, here, there), jnp.where(ctx == 0, there, here)], axis=axis
    )
    spare = -small.shape[1] % 128
    packed = jnp.concatenate(
        [w_query, w_key, w_value, w_out.T, small, jnp.zeros((part, spare), bf16)], axis=1
    )
    packed = lax.all_gather(packed, "fsdp", axis=0, tiled=True)
    shard_list = []
    for chunk in range(CHUNKS):
        first = ctx * mine + chunk * each
        pick = lambda w: lax.dynamic_slice_in_dim(w, first, each, 0)
        shard_list.append(jnp.stack([pick(w_gate), pick(w_up), pick(w_down).transpose(0, 2, 1)]))
    packed, *shard_list = after(packed, *shard_list)
    qkv_w = packed[:, : q_width + 2 * kv_width]
    at = q_width + 2 * kv_width
    out_w = packed[:, at : at + q_width]
    at += q_width
    router_w = packed[:, at : at + experts]
    gain_one = packed[:, at + experts].astype(f32)
    gain_two = packed[:, at + experts + 1].astype(f32)

    stacked = [lax.all_gather(shard, "fsdp", axis=0) for shard in shard_list]
    ids_all = ordered(expert_ids, swap(expert_ids))

    inputs = tokens.astype(f32)
    rms_one = lax.rsqrt(jnp.mean(inputs * inputs, axis=1, keepdims=True) + epsilon)
    normed = (inputs * rms_one * gain_one).astype(bf16)
    start = ctx * rows
    cosine, sine = rope_tables(start + jnp.arange(rows, dtype=jnp.int32))
    lin = jnp.dot(normed, qkv_w, preferred_element_type=f32)
    turned = rotate(lin[:, : q_width + kv_width], cosine, sine).astype(bf16)
    queries = turned[:, :heads].transpose(1, 0, 2) * bf16(HD**-0.5)
    keys_values = jnp.concatenate(
        [turned[:, heads:], lin[:, q_width + kv_width :].astype(bf16).reshape(rows, kv_heads, HD)], axis=1
    ).reshape(rows, 2 * kv_width)
    keys_values = ordered(keys_values, swap(keys_values))
    grad_here, keys_values = after(out_grad, keys_values)
    grad_all = ordered(grad_here, swap(grad_here))
    keys_values = keys_values.reshape(length, 2 * kv_heads, HD).transpose(1, 0, 2)
    keys, values = keys_values[:kv_heads], keys_values[kv_heads:]
    query_doc = lax.dynamic_slice_in_dim(doc_ids, start, rows)
    query_block = lax.dynamic_slice_in_dim(block_ids, start, rows)
    base = start.astype(jnp.int32).reshape(1)
    tokens_own = lax.dynamic_slice_in_dim(tokens, tp * own, own)
    grad_own = lax.dynamic_slice_in_dim(out_grad, tp * own, own)
    attn_mix, hidden, normed_two = mid(
        tokens_own, queries, keys, values, query_doc[:, None], query_block[:, None], doc_ids[None],
        block_ids[None], out_w, gain_two[None],
    )
    normed_two = normed_two.reshape(ctx_size * rows, width)

    logits = jnp.dot(normed_two, router_w, preferred_element_type=f32)
    chosen = jnp.any(ids_all[:, :, None] == jnp.arange(experts, dtype=jnp.int32)[None, None, :], axis=1)
    masked = jnp.where(chosen, logits, masked_score)
    powers = jnp.exp(masked - jnp.max(masked, axis=1, keepdims=True))
    gates = powers / jnp.sum(powers, axis=1, keepdims=True)
    gates_mine = lax.dynamic_slice_in_dim(gates, ctx * mine, mine, 1)

    normed_t, grad_t = normed_two.T, grad_all.T
    inner_all, outer_all, dots_all, shard_grads = [], [], [], []
    for chunk in range(CHUNKS):
        inner, outer, grads, dots = moe_main(
            normed_two, grad_all, normed_t, grad_t,
            gates_mine[:, chunk * each : (chunk + 1) * each], stacked[chunk],
        )
        inner_all.append(inner)
        outer_all.append(outer)
        dots_all.append(dots)
        shard_grads.append(lax.psum_scatter(grads, "fsdp", scatter_dimension=0, tiled=False))
    combined = moe_back(inner_all, stacked, 2, 1)

    dots = jnp.concatenate(dots_all, axis=0).transpose(1, 0, 2).reshape(ctx_size * rows, mine)
    weighted = gates_mine * dots
    dots_sum = jnp.sum(weighted, axis=1, keepdims=True)
    spread = lax.dynamic_update_slice_in_dim(jnp.zeros_like(gates), weighted, ctx * mine, 1)
    logit_grad = (spread - gates * dots_sum).astype(bf16)
    router_grad = lax.dot_general(
        normed_two, logit_grad, (((0,), (0,)), ((), ())), preferred_element_type=f32
    )
    grad_own, shard_grads[0] = after(grad_own, shard_grads[0])
    branch_grad, hidden_grad, gain_two_grad = turn(
        outer_all, stacked, logit_grad, router_w, hidden, grad_own, gain_two[None]
    )
    branch_grad, *first = after(branch_grad, *shard_grads[:3])
    there = [swap(piece) for piece in first]
    branch_grad = branch_grad.reshape(rows, width)

    out_w_grad = lax.dot_general(
        branch_grad, attn_mix, (((0,), (0,)), ((), ())), preferred_element_type=f32
    )
    mix_grad = jnp.dot(branch_grad, out_w, preferred_element_type=f32).astype(bf16)
    query_grad, key_grad, value_grad = flash_bwd(
        base, queries, mix_grad.reshape(rows, heads, HD).transpose(1, 0, 2), keys, values,
        query_doc[None], query_block[None], doc_ids[:, None], block_ids[:, None],
    )
    query_grad, key_grad, value_grad, *there = after(query_grad, key_grad, value_grad, *there)
    kv_grad = jnp.concatenate([key_grad, value_grad], axis=0).transpose(1, 0, 2).reshape(length, 2 * kv_width)
    kv_grad = kv_grad.astype(bf16)
    kept = lax.dynamic_slice_in_dim(kv_grad, start, rows)
    given = lax.dynamic_slice_in_dim(kv_grad, rows - start, rows)
    kv_grad = kept.astype(f32) + swap(given).astype(f32)
    kv_grad, last = after(kv_grad, shard_grads[3])
    there.append(swap(last))
    query_grad = (query_grad * HD**-0.5).transpose(1, 0, 2).reshape(rows, q_width)
    turned_grad = rotate(
        jnp.concatenate([query_grad, kv_grad[:, :kv_width]], axis=1), cosine, -sine
    ).reshape(rows, q_width + kv_width)
    lin_grad = jnp.concatenate([turned_grad, kv_grad[:, kv_width:]], axis=1).astype(bf16)
    qkv_grad = lax.dot_general(normed, lin_grad, (((0,), (0,)), ((), ())), preferred_element_type=f32)

    input_grad, gain_one_grad = tail(tokens_own, hidden_grad, lin_grad, qkv_w, gain_one[None])
    input_grad = input_grad.reshape(rows, width)
    hidden, gain_one_grad = after(hidden, gain_one_grad)
    mixed = lax.psum_scatter(combined, ("ctx", "tp"), scatter_dimension=0, tiled=True)
    block_out = lax.all_gather((hidden + mixed.astype(f32)).astype(bf16), "tp", axis=0, tiled=True)

    big = jnp.concatenate([qkv_grad, out_w_grad], axis=1).astype(bf16)
    big = lax.psum_scatter(big, "fsdp", scatter_dimension=0, tiled=True)
    big = big.astype(f32) + swap(big).astype(f32)
    everywhere = ("fsdp", "ctx", "tp")
    tiny = lax.psum(jnp.concatenate([router_grad.T, gain_two_grad], axis=0), everywhere)
    gain_one_grad = lax.psum(gain_one_grad, everywhere)[0]
    mine_of = lambda x: lax.dynamic_slice_in_dim(x, lax.axis_index("fsdp") * part, part, x.ndim - 1)

    gate_s, up_s, down_s = [
        ordered(
            jnp.concatenate([piece[kind] for piece in shard_grads]),
            jnp.concatenate([piece[kind] for piece in there]),
        ).astype(f32)
        for kind in range(3)
    ]
    at = q_width + 2 * kv_width
    return (
        block_out,
        input_grad,
        mine_of(gain_one_grad),
        big[:, :q_width],
        big[:, q_width : q_width + kv_width],
        big[:, q_width + kv_width : at],
        big[:, at : at + q_width].T,
        mine_of(tiny[experts]),
        mine_of(tiny[:experts]).T,
        gate_s,
        up_s,
        down_s.transpose(0, 2, 1),
    )


def solution(mesh):
    rows = P(("fsdp", "ctx"), None)
    return jax.shard_map(
        per_device,
        mesh=mesh,
        in_specs=(
            rows, rows, P("fsdp"), P("fsdp"), rows, P("fsdp"), P("fsdp", "tp"), P("fsdp", "tp"),
            P("fsdp", "tp"), P("tp", "fsdp"), P("fsdp"), P("fsdp", None), P(None, "fsdp", "tp"),
            P(None, "fsdp", "tp"), P(None, "tp", "fsdp"),
        ),
        out_specs=(
            rows, rows, P("fsdp"), P("fsdp", "tp"), P("fsdp", "tp"), P("fsdp", "tp"), P("tp", "fsdp"),
            P("fsdp"), P("fsdp", None), P(None, "fsdp", "tp"), P(None, "fsdp", "tp"), P(None, "tp", "fsdp"),
        ),
        check_vma=False,
    )
```

```python
import functools
import jax
import jax.numpy as jnp
from jax import lax
from jax.experimental import pallas as pl
from jax.experimental.pallas import tpu as pltpu

HD = 64
DOC = 1024
BLK = 256
QB = 256
BAND = DOC + 2 * BLK
masked_score = -1e30
epsilon = 1e-06
VL = 60 * 1024 * 1024

def nt(a, b):
    return lax.dot_general(a, b, (((1,), (1,)), ((), ())), preferred_element_type=jnp.float32)

def tn(a, b):
    return lax.dot_general(a, b, (((0,), (0,)), ((), ())), preferred_element_type=jnp.float32)

def nn(a, b):
    return jnp.dot(a, b, preferred_element_type=jnp.float32)

def band_start(row, length):
    return pl.multiple_of(jnp.clip(row - DOC, 0, length - BAND), QB)

def flash_fwd_body(base_ref, q_ref, k_ref, v_ref, docq_ref, blkq_ref, dock_ref, blkk_ref, o_ref, *, share, length):
    step = pl.program_id(0)
    start = band_start(base_ref[0] + step * QB, length)
    keys = pl.ds(start, BAND)
    dock = dock_ref[:, keys]
    blkk = blkk_ref[:, keys]
    ok = (docq_ref[...] == dock) & (blkk <= blkq_ref[...])
    bias = jnp.where(ok, 0.0, masked_score)
    for head in range(q_ref.shape[0]):
        s = nt(q_ref[head], k_ref[head // share, keys, :]) + bias
        top = jnp.max(s, axis=1, keepdims=True)
        e = jnp.exp(s - top)
        p = e * (1.0 / jnp.sum(e, axis=1, keepdims=True))
        o_ref[head] = nn(p.astype(jnp.bfloat16), v_ref[head // share, keys, :]).astype(jnp.bfloat16)

def flash_fwd(base, q, k, v, docq, blkq, dock, blkk):
    heads, rows, _ = q.shape
    kv, length, _ = k.shape
    full = lambda shape: pl.BlockSpec(shape, lambda i, b: (0,) * len(shape))
    return pl.pallas_call(
        functools.partial(flash_fwd_body, share=heads // kv, length=length),
        grid_spec=pltpu.PrefetchScalarGridSpec(
            num_scalar_prefetch=1, grid=(rows // QB,),
            in_specs=[
                pl.BlockSpec((heads, QB, HD), lambda i, b: (0, i, 0)),
                full(k.shape), full(v.shape),
                pl.BlockSpec((QB, 1), lambda i, b: (i, 0)),
                pl.BlockSpec((QB, 1), lambda i, b: (i, 0)),
                full((1, length)), full((1, length)),
            ],
            out_specs=pl.BlockSpec((heads, QB, HD), lambda i, b: (0, i, 0)),
        ),
        out_shape=jax.ShapeDtypeStruct(q.shape, jnp.bfloat16),
        compiler_params=pltpu.CompilerParams(vmem_limit_bytes=VL),
        name="flash_fwd",
    )(base, q, k, v, docq, blkq, dock, blkk)

def flash_bwd_body(base_ref, q_ref, g_ref, k_ref, v_ref, docq_ref, blkq_ref, dock_ref, blkk_ref, dq_ref, dk_ref, dv_ref, *, share, length):
    step = pl.program_id(0)
    start = band_start(base_ref[0] + step * QB, length)
    keys = pl.ds(start, BAND)

    @pl.when(step == 0)
    def _():
        dk_ref[...] = jnp.zeros_like(dk_ref)
        dv_ref[...] = jnp.zeros_like(dv_ref)

    ok = (docq_ref[...] == dock_ref[keys, :]) & (blkk_ref[keys, :] <= blkq_ref[...])
    bias = jnp.where(ok, 0.0, masked_score)
    for head in range(q_ref.shape[0]):
        kvh = head // share
        q = q_ref[head]
        g = g_ref[head]
        k = k_ref[kvh, keys, :]
        s = nt(k, q) + bias
        e = jnp.exp(s - jnp.max(s, axis=0, keepdims=True))
        p = e * (1.0 / jnp.sum(e, axis=0, keepdims=True))
        dp = nt(v_ref[kvh, keys, :], g)
        delta = jnp.sum(dp * p, axis=0, keepdims=True)
        ds = (p * (dp - delta)).astype(jnp.bfloat16)
        dq_ref[head] = tn(ds, k)
        dk_ref[kvh, keys, :] += nn(ds, q)
        dv_ref[kvh, keys, :] += nn(p.astype(jnp.bfloat16), g)

def flash_bwd(base, q, g, k, v, docq, blkq, dock, blkk):
    heads, rows, _ = q.shape
    kv, length, _ = k.shape
    full = lambda shape: pl.BlockSpec(shape, lambda i, b: (0,) * len(shape))
    return pl.pallas_call(
        functools.partial(flash_bwd_body, share=heads // kv, length=length),
        grid_spec=pltpu.PrefetchScalarGridSpec(
            num_scalar_prefetch=1, grid=(rows // QB,),
            in_specs=[
                pl.BlockSpec((heads, QB, HD), lambda i, b: (0, i, 0)),
                pl.BlockSpec((heads, QB, HD), lambda i, b: (0, i, 0)),
                full(k.shape), full(v.shape),
                pl.BlockSpec((1, QB), lambda i, b: (0, i)),
                pl.BlockSpec((1, QB), lambda i, b: (0, i)),
                full((length, 1)), full((length, 1)),
            ],
            out_specs=[
                pl.BlockSpec((heads, QB, HD), lambda i, b: (0, i, 0)),
                full(k.shape), full(v.shape),
            ],
        ),
        out_shape=[
            jax.ShapeDtypeStruct(q.shape, jnp.float32),
            jax.ShapeDtypeStruct(k.shape, jnp.float32),
            jax.ShapeDtypeStruct(v.shape, jnp.float32),
        ],
        compiler_params=pltpu.CompilerParams(vmem_limit_bytes=VL),
        cost_estimate=busy(55),
        name="flash_bwd",
    )(base, q, g, k, v, docq, blkq, dock, blkk)

PAIR = 2
TM = 512

def moe_body(x_ref, g_ref, xt_ref, gt_ref, gates_ref, w_ref, a_ref, gu_ref, grads_ref, dots_ref):
    rows, width = x_ref.shape
    shards, _, pair, part, ff = w_ref.shape
    step = pl.program_id(0)

    def weights(which):
        return jnp.concatenate(
            [jnp.concatenate([w_ref[z, which, e] for z in range(shards)], axis=0) for e in range(pair)], axis=1
        )

    gate_w = weights(0)
    up_w = weights(1)
    down_w = weights(2)
    experts = gates_ref.shape[1]

    def tile(i, carry):
        here = pl.ds(pl.multiple_of(i * TM, TM), TM)
        x = x_ref[here, :]
        gate_val = nn(x, gate_w)
        up_val = nn(x, up_w)
        back = nn(g_ref[here, :], down_w)
        lanes = lax.broadcasted_iota(jnp.int32, (TM, experts), 1)
        gates = gates_ref[here, :]
        gate = jnp.concatenate(
            [
                jnp.broadcast_to(
                    jnp.sum(jnp.where(lanes == step * pair + e, gates, 0.0), axis=1, keepdims=True), (TM, ff)
                )
                for e in range(pair)
            ],
            axis=1,
        )
        sig = 1.0 / (1.0 + jnp.exp(-gate_val))
        silu = gate_val * sig
        inner = silu * up_val
        a_ref[here, :] = (inner * gate).astype(jnp.bfloat16)
        prod = inner * back
        dots = jnp.where(step == 0, 0.0, dots_ref[here, :])
        for e in range(pair):
            total = jnp.sum(prod[:, e * ff : (e + 1) * ff], axis=1, keepdims=True)
            dots = jnp.where(lanes == step * pair + e, total, dots)
        dots_ref[here, :] = dots
        back = back * gate
        gu_ref[here, : pair * ff] = (back * up_val * sig * (1.0 + gate_val * (1.0 - sig))).astype(jnp.bfloat16)
        gu_ref[here, pair * ff :] = (back * silu).astype(jnp.bfloat16)
        return carry

    lax.fori_loop(0, rows // TM, tile, 0)
    for z in range(shards):
        part_rows = pl.ds(z * part, part)
        both = nn(xt_ref[part_rows, :], gu_ref[...])
        down = nn(gt_ref[part_rows, :], a_ref[...])
        for e in range(pair):
            grads_ref[z, 0, e] = both[:, e * ff : (e + 1) * ff].astype(jnp.bfloat16)
            grads_ref[z, 1, e] = both[:, (pair + e) * ff : (pair + e + 1) * ff].astype(jnp.bfloat16)
            grads_ref[z, 2, e] = down[:, e * ff : (e + 1) * ff].astype(jnp.bfloat16)

def moe_main(x, g, xt, gt, gates, w):
    rows, width = x.shape
    shards, three, count, part, ff = w.shape
    one = lambda shape: pl.BlockSpec(shape, lambda i: (0,) * len(shape), pipeline_mode=pl.Buffered(1))
    return pl.pallas_call(
        moe_body,
        grid=(count // PAIR,),
        in_specs=[
            one(x.shape), one(g.shape), one(xt.shape), one(gt.shape), one(gates.shape),
            pl.BlockSpec((shards, 3, PAIR, part, ff), lambda i: (0, 0, i, 0, 0)),
        ],
        out_specs=[
            pl.BlockSpec((rows, PAIR * ff), lambda i: (0, i)),
            pl.BlockSpec((rows, 2 * PAIR * ff), lambda i: (0, i)),
            pl.BlockSpec((shards, 3, PAIR, part, ff), lambda i: (0, 0, i, 0, 0)),
            pl.BlockSpec((rows, count), lambda i: (0, 0)),
        ],
        out_shape=[
            jax.ShapeDtypeStruct((rows, count * ff), jnp.bfloat16),
            jax.ShapeDtypeStruct((rows, 2 * count * ff), jnp.bfloat16),
            jax.ShapeDtypeStruct(w.shape, jnp.bfloat16),
            jax.ShapeDtypeStruct((rows, count), jnp.float32),
        ],
        compiler_params=pltpu.CompilerParams(vmem_limit_bytes=VL),
        cost_estimate=pl.CostEstimate(flops=2 * rows * width * count * ff * 6, bytes_accessed=8 * rows * width + 12 * count * ff * width, transcendentals=0),
        name="moe_main",
    )(x, g, xt, gt, gates, w)

def back_body(*refs, count, first, kinds):
    gu_refs, w_refs, o_ref = refs[:count], refs[count : 2 * count], refs[2 * count]
    shards, _, experts, part, ff = w_refs[0].shape
    for z in range(shards):
        total = None
        for gu_ref, w_ref in zip(gu_refs, w_refs):
            w = jnp.concatenate(
                [
                    w_ref[z, kind, p * PAIR + e]
                    for p in range(experts // PAIR)
                    for kind in range(kinds)
                    for e in range(PAIR)
                ],
                axis=1,
            )
            piece = nt(gu_ref[...], w)
            total = piece if total is None else total + piece
        o_ref[:, z * part : (z + 1) * part] = total.astype(o_ref.dtype)


def moe_back(gus, ws, first, kinds):
    shards, three, experts, part, ff = ws[0].shape
    rows = gus[0].shape[0]
    width = shards * part
    count = len(gus)
    return pl.pallas_call(
        functools.partial(back_body, count=count, first=first, kinds=kinds),
        grid=(rows // TM,),
        in_specs=[pl.BlockSpec((TM, kinds * experts * ff), lambda i: (i, 0)) for _ in gus]
        + [
            pl.BlockSpec(
                (shards, kinds, experts, part, ff),
                lambda i: (0, first // kinds, 0, 0, 0),
                pipeline_mode=pl.Buffered(1),
            )
            for _ in ws
        ],
        out_specs=pl.BlockSpec((TM, width), lambda i: (i, 0)),
        out_shape=jax.ShapeDtypeStruct((rows, width), jnp.bfloat16),
        compiler_params=pltpu.CompilerParams(vmem_limit_bytes=VL),
        cost_estimate=pl.CostEstimate(
            flops=2 * rows * width * count * experts * ff * kinds,
            bytes_accessed=2 * rows * kinds * count * experts * ff,
            transcendentals=0,
        ),
        name="moe_back" if kinds == 2 else "moe_out",
    )(*gus, *ws)


MESH = pl.DeviceIdType.MESH


class Place:
    def __init__(self):
        self.ctx = lax.axis_index("ctx")
        self.tp = lax.axis_index("tp")
        self.core = lax.rem(self.tp, 2)
        self.high = self.tp // 2
        self.pair_tp = self.high * 2 + 1 - self.core
        self.far_tp = (1 - self.high) * 2 + self.core
        self.cross_tp = (1 - self.high) * 2 + 1 - self.core
        self.pair = {"tp": self.pair_tp}
        self.far = {"tp": self.far_tp}
        self.side = {"ctx": 1 - self.ctx}

    def meet(self, who):
        barrier = pltpu.get_barrier_semaphore()
        for device in who:
            pl.semaphore_signal(barrier, inc=1, device_id=device, device_id_type=MESH)
        pl.semaphore_wait(barrier, len(who))


def push(src, dst, sems, slot, device):
    return pltpu.make_async_remote_copy(
        src_ref=src, dst_ref=dst, send_sem=sems.at[0, slot], recv_sem=sems.at[1, slot],
        device_id=device, device_id_type=MESH,
    )


def gather_four(place, all_ref, sems, at):
    here, far = all_ref.at[place.tp], all_ref.at[place.far_tp]
    to_far = push(here, here, sems, at, place.far)
    to_pair = push(here, here, sems, at + 1, place.pair)
    to_far.start()
    to_pair.start()
    to_far.wait_recv()
    on = push(far, far, sems, at + 2, place.pair)
    on.start()
    to_pair.wait_recv()
    on.wait_recv()
    to_far.wait_send()
    to_pair.wait_send()
    on.wait_send()


def gather_eight(place, all_ref, sems, at):
    rows = all_ref.shape[1]
    top, low = pl.ds(0, rows // 2), pl.ds(rows // 2, rows // 2)
    part = lambda ctx, tp: all_ref.at[ctx * 4 + tp]
    other = 1 - place.ctx
    here = part(place.ctx, place.tp)
    side = part(other, place.tp)
    far = part(place.ctx, place.far_tp)
    cross = part(other, place.far_tp)
    side_top, far_low = side.at[top], far.at[low]
    cross_top, cross_low = cross.at[top], cross.at[low]
    to_side = push(here, here, sems, at, place.side)
    to_far = push(here, here, sems, at + 1, place.far)
    to_pair = push(here, here, sems, at + 2, place.pair)
    for copy in (to_side, to_far, to_pair):
        copy.start()
    to_side.wait_recv()
    turn_far = push(side_top, side_top, sems, at + 3, place.far)
    pair_side = push(side, side, sems, at + 5, place.pair)
    turn_far.start()
    pair_side.start()
    to_far.wait_recv()
    turn_side = push(far_low, far_low, sems, at + 4, place.side)
    pair_far = push(far, far, sems, at + 6, place.pair)
    turn_side.start()
    pair_far.start()
    turn_far.wait_recv()
    pair_top = push(cross_top, cross_top, sems, at + 7, place.pair)
    pair_top.start()
    turn_side.wait_recv()
    pair_low = push(cross_low, cross_low, sems, at + 8, place.pair)
    pair_low.start()
    for copy in (to_pair, pair_side, pair_far, pair_top, pair_low):
        copy.wait_recv()
    for copy in (to_side, to_far, to_pair, turn_far, turn_side, pair_side, pair_far, pair_top, pair_low):
        copy.wait_send()


def reduce_four(place, produce, send_ref, pair_in, far_in, own_ref, sems, at):
    def fold(j):
        slot = j // 2

        @pl.when(lax.rem(j, 2) == place.core)
        def _():
            push(send_ref.at[j], pair_in.at[slot], sems, at + slot, place.pair).wait_recv()
            total = send_ref[j].astype(jnp.float32) + pair_in[slot].astype(jnp.float32)

            @pl.when(slot == place.high)
            def _():
                own_ref[...] = total

            @pl.when(slot != place.high)
            def _():
                send_ref[j] = total.astype(jnp.bfloat16)
                push(send_ref.at[j], far_in, sems, at + 2, place.far).start()

    def step(j, carry):
        produce(j)

        @pl.when(lax.rem(j, 2) != place.core)
        def _():
            slot = j // 2
            push(send_ref.at[j], pair_in.at[slot], sems, at + slot, place.pair).start()

        @pl.when(j > 0)
        def _():
            fold(j - 1)

        return carry

    lax.fori_loop(0, 4, step, 0)
    fold(3)
    last = push(send_ref.at[place.far_tp], far_in, sems, at + 2, place.far)
    last.wait_recv()
    own_ref[...] += far_in[...].astype(jnp.float32)
    last.wait_send()
    for slot in range(2):
        push(send_ref.at[place.pair_tp], pair_in.at[slot], sems, at + slot, place.pair).wait_send()


SMEMS = pl.BlockSpec(memory_space=pltpu.SMEM)
WHOLE = pl.BlockSpec(memory_space=pltpu.VMEM)


def normalize(x):
    r = lax.rsqrt(jnp.mean(x * x, axis=1, keepdims=True) + epsilon)
    return r, x * r


def mid_body(tok_ref, q_ref, k_ref, v_ref, docq_ref, blkq_ref, dock_ref, blkk_ref, w_ref, gain_ref,
             mix_ref, hid_ref, all_ref, send, pair_in, far_in, own, sems, *, share, length):
    place = Place()
    place.meet((place.pair, place.far, place.side))
    heads, rows, _ = q_ref.shape
    block = rows // 4
    band = min(DOC + block + BLK, length)

    def produce(j):
        at = pl.multiple_of(j * block, block)
        here = pl.ds(at, block)
        start = pl.multiple_of(jnp.clip(place.ctx * rows + at - DOC, 0, length - band), 128)
        keys = pl.ds(start, band)
        ok = (docq_ref[here, :] == dock_ref[:, keys]) & (blkk_ref[:, keys] <= blkq_ref[here, :])
        bias = jnp.where(ok, 0.0, masked_score)
        outs = []
        for head in range(heads):
            s = nt(q_ref[head, here, :], k_ref[head // share, keys, :]) + bias
            e = jnp.exp(s - jnp.max(s, axis=1, keepdims=True))
            p = e * (1.0 / jnp.sum(e, axis=1, keepdims=True))
            outs.append(nn(p.astype(jnp.bfloat16), v_ref[head // share, keys, :]).astype(jnp.bfloat16))
        mix = jnp.concatenate(outs, axis=1)
        mix_ref[here, :] = mix
        send[j] = nt(mix, w_ref[...]).astype(jnp.bfloat16)

    reduce_four(place, produce, send, pair_in, far_in, own, sems, 0)
    hidden = tok_ref[...].astype(jnp.float32) + own[...]
    hid_ref[...] = hidden
    all_ref[place.ctx * 4 + place.tp] = (normalize(hidden)[1] * gain_ref[...]).astype(jnp.bfloat16)
    gather_eight(place, all_ref, sems, 3)


def mid(tok, q, k, v, docq, blkq, dock, blkk, out_w, gain):
    heads, rows, _ = q.shape
    kv, length, _ = k.shape
    own, width = tok.shape
    return pl.pallas_call(
        functools.partial(mid_body, share=heads // kv, length=length),
        in_specs=[WHOLE] * 10,
        out_specs=[WHOLE] * 3,
        out_shape=[
            jax.ShapeDtypeStruct((rows, heads * HD), jnp.bfloat16),
            jax.ShapeDtypeStruct((own, width), jnp.float32),
            jax.ShapeDtypeStruct((8, own, width), jnp.bfloat16),
        ],
        scratch_shapes=[
            pltpu.VMEM((4, own, width), jnp.bfloat16),
            pltpu.VMEM((2, own, width), jnp.bfloat16),
            pltpu.VMEM((own, width), jnp.bfloat16),
            pltpu.VMEM((own, width), jnp.float32),
            pltpu.SemaphoreType.DMA((2, 12)),
        ],
        compiler_params=pltpu.CompilerParams(vmem_limit_bytes=VL, collective_id=0, has_side_effects=True),
        cost_estimate=busy(100),
        name="mid",
    )(tok, q, k, v, docq, blkq, dock, blkk, out_w, gain)


def tail_body(tok_ref, hg_ref, lin_ref, w_ref, gain_ref, small_ref, all_ref, sum_ref,
              send, pair_in, far_in, own, mine, theirs, split, split_in, sems, small_sems, *, shards):
    place = Place()
    z = lax.axis_index("fsdp")
    others = [{"fsdp": lax.rem(z + d, shards)} for d in range(1, shards)]
    place.meet((place.pair, place.far, place.side, *others))
    block = lin_ref.shape[0] // 4
    part = sum_ref.shape[1]

    def produce(j):
        here = pl.ds(pl.multiple_of(j * block, block), block)
        send[j] = nt(lin_ref[here, :], w_ref[...]).astype(jnp.bfloat16)

    reduce_four(place, produce, send, pair_in, far_in, own, sems, 0)
    one_grad = own[...]
    r, xhat = normalize(tok_ref[...].astype(jnp.float32))
    n = one_grad * gain_ref[...]
    grad = hg_ref[...] + r * (n - xhat * jnp.mean(n * xhat, axis=1, keepdims=True))
    all_ref[place.tp] = grad.astype(jnp.bfloat16)
    row = lax.broadcasted_iota(jnp.int32, small_ref.shape, 0)
    mine[0] = jnp.where(
        row == small_ref.shape[0] - 1, jnp.sum(one_grad * xhat, axis=0, keepdims=True), small_ref[...]
    )
    hops = [
        push(mine.at[i], theirs.at[i], small_sems, i, device)
        for i, device in enumerate((place.pair, place.side, place.far))
    ]
    hops[0].start()
    here, far = all_ref.at[place.tp], all_ref.at[place.far_tp]
    to_far = push(here, here, sems, 3, place.far)
    to_pair = push(here, here, sems, 4, place.pair)
    to_far.start()
    to_pair.start()
    for i in range(2):
        hops[i].wait_recv()
        mine[i + 1] = mine[i] + theirs[i]
        hops[i + 1].start()
    to_far.wait_recv()
    on = push(far, far, sems, 5, place.pair)
    on.start()
    hops[2].wait_recv()
    total = mine[2] + theirs[2]
    for j in range(shards):
        split[j] = total[:, j * part : (j + 1) * part]
    spread = [
        push(split.at[lax.rem(z + d, shards)], split_in.at[d - 1], small_sems, 2 + d, others[d - 1])
        for d in range(1, shards)
    ]
    for copy in spread:
        copy.start()
    to_pair.wait_recv()
    on.wait_recv()
    result = split[z]
    for d in range(1, shards):
        spread[d - 1].wait_recv()
        result = result + split_in[d - 1]
    sum_ref[...] = result
    for copy in (to_far, to_pair, on, *hops, *spread):
        copy.wait_send()


def tail(tok, hidden_grad, lin_grad, qkv_w, gain, small, shards):
    own, width = tok.shape
    count = small.shape[0]
    part = width // shards
    return pl.pallas_call(
        functools.partial(tail_body, shards=shards),
        in_specs=[WHOLE] * 6,
        out_specs=[WHOLE] * 2,
        out_shape=[
            jax.ShapeDtypeStruct((4, own, width), jnp.bfloat16),
            jax.ShapeDtypeStruct((count, part), jnp.float32),
        ],
        scratch_shapes=[
            pltpu.VMEM((4, own, width), jnp.bfloat16),
            pltpu.VMEM((2, own, width), jnp.bfloat16),
            pltpu.VMEM((own, width), jnp.bfloat16),
            pltpu.VMEM((own, width), jnp.float32),
            pltpu.VMEM((3, count, width), jnp.float32),
            pltpu.VMEM((3, count, width), jnp.float32),
            pltpu.VMEM((shards, count, part), jnp.float32),
            pltpu.VMEM((shards - 1, count, part), jnp.float32),
            pltpu.SemaphoreType.DMA((2, 6)),
            pltpu.SemaphoreType.DMA((2, 2 + shards)),
        ],
        compiler_params=pltpu.CompilerParams(vmem_limit_bytes=VL, collective_id=1, has_side_effects=True),
        cost_estimate=busy(50),
        name="tail",
    )(tok, hidden_grad, lin_grad, qkv_w, gain, small)


def turn_body(*refs, count, kinds, first, finish):
    gu_refs, w_refs = refs[:count], refs[count : 2 * count]
    lg_ref, router_ref, hid_ref, extra_ref, gain_ref = refs[2 * count : 2 * count + 5]
    outs = refs[2 * count + 5 : 2 * count + 8]
    gu_buf, gu_sem, give, keep, pair_in, cut, own, sems = refs[2 * count + 8 :]
    all_ref = outs[0]
    place = Place()
    place.meet((place.pair, place.far, place.side))
    block = hid_ref.shape[0]
    shards, _, experts, part, ff = w_refs[0].shape
    half = block // 2
    top, low = pl.ds(0, half), pl.ds(half, half)
    bf = jnp.bfloat16
    f = jnp.float32
    order = [(1, 1), (1, 0), (0, 1), (0, 0)]

    def tile_of(step):
        dx, dy = order[step // 2]
        ctx = place.ctx + dx * (1 - 2 * place.ctx)
        high = place.high + dy * (1 - 2 * place.high)
        core = 1 - place.core if step % 2 == 0 else place.core
        return ctx * 4 + high * 2 + core

    def fetch(step):
        at = pl.ds(pl.multiple_of(tile_of(step) * block, block), block)
        return [
            pltpu.make_async_copy(gu.at[at, :], gu_buf.at[step % 2, n], gu_sem.at[step % 2, n])
            for n, gu in enumerate(gu_refs)
        ]

    for copy in fetch(0):
        copy.start()

    def compute(step, dst):
        for copy in fetch(step):
            copy.wait()
        if step + 1 < 8:
            for copy in fetch(step + 1):
                copy.start()
        at = pl.ds(pl.multiple_of(tile_of(step) * block, block), block)
        for z in range(shards):
            cols = slice(z * part, (z + 1) * part)
            total = None
            if lg_ref is not None:
                total = nt(lg_ref[at, :], router_ref[cols, :])
            for n, w_ref in enumerate(w_refs):
                w = jnp.concatenate(
                    [
                        w_ref[z, kind, p * PAIR + e]
                        for p in range(experts // PAIR)
                        for kind in range(kinds)
                        for e in range(PAIR)
                    ],
                    axis=1,
                )
                piece = nt(gu_buf[step % 2, n], w)
                total = piece if total is None else total + piece
            dst[:, cols] = total.astype(bf)

    copies = []

    def send(src, dst, slot, device):
        copy = push(src, dst, sems, slot, device)
        copy.start()
        copies.append(copy)
        return copy

    for k in range(4):
        compute(2 * k, give.at[k])
        got = send(give.at[k], pair_in.at[k], k, place.pair)
        compute(2 * k + 1, keep.at[k])
        got.wait_recv()
        total = keep[k].astype(f) + pair_in[k].astype(f)
        if k == 0:
            keep[k] = total.astype(bf)
            a_cross = send(keep.at[k, top], cut.at[0], 4, place.side)
            b_cross = send(keep.at[k, low], cut.at[1], 5, place.far)
        elif k == 1:
            b_cross.wait_recv()
            keep[k, top] = total[:half].astype(bf)
            keep[k, low] = (total[half:] + cut[1].astype(f)).astype(bf)
            a_first = send(keep.at[k, top], cut.at[2], 6, place.side)
            b_last = send(keep.at[k, low], cut.at[5], 9, place.side)
        elif k == 2:
            a_cross.wait_recv()
            keep[k, low] = total[half:].astype(bf)
            keep[k, top] = (total[:half] + cut[0].astype(f)).astype(bf)
            b_first = send(keep.at[k, low], cut.at[4], 8, place.far)
            a_last = send(keep.at[k, top], cut.at[3], 7, place.far)
        else:
            for copy in (a_first, a_last, b_first, b_last):
                copy.wait_recv()
            own[top, :] = total[:half] + cut[2].astype(f) + cut[3].astype(f)
            own[low, :] = total[half:] + cut[4].astype(f) + cut[5].astype(f)
    finish(place, own, hid_ref, extra_ref, gain_ref, outs)
    gather_four(place, all_ref, sems, 10)
    for copy in copies:
        copy.wait_send()


def turn_back(place, own, hid_ref, grad_ref, gain_ref, outs):
    all_ref, hg_ref, gg_ref = outs
    two_grad = own[...]
    r, hhat = normalize(hid_ref[...])
    gg_ref[...] = jnp.sum(two_grad * hhat, axis=0, keepdims=True)
    m = two_grad * gain_ref[...]
    grad = grad_ref[...].astype(jnp.float32) + r * (m - hhat * jnp.mean(m * hhat, axis=1, keepdims=True))
    hg_ref[...] = grad
    all_ref[place.tp] = grad.astype(jnp.bfloat16)


def turn(gus, ws, logit_grad, router_w, hidden, grad_own, gain):
    shards, _, experts, part, ff = ws[0].shape
    own, width = hidden.shape
    count = len(gus)
    kinds = 2
    cols = gus[0].shape[1]
    anys = pl.BlockSpec(memory_space=pl.ANY)
    return pl.pallas_call(
        functools.partial(turn_body, count=count, kinds=kinds, first=0, finish=turn_back),
        grid=(1,),
        in_specs=[anys] * count
        + [
            pl.BlockSpec((shards, kinds, experts, part, ff), lambda i: (0, 0, 0, 0, 0), pipeline_mode=pl.Buffered(1))
            for _ in ws
        ]
        + [WHOLE] * 5,
        out_specs=[WHOLE] * 3,
        out_shape=[
            jax.ShapeDtypeStruct((4, own, width), jnp.bfloat16),
            jax.ShapeDtypeStruct((own, width), jnp.float32),
            jax.ShapeDtypeStruct((1, width), jnp.float32),
        ],
        scratch_shapes=[
            pltpu.VMEM((2, count, own, cols), jnp.bfloat16),
            pltpu.SemaphoreType.DMA((2, count)),
            pltpu.VMEM((4, own, width), jnp.bfloat16),
            pltpu.VMEM((4, own, width), jnp.bfloat16),
            pltpu.VMEM((4, own, width), jnp.bfloat16),
            pltpu.VMEM((6, own // 2, width), jnp.bfloat16),
            pltpu.VMEM((own, width), jnp.float32),
            pltpu.SemaphoreType.DMA((2, 13)),
        ],
        compiler_params=pltpu.CompilerParams(vmem_limit_bytes=VL, collective_id=2, has_side_effects=True),
        cost_estimate=busy(75),
        name="turn",
    )(*gus, *ws, logit_grad, router_w, hidden, grad_own, gain)


from jax.sharding import PartitionSpec as P

rope_base = 10000.0
CHUNKS = 4
bf16 = jnp.bfloat16
f32 = jnp.float32


def rope_tables(positions):
    half = HD // 2
    frequency = rope_base ** (-2.0 * jnp.arange(half, dtype=f32) / HD)
    angles = positions.astype(f32)[:, None] * frequency[None, :]
    return jnp.cos(angles)[:, None, :], jnp.sin(angles)[:, None, :]


def busy(us):
    return pl.CostEstimate(flops=int(us * 1e9), bytes_accessed=1 << 20, transcendentals=0)


def swap(x):
    return lax.ppermute(x, "ctx", [(0, 1), (1, 0)])


def after(x, *done):
    return lax.optimization_barrier((x, *done))


def rotate(values, cosine, sine):
    shaped = values.reshape(values.shape[0], -1, HD)
    a, b = shaped[:, :, : HD // 2], shaped[:, :, HD // 2 :]
    return jnp.concatenate([a * cosine - b * sine, b * cosine + a * sine], axis=2)


def per_device(
    tokens, out_grad, doc_ids, block_ids, expert_ids, norm1_gain, w_query, w_key, w_value, w_out,
    norm2_gain, w_router, w_gate, w_up, w_down,
):
    shards = lax.axis_size("fsdp")
    ctx_size = lax.axis_size("ctx")
    tp_size = lax.axis_size("tp")
    ctx = lax.axis_index("ctx")
    tp = lax.axis_index("tp")
    rows, width = tokens.shape
    part = width // shards
    own = rows // tp_size
    length = doc_ids.shape[0]
    q_width, kv_width = w_query.shape[1], w_key.shape[1]
    heads, kv_heads = q_width // HD, kv_width // HD
    experts = w_gate.shape[0]
    mine = experts // ctx_size
    each = mine // CHUNKS
    ff = w_gate.shape[2]

    small = jnp.concatenate([w_router, norm1_gain[:, None], norm2_gain[:, None]], axis=1)
    ordered = lambda here, there, axis=0: jnp.concatenate(
        [jnp.where(ctx == 0, here, there), jnp.where(ctx == 0, there, here)], axis=axis
    )
    spare = -small.shape[1] % 128
    packed = jnp.concatenate(
        [w_query, w_key, w_value, w_out.T, small, jnp.zeros((part, spare), bf16)], axis=1
    )
    packed = lax.all_gather(packed, "fsdp", axis=0, tiled=True)
    shard_list = []
    for chunk in range(CHUNKS):
        first = ctx * mine + chunk * each
        pick = lambda w: lax.dynamic_slice_in_dim(w, first, each, 0)
        shard_list.append(jnp.stack([pick(w_gate), pick(w_up), pick(w_down).transpose(0, 2, 1)]))
    packed, *shard_list = after(packed, *shard_list)
    qkv_w = packed[:, : q_width + 2 * kv_width]
    at = q_width + 2 * kv_width
    out_w = packed[:, at : at + q_width]
    at += q_width
    router_w = packed[:, at : at + experts]
    gain_one = packed[:, at + experts].astype(f32)
    gain_two = packed[:, at + experts + 1].astype(f32)

    stacked = [lax.all_gather(shard, "fsdp", axis=0) for shard in shard_list]
    ids_all = ordered(expert_ids, swap(expert_ids))

    inputs = tokens.astype(f32)
    rms_one = lax.rsqrt(jnp.mean(inputs * inputs, axis=1, keepdims=True) + epsilon)
    normed = (inputs * rms_one * gain_one).astype(bf16)
    start = ctx * rows
    cosine, sine = rope_tables(start + jnp.arange(rows, dtype=jnp.int32))
    kv_lin = jnp.dot(normed, qkv_w[:, q_width:], preferred_element_type=f32)
    keys_values = jnp.concatenate(
        [rotate(kv_lin[:, :kv_width], cosine, sine).reshape(rows, kv_width), kv_lin[:, kv_width:]], axis=1
    ).astype(bf16)
    queries = rotate(jnp.dot(normed, qkv_w[:, :q_width], preferred_element_type=f32), cosine, sine)
    queries = queries.astype(bf16).transpose(1, 0, 2) * bf16(HD**-0.5)
    keys_values = ordered(keys_values, swap(keys_values))
    grad_here, keys_values = after(out_grad, keys_values)
    grad_all = ordered(grad_here, swap(grad_here))
    keys_values = keys_values.reshape(length, 2 * kv_heads, HD).transpose(1, 0, 2)
    keys, values = keys_values[:kv_heads], keys_values[kv_heads:]
    query_doc = lax.dynamic_slice_in_dim(doc_ids, start, rows)
    query_block = lax.dynamic_slice_in_dim(block_ids, start, rows)
    base = start.astype(jnp.int32).reshape(1)
    tokens_own = lax.dynamic_slice_in_dim(tokens, tp * own, own)
    grad_own = lax.dynamic_slice_in_dim(out_grad, tp * own, own)
    attn_mix, hidden, normed_two = mid(
        tokens_own, queries, keys, values, query_doc[:, None], query_block[:, None], doc_ids[None],
        block_ids[None], out_w, gain_two[None],
    )
    normed_two = normed_two.reshape(ctx_size * rows, width)

    logits = jnp.dot(normed_two, router_w, preferred_element_type=f32)
    chosen = jnp.any(ids_all[:, :, None] == jnp.arange(experts, dtype=jnp.int32)[None, None, :], axis=1)
    masked = jnp.where(chosen, logits, masked_score)
    powers = jnp.exp(masked - jnp.max(masked, axis=1, keepdims=True))
    gates = powers / jnp.sum(powers, axis=1, keepdims=True)
    gates_mine = jnp.where(ctx == 0, gates[:, :mine], gates[:, mine:])

    normed_t, grad_t = normed_two.T, grad_all.T
    inner_all, outer_all, dots_all, shard_grads = [], [], [], []
    for chunk in range(CHUNKS):
        inner, outer, grads, dots = moe_main(
            normed_two, grad_all, normed_t, grad_t,
            gates_mine[:, chunk * each : (chunk + 1) * each], stacked[chunk],
        )
        inner_all.append(inner)
        outer_all.append(outer)
        dots_all.append(dots)
        shard_grads.append(lax.psum_scatter(grads, "fsdp", scatter_dimension=0, tiled=False))
    combined = moe_back(inner_all, stacked, 2, 1)

    dots = jnp.concatenate(dots_all, axis=1)
    weighted = gates * ordered(dots, jnp.zeros_like(dots), axis=1)
    dots_sum = jnp.sum(weighted, axis=1, keepdims=True)
    logit_grad = (weighted - gates * dots_sum).astype(bf16)
    router_grad = lax.dot_general(
        logit_grad, normed_two, (((0,), (0,)), ((), ())), preferred_element_type=f32
    )
    grad_own, shard_grads[0] = after(grad_own, shard_grads[0])
    branch_grad, hidden_grad, gain_two_grad = turn(
        outer_all, stacked, logit_grad, router_w, hidden, grad_own, gain_two[None]
    )
    branch_grad, *first = after(branch_grad, *shard_grads[:3])
    there = [swap(piece) for piece in first]
    branch_grad = branch_grad.reshape(rows, width)

    out_w_grad = lax.dot_general(
        branch_grad, attn_mix, (((0,), (0,)), ((), ())), preferred_element_type=f32
    )
    mix_grad = jnp.dot(branch_grad, out_w, preferred_element_type=f32).astype(bf16)
    query_grad, key_grad, value_grad = flash_bwd(
        base, queries, mix_grad.reshape(rows, heads, HD).transpose(1, 0, 2), keys, values,
        query_doc[None], query_block[None], doc_ids[:, None], block_ids[:, None],
    )
    query_grad, key_grad, value_grad, *there = after(query_grad, key_grad, value_grad, *there)
    kv_grad = jnp.concatenate([key_grad, value_grad], axis=0).transpose(1, 0, 2).reshape(length, 2 * kv_width)
    kv_grad = kv_grad.astype(bf16)
    kept = lax.dynamic_slice_in_dim(kv_grad, start, rows)
    given = lax.dynamic_slice_in_dim(kv_grad, rows - start, rows)
    kv_grad = kept.astype(f32) + swap(given).astype(f32)
    kv_grad, last = after(kv_grad, shard_grads[3])
    there.append(swap(last))
    query_grad = (query_grad * HD**-0.5).transpose(1, 0, 2).reshape(rows, q_width)
    turned_grad = rotate(
        jnp.concatenate([query_grad, kv_grad[:, :kv_width]], axis=1), cosine, -sine
    ).reshape(rows, q_width + kv_width)
    lin_grad = jnp.concatenate([turned_grad, kv_grad[:, kv_width:]], axis=1).astype(bf16)
    qkv_grad = lax.dot_general(normed, lin_grad, (((0,), (0,)), ((), ())), preferred_element_type=f32)

    small_grads = jnp.concatenate(
        [router_grad, gain_two_grad, jnp.zeros((8 - (experts + 1) % 8, width), f32)], axis=0
    )
    input_grad, small_grads = tail(
        tokens_own, hidden_grad, lin_grad, qkv_w, gain_one[None], small_grads, shards
    )
    input_grad = input_grad.reshape(rows, width)
    hidden, small_grads = after(hidden, small_grads)
    mixed = lax.psum_scatter(combined, ("ctx", "tp"), scatter_dimension=0, tiled=True)
    block_out = lax.all_gather((hidden + mixed.astype(f32)).astype(bf16), "tp", axis=0, tiled=True)

    big = jnp.concatenate([qkv_grad, out_w_grad], axis=1).astype(bf16)
    big = lax.psum_scatter(big, "fsdp", scatter_dimension=0, tiled=True)
    big = big.astype(f32) + swap(big).astype(f32)
    gate_s, up_s, down_s = [
        ordered(
            jnp.concatenate([piece[kind] for piece in shard_grads]),
            jnp.concatenate([piece[kind] for piece in there]),
        ).astype(f32)
        for kind in range(3)
    ]
    at = q_width + 2 * kv_width
    return (
        block_out,
        input_grad,
        small_grads[-1],
        big[:, :q_width],
        big[:, q_width : q_width + kv_width],
        big[:, q_width + kv_width : at],
        big[:, at : at + q_width].T,
        small_grads[experts],
        small_grads[:experts].T,
        gate_s,
        up_s,
        down_s.transpose(0, 2, 1),
    )


def solution(mesh):
    rows = P(("fsdp", "ctx"), None)
    return jax.shard_map(
        per_device,
        mesh=mesh,
        in_specs=(
            rows, rows, P("fsdp"), P("fsdp"), rows, P("fsdp"), P("fsdp", "tp"), P("fsdp", "tp"),
            P("fsdp", "tp"), P("tp", "fsdp"), P("fsdp"), P("fsdp", None), P(None, "fsdp", "tp"),
            P(None, "fsdp", "tp"), P(None, "tp", "fsdp"),
        ),
        out_specs=(
            rows, rows, P("fsdp"), P("fsdp", "tp"), P("fsdp", "tp"), P("fsdp", "tp"), P("tp", "fsdp"),
            P("fsdp"), P("fsdp", None), P(None, "fsdp", "tp"), P(None, "fsdp", "tp"), P(None, "tp", "fsdp"),
        ),
        check_vma=False,
    )
```

```python
import functools
import jax
import jax.numpy as jnp
from jax import lax
from jax.experimental import pallas as pl
from jax.experimental.pallas import tpu as pltpu

HD = 64
DOC = 1024
BLK = 256
QB = 256
BAND = DOC + 2 * BLK
masked_score = -1e30
epsilon = 1e-06
VL = 60 * 1024 * 1024

def nt(a, b):
    return lax.dot_general(a, b, (((1,), (1,)), ((), ())), preferred_element_type=jnp.float32)

def tn(a, b):
    return lax.dot_general(a, b, (((0,), (0,)), ((), ())), preferred_element_type=jnp.float32)

def nn(a, b):
    return jnp.dot(a, b, preferred_element_type=jnp.float32)

def band_start(row, length):
    return pl.multiple_of(jnp.clip(row - DOC, 0, length - BAND), QB)

def flash_fwd_body(base_ref, q_ref, k_ref, v_ref, docq_ref, blkq_ref, dock_ref, blkk_ref, o_ref, *, share, length):
    step = pl.program_id(0)
    start = band_start(base_ref[0] + step * QB, length)
    keys = pl.ds(start, BAND)
    dock = dock_ref[:, keys]
    blkk = blkk_ref[:, keys]
    ok = (docq_ref[...] == dock) & (blkk <= blkq_ref[...])
    bias = jnp.where(ok, 0.0, masked_score)
    for head in range(q_ref.shape[0]):
        s = nt(q_ref[head], k_ref[head // share, keys, :]) + bias
        top = jnp.max(s, axis=1, keepdims=True)
        e = jnp.exp(s - top)
        p = e * (1.0 / jnp.sum(e, axis=1, keepdims=True))
        o_ref[head] = nn(p.astype(jnp.bfloat16), v_ref[head // share, keys, :]).astype(jnp.bfloat16)

def flash_fwd(base, q, k, v, docq, blkq, dock, blkk):
    heads, rows, _ = q.shape
    kv, length, _ = k.shape
    full = lambda shape: pl.BlockSpec(shape, lambda i, b: (0,) * len(shape))
    return pl.pallas_call(
        functools.partial(flash_fwd_body, share=heads // kv, length=length),
        grid_spec=pltpu.PrefetchScalarGridSpec(
            num_scalar_prefetch=1, grid=(rows // QB,),
            in_specs=[
                pl.BlockSpec((heads, QB, HD), lambda i, b: (0, i, 0)),
                full(k.shape), full(v.shape),
                pl.BlockSpec((QB, 1), lambda i, b: (i, 0)),
                pl.BlockSpec((QB, 1), lambda i, b: (i, 0)),
                full((1, length)), full((1, length)),
            ],
            out_specs=pl.BlockSpec((heads, QB, HD), lambda i, b: (0, i, 0)),
        ),
        out_shape=jax.ShapeDtypeStruct(q.shape, jnp.bfloat16),
        compiler_params=pltpu.CompilerParams(vmem_limit_bytes=VL),
        name="flash_fwd",
    )(base, q, k, v, docq, blkq, dock, blkk)

def flash_bwd_body(base_ref, q_ref, g_ref, k_ref, v_ref, docq_ref, blkq_ref, dock_ref, blkk_ref, dq_ref, dk_ref, dv_ref, *, share, length):
    step = pl.program_id(0)
    start = band_start(base_ref[0] + step * QB, length)
    keys = pl.ds(start, BAND)

    @pl.when(step == 0)
    def _():
        dk_ref[...] = jnp.zeros_like(dk_ref)
        dv_ref[...] = jnp.zeros_like(dv_ref)

    ok = (docq_ref[...] == dock_ref[keys, :]) & (blkk_ref[keys, :] <= blkq_ref[...])
    bias = jnp.where(ok, 0.0, masked_score)
    for head in range(q_ref.shape[0]):
        kvh = head // share
        q = q_ref[head]
        g = g_ref[head]
        k = k_ref[kvh, keys, :]
        s = nt(k, q) + bias
        e = jnp.exp(s - jnp.max(s, axis=0, keepdims=True))
        p = e * (1.0 / jnp.sum(e, axis=0, keepdims=True))
        dp = nt(v_ref[kvh, keys, :], g)
        delta = jnp.sum(dp * p, axis=0, keepdims=True)
        ds = (p * (dp - delta)).astype(jnp.bfloat16)
        dq_ref[head] = tn(ds, k)
        dk_ref[kvh, keys, :] += nn(ds, q)
        dv_ref[kvh, keys, :] += nn(p.astype(jnp.bfloat16), g)

def flash_bwd(base, q, g, k, v, docq, blkq, dock, blkk):
    heads, rows, _ = q.shape
    kv, length, _ = k.shape
    full = lambda shape: pl.BlockSpec(shape, lambda i, b: (0,) * len(shape))
    return pl.pallas_call(
        functools.partial(flash_bwd_body, share=heads // kv, length=length),
        grid_spec=pltpu.PrefetchScalarGridSpec(
            num_scalar_prefetch=1, grid=(rows // QB,),
            in_specs=[
                pl.BlockSpec((heads, QB, HD), lambda i, b: (0, i, 0)),
                pl.BlockSpec((heads, QB, HD), lambda i, b: (0, i, 0)),
                full(k.shape), full(v.shape),
                pl.BlockSpec((1, QB), lambda i, b: (0, i)),
                pl.BlockSpec((1, QB), lambda i, b: (0, i)),
                full((length, 1)), full((length, 1)),
            ],
            out_specs=[
                pl.BlockSpec((heads, QB, HD), lambda i, b: (0, i, 0)),
                full(k.shape), full(v.shape),
            ],
        ),
        out_shape=[
            jax.ShapeDtypeStruct(q.shape, jnp.float32),
            jax.ShapeDtypeStruct(k.shape, jnp.float32),
            jax.ShapeDtypeStruct(v.shape, jnp.float32),
        ],
        compiler_params=pltpu.CompilerParams(vmem_limit_bytes=VL),
        cost_estimate=busy(55),
        name="flash_bwd",
    )(base, q, g, k, v, docq, blkq, dock, blkk)

PAIR = 2
TM = 512

def moe_body(base_ref, x_ref, g_ref, xt_ref, gt_ref, gates_ref, prev_ref, w_ref, a_ref, gu_ref, grads_ref, dots_ref):
    rows, width = x_ref.shape
    shards, _, pair, part, ff = w_ref.shape
    step = pl.program_id(0)

    def weights(which):
        return jnp.concatenate(
            [jnp.concatenate([w_ref[z, which, e] for z in range(shards)], axis=0) for e in range(pair)], axis=1
        )

    gate_w = weights(0)
    up_w = weights(1)
    down_w = weights(2)
    experts = gates_ref.shape[1]
    lane = base_ref[0] + step * pair

    def tile(i, carry):
        here = pl.ds(pl.multiple_of(i * TM, TM), TM)
        x = x_ref[here, :]
        gate_val = nn(x, gate_w)
        up_val = nn(x, up_w)
        back = nn(g_ref[here, :], down_w)
        lanes = lax.broadcasted_iota(jnp.int32, (TM, experts), 1)
        gates = gates_ref[here, :]
        gate = jnp.concatenate(
            [
                jnp.broadcast_to(
                    jnp.sum(jnp.where(lanes == lane + e, gates, 0.0), axis=1, keepdims=True), (TM, ff)
                )
                for e in range(pair)
            ],
            axis=1,
        )
        sig = 1.0 / (1.0 + jnp.exp(-gate_val))
        silu = gate_val * sig
        inner = silu * up_val
        a_ref[here, :] = (inner * gate).astype(jnp.bfloat16)
        prod = inner * back
        dots = jnp.where(step == 0, prev_ref[here, :], dots_ref[here, :])
        for e in range(pair):
            total = jnp.sum(prod[:, e * ff : (e + 1) * ff], axis=1, keepdims=True)
            dots = jnp.where(lanes == lane + e, total, dots)
        dots_ref[here, :] = dots
        back = back * gate
        gu_ref[here, : pair * ff] = (back * up_val * sig * (1.0 + gate_val * (1.0 - sig))).astype(jnp.bfloat16)
        gu_ref[here, pair * ff :] = (back * silu).astype(jnp.bfloat16)
        return carry

    lax.fori_loop(0, rows // TM, tile, 0)
    for z in range(shards):
        part_rows = pl.ds(z * part, part)
        both = nn(xt_ref[part_rows, :], gu_ref[...])
        down = nn(gt_ref[part_rows, :], a_ref[...])
        for e in range(pair):
            grads_ref[z, 0, e] = both[:, e * ff : (e + 1) * ff].astype(jnp.bfloat16)
            grads_ref[z, 1, e] = both[:, (pair + e) * ff : (pair + e + 1) * ff].astype(jnp.bfloat16)
            grads_ref[z, 2, e] = down[:, e * ff : (e + 1) * ff].astype(jnp.bfloat16)

def moe_main(base, x, g, xt, gt, gates, dots, w):
    rows, width = x.shape
    shards, three, count, part, ff = w.shape
    one = lambda shape: pl.BlockSpec(shape, lambda i: (0,) * len(shape), pipeline_mode=pl.Buffered(1))
    return pl.pallas_call(
        moe_body,
        grid=(count // PAIR,),
        in_specs=[
            SMEMS, one(x.shape), one(g.shape), one(xt.shape), one(gt.shape), one(gates.shape), one(dots.shape),
            pl.BlockSpec((shards, 3, PAIR, part, ff), lambda i: (0, 0, i, 0, 0)),
        ],
        out_specs=[
            pl.BlockSpec((rows, PAIR * ff), lambda i: (0, i)),
            pl.BlockSpec((rows, 2 * PAIR * ff), lambda i: (0, i)),
            pl.BlockSpec((shards, 3, PAIR, part, ff), lambda i: (0, 0, i, 0, 0)),
            one(dots.shape),
        ],
        out_shape=[
            jax.ShapeDtypeStruct((rows, count * ff), jnp.bfloat16),
            jax.ShapeDtypeStruct((rows, 2 * count * ff), jnp.bfloat16),
            jax.ShapeDtypeStruct(w.shape, jnp.bfloat16),
            jax.ShapeDtypeStruct(dots.shape, jnp.float32),
        ],
        compiler_params=pltpu.CompilerParams(vmem_limit_bytes=VL),
        cost_estimate=pl.CostEstimate(flops=2 * rows * width * count * ff * 6, bytes_accessed=8 * rows * width + 12 * count * ff * width, transcendentals=0),
        name="moe_main",
        input_output_aliases={6: 3},
    )(base, x, g, xt, gt, gates, dots, w)

def back_body(*refs, count, first, kinds):
    gu_refs, w_refs, o_ref = refs[:count], refs[count : 2 * count], refs[2 * count]
    shards, _, experts, part, ff = w_refs[0].shape
    for z in range(shards):
        total = None
        for gu_ref, w_ref in zip(gu_refs, w_refs):
            w = jnp.concatenate(
                [
                    w_ref[z, kind, p * PAIR + e]
                    for p in range(experts // PAIR)
                    for kind in range(kinds)
                    for e in range(PAIR)
                ],
                axis=1,
            )
            piece = nt(gu_ref[...], w)
            total = piece if total is None else total + piece
        o_ref[:, z * part : (z + 1) * part] = total.astype(o_ref.dtype)


def moe_back(gus, ws, first, kinds):
    shards, three, experts, part, ff = ws[0].shape
    rows = gus[0].shape[0]
    width = shards * part
    count = len(gus)
    return pl.pallas_call(
        functools.partial(back_body, count=count, first=first, kinds=kinds),
        grid=(rows // TM,),
        in_specs=[pl.BlockSpec((TM, kinds * experts * ff), lambda i: (i, 0)) for _ in gus]
        + [
            pl.BlockSpec(
                (shards, kinds, experts, part, ff),
                lambda i: (0, first // kinds, 0, 0, 0),
                pipeline_mode=pl.Buffered(1),
            )
            for _ in ws
        ],
        out_specs=pl.BlockSpec((TM, width), lambda i: (i, 0)),
        out_shape=jax.ShapeDtypeStruct((rows, width), jnp.bfloat16),
        compiler_params=pltpu.CompilerParams(vmem_limit_bytes=VL),
        cost_estimate=pl.CostEstimate(
            flops=2 * rows * width * count * experts * ff * kinds,
            bytes_accessed=2 * rows * kinds * count * experts * ff,
            transcendentals=0,
        ),
        name="moe_back" if kinds == 2 else "moe_out",
    )(*gus, *ws)


MESH = pl.DeviceIdType.MESH


class Place:
    def __init__(self):
        self.ctx = lax.axis_index("ctx")
        self.tp = lax.axis_index("tp")
        self.core = lax.rem(self.tp, 2)
        self.high = self.tp // 2
        self.pair_tp = self.high * 2 + 1 - self.core
        self.far_tp = (1 - self.high) * 2 + self.core
        self.cross_tp = (1 - self.high) * 2 + 1 - self.core
        self.pair = {"tp": self.pair_tp}
        self.far = {"tp": self.far_tp}
        self.side = {"ctx": 1 - self.ctx}

    def meet(self, who):
        barrier = pltpu.get_barrier_semaphore()
        for device in who:
            pl.semaphore_signal(barrier, inc=1, device_id=device, device_id_type=MESH)
        pl.semaphore_wait(barrier, len(who))


def push(src, dst, sems, slot, device):
    return pltpu.make_async_remote_copy(
        src_ref=src, dst_ref=dst, send_sem=sems.at[0, slot], recv_sem=sems.at[1, slot],
        device_id=device, device_id_type=MESH,
    )


def gather_four(place, all_ref, sems, at):
    here, far = all_ref.at[place.tp], all_ref.at[place.far_tp]
    to_far = push(here, here, sems, at, place.far)
    to_pair = push(here, here, sems, at + 1, place.pair)
    to_far.start()
    to_pair.start()
    to_far.wait_recv()
    on = push(far, far, sems, at + 2, place.pair)
    on.start()
    to_pair.wait_recv()
    on.wait_recv()
    to_far.wait_send()
    to_pair.wait_send()
    on.wait_send()


def gather_eight(place, all_ref, sems, at):
    rows = all_ref.shape[1]
    top, low = pl.ds(0, rows // 2), pl.ds(rows // 2, rows // 2)
    part = lambda ctx, tp: all_ref.at[ctx * 4 + tp]
    other = 1 - place.ctx
    here = part(place.ctx, place.tp)
    side = part(other, place.tp)
    far = part(place.ctx, place.far_tp)
    cross = part(other, place.far_tp)
    side_top, far_low = side.at[top], far.at[low]
    cross_top, cross_low = cross.at[top], cross.at[low]
    to_side = push(here, here, sems, at, place.side)
    to_far = push(here, here, sems, at + 1, place.far)
    to_pair = push(here, here, sems, at + 2, place.pair)
    for copy in (to_side, to_far, to_pair):
        copy.start()
    to_side.wait_recv()
    turn_far = push(side_top, side_top, sems, at + 3, place.far)
    pair_side = push(side, side, sems, at + 5, place.pair)
    turn_far.start()
    pair_side.start()
    to_far.wait_recv()
    turn_side = push(far_low, far_low, sems, at + 4, place.side)
    pair_far = push(far, far, sems, at + 6, place.pair)
    turn_side.start()
    pair_far.start()
    turn_far.wait_recv()
    pair_top = push(cross_top, cross_top, sems, at + 7, place.pair)
    pair_top.start()
    turn_side.wait_recv()
    pair_low = push(cross_low, cross_low, sems, at + 8, place.pair)
    pair_low.start()
    for copy in (to_pair, pair_side, pair_far, pair_top, pair_low):
        copy.wait_recv()
    for copy in (to_side, to_far, to_pair, turn_far, turn_side, pair_side, pair_far, pair_top, pair_low):
        copy.wait_send()


def reduce_four(place, produce, send_ref, pair_in, far_in, own_ref, sems, at):
    def fold(j):
        slot = j // 2

        @pl.when(lax.rem(j, 2) == place.core)
        def _():
            push(send_ref.at[j], pair_in.at[slot], sems, at + slot, place.pair).wait_recv()
            total = send_ref[j].astype(jnp.float32) + pair_in[slot].astype(jnp.float32)

            @pl.when(slot == place.high)
            def _():
                own_ref[...] = total

            @pl.when(slot != place.high)
            def _():
                send_ref[j] = total.astype(jnp.bfloat16)
                push(send_ref.at[j], far_in, sems, at + 2, place.far).start()

    def step(j, carry):
        produce(j)

        @pl.when(lax.rem(j, 2) != place.core)
        def _():
            slot = j // 2
            push(send_ref.at[j], pair_in.at[slot], sems, at + slot, place.pair).start()

        @pl.when(j > 0)
        def _():
            fold(j - 1)

        return carry

    lax.fori_loop(0, 4, step, 0)
    fold(3)
    last = push(send_ref.at[place.far_tp], far_in, sems, at + 2, place.far)
    last.wait_recv()
    own_ref[...] += far_in[...].astype(jnp.float32)
    last.wait_send()
    for slot in range(2):
        push(send_ref.at[place.pair_tp], pair_in.at[slot], sems, at + slot, place.pair).wait_send()


SMEMS = pl.BlockSpec(memory_space=pltpu.SMEM)
WHOLE = pl.BlockSpec(memory_space=pltpu.VMEM)


def normalize(x):
    r = lax.rsqrt(jnp.mean(x * x, axis=1, keepdims=True) + epsilon)
    return r, x * r


def mid_body(tok_ref, q_ref, k_ref, v_ref, docq_ref, blkq_ref, dock_ref, blkk_ref, w_ref, gain_ref,
             mix_ref, hid_ref, all_ref, send, pair_in, far_in, own, sems, *, share, length):
    place = Place()
    place.meet((place.pair, place.far, place.side))
    heads, rows, _ = q_ref.shape
    block = rows // 4
    band = min(DOC + block + BLK, length)

    def produce(j):
        at = pl.multiple_of(j * block, block)
        here = pl.ds(at, block)
        start = pl.multiple_of(jnp.clip(place.ctx * rows + at - DOC, 0, length - band), 128)
        keys = pl.ds(start, band)
        ok = (docq_ref[here, :] == dock_ref[:, keys]) & (blkk_ref[:, keys] <= blkq_ref[here, :])
        bias = jnp.where(ok, 0.0, masked_score)
        outs = []
        for head in range(heads):
            s = nt(q_ref[head, here, :], k_ref[head // share, keys, :]) + bias
            e = jnp.exp(s - jnp.max(s, axis=1, keepdims=True))
            p = e * (1.0 / jnp.sum(e, axis=1, keepdims=True))
            outs.append(nn(p.astype(jnp.bfloat16), v_ref[head // share, keys, :]).astype(jnp.bfloat16))
        mix = jnp.concatenate(outs, axis=1)
        mix_ref[here, :] = mix
        send[j] = nt(mix, w_ref[...]).astype(jnp.bfloat16)

    reduce_four(place, produce, send, pair_in, far_in, own, sems, 0)
    hidden = tok_ref[...].astype(jnp.float32) + own[...]
    hid_ref[...] = hidden
    all_ref[place.ctx * 4 + place.tp] = (normalize(hidden)[1] * gain_ref[...]).astype(jnp.bfloat16)
    gather_eight(place, all_ref, sems, 3)


def mid(tok, q, k, v, docq, blkq, dock, blkk, out_w, gain):
    heads, rows, _ = q.shape
    kv, length, _ = k.shape
    own, width = tok.shape
    return pl.pallas_call(
        functools.partial(mid_body, share=heads // kv, length=length),
        in_specs=[WHOLE] * 10,
        out_specs=[WHOLE] * 3,
        out_shape=[
            jax.ShapeDtypeStruct((rows, heads * HD), jnp.bfloat16),
            jax.ShapeDtypeStruct((own, width), jnp.float32),
            jax.ShapeDtypeStruct((8, own, width), jnp.bfloat16),
        ],
        scratch_shapes=[
            pltpu.VMEM((4, own, width), jnp.bfloat16),
            pltpu.VMEM((2, own, width), jnp.bfloat16),
            pltpu.VMEM((own, width), jnp.bfloat16),
            pltpu.VMEM((own, width), jnp.float32),
            pltpu.SemaphoreType.DMA((2, 12)),
        ],
        compiler_params=pltpu.CompilerParams(vmem_limit_bytes=VL, collective_id=0, has_side_effects=True),
        cost_estimate=busy(100),
        name="mid",
    )(tok, q, k, v, docq, blkq, dock, blkk, out_w, gain)


def tail_body(tok_ref, hg_ref, lin_ref, w_ref, gain_ref, small_ref, all_ref, sum_ref,
              send, pair_in, far_in, own, mine, theirs, split, split_in, sems, small_sems, *, shards):
    place = Place()
    z = lax.axis_index("fsdp")
    others = [{"fsdp": lax.rem(z + d, shards)} for d in range(1, shards)]
    place.meet((place.pair, place.far, place.side, *others))
    block = lin_ref.shape[0] // 4
    part = sum_ref.shape[1]

    def produce(j):
        here = pl.ds(pl.multiple_of(j * block, block), block)
        send[j] = nt(lin_ref[here, :], w_ref[...]).astype(jnp.bfloat16)

    reduce_four(place, produce, send, pair_in, far_in, own, sems, 0)
    one_grad = own[...]
    r, xhat = normalize(tok_ref[...].astype(jnp.float32))
    n = one_grad * gain_ref[...]
    grad = hg_ref[...] + r * (n - xhat * jnp.mean(n * xhat, axis=1, keepdims=True))
    all_ref[place.tp] = grad.astype(jnp.bfloat16)
    row = lax.broadcasted_iota(jnp.int32, small_ref.shape, 0)
    mine[0] = jnp.where(
        row == small_ref.shape[0] - 1, jnp.sum(one_grad * xhat, axis=0, keepdims=True), small_ref[...]
    )
    hops = [
        push(mine.at[i], theirs.at[i], small_sems, i, device)
        for i, device in enumerate((place.pair, place.side, place.far))
    ]
    hops[0].start()
    here, far = all_ref.at[place.tp], all_ref.at[place.far_tp]
    to_far = push(here, here, sems, 3, place.far)
    to_pair = push(here, here, sems, 4, place.pair)
    to_far.start()
    to_pair.start()
    for i in range(2):
        hops[i].wait_recv()
        mine[i + 1] = mine[i] + theirs[i]
        hops[i + 1].start()
    to_far.wait_recv()
    on = push(far, far, sems, 5, place.pair)
    on.start()
    hops[2].wait_recv()
    total = mine[2] + theirs[2]
    for j in range(shards):
        split[j] = total[:, j * part : (j + 1) * part]
    spread = [
        push(split.at[lax.rem(z + d, shards)], split_in.at[d - 1], small_sems, 2 + d, others[d - 1])
        for d in range(1, shards)
    ]
    for copy in spread:
        copy.start()
    to_pair.wait_recv()
    on.wait_recv()
    result = split[z]
    for d in range(1, shards):
        spread[d - 1].wait_recv()
        result = result + split_in[d - 1]
    sum_ref[...] = result
    for copy in (to_far, to_pair, on, *hops, *spread):
        copy.wait_send()


def tail(tok, hidden_grad, lin_grad, qkv_w, gain, small, shards):
    own, width = tok.shape
    count = small.shape[0]
    part = width // shards
    return pl.pallas_call(
        functools.partial(tail_body, shards=shards),
        in_specs=[WHOLE] * 6,
        out_specs=[WHOLE] * 2,
        out_shape=[
            jax.ShapeDtypeStruct((4, own, width), jnp.bfloat16),
            jax.ShapeDtypeStruct((count, part), jnp.float32),
        ],
        scratch_shapes=[
            pltpu.VMEM((4, own, width), jnp.bfloat16),
            pltpu.VMEM((2, own, width), jnp.bfloat16),
            pltpu.VMEM((own, width), jnp.bfloat16),
            pltpu.VMEM((own, width), jnp.float32),
            pltpu.VMEM((3, count, width), jnp.float32),
            pltpu.VMEM((3, count, width), jnp.float32),
            pltpu.VMEM((shards, count, part), jnp.float32),
            pltpu.VMEM((shards - 1, count, part), jnp.float32),
            pltpu.SemaphoreType.DMA((2, 6)),
            pltpu.SemaphoreType.DMA((2, 2 + shards)),
        ],
        compiler_params=pltpu.CompilerParams(vmem_limit_bytes=VL, collective_id=1, has_side_effects=True),
        cost_estimate=busy(50),
        name="tail",
    )(tok, hidden_grad, lin_grad, qkv_w, gain, small)


def turn_body(*refs, count, kinds, first, finish):
    gu_refs, w_refs = refs[:count], refs[count : 2 * count]
    lg_ref, router_ref, hid_ref, extra_ref, gain_ref = refs[2 * count : 2 * count + 5]
    outs = refs[2 * count + 5 : 2 * count + 8]
    gu_buf, gu_sem, give, keep, pair_in, cut, own, sems = refs[2 * count + 8 :]
    all_ref = outs[0]
    place = Place()
    place.meet((place.pair, place.far, place.side))
    block = hid_ref.shape[0]
    shards, _, experts, part, ff = w_refs[0].shape
    half = block // 2
    top, low = pl.ds(0, half), pl.ds(half, half)
    bf = jnp.bfloat16
    f = jnp.float32
    order = [(1, 1), (1, 0), (0, 1), (0, 0)]

    def tile_of(step):
        dx, dy = order[step // 2]
        ctx = place.ctx + dx * (1 - 2 * place.ctx)
        high = place.high + dy * (1 - 2 * place.high)
        core = 1 - place.core if step % 2 == 0 else place.core
        return ctx * 4 + high * 2 + core

    def fetch(step):
        at = pl.ds(pl.multiple_of(tile_of(step) * block, block), block)
        return [
            pltpu.make_async_copy(gu.at[at, :], gu_buf.at[step % 2, n], gu_sem.at[step % 2, n])
            for n, gu in enumerate(gu_refs)
        ]

    for copy in fetch(0):
        copy.start()

    def compute(step, dst):
        for copy in fetch(step):
            copy.wait()
        if step + 1 < 8:
            for copy in fetch(step + 1):
                copy.start()
        at = pl.ds(pl.multiple_of(tile_of(step) * block, block), block)
        for z in range(shards):
            cols = slice(z * part, (z + 1) * part)
            total = None
            if lg_ref is not None:
                total = nt(lg_ref[at, :], router_ref[cols, :])
            for n, w_ref in enumerate(w_refs):
                w = jnp.concatenate(
                    [
                        w_ref[z, kind, p * PAIR + e]
                        for p in range(experts // PAIR)
                        for kind in range(kinds)
                        for e in range(PAIR)
                    ],
                    axis=1,
                )
                piece = nt(gu_buf[step % 2, n], w)
                total = piece if total is None else total + piece
            dst[:, cols] = total.astype(bf)

    copies = []

    def send(src, dst, slot, device):
        copy = push(src, dst, sems, slot, device)
        copy.start()
        copies.append(copy)
        return copy

    for k in range(4):
        compute(2 * k, give.at[k])
        got = send(give.at[k], pair_in.at[k], k, place.pair)
        compute(2 * k + 1, keep.at[k])
        got.wait_recv()
        total = keep[k].astype(f) + pair_in[k].astype(f)
        if k == 0:
            keep[k] = total.astype(bf)
            a_cross = send(keep.at[k, top], cut.at[0], 4, place.side)
            b_cross = send(keep.at[k, low], cut.at[1], 5, place.far)
        elif k == 1:
            b_cross.wait_recv()
            keep[k, top] = total[:half].astype(bf)
            keep[k, low] = (total[half:] + cut[1].astype(f)).astype(bf)
            a_first = send(keep.at[k, top], cut.at[2], 6, place.side)
            b_last = send(keep.at[k, low], cut.at[5], 9, place.side)
        elif k == 2:
            a_cross.wait_recv()
            keep[k, low] = total[half:].astype(bf)
            keep[k, top] = (total[:half] + cut[0].astype(f)).astype(bf)
            b_first = send(keep.at[k, low], cut.at[4], 8, place.far)
            a_last = send(keep.at[k, top], cut.at[3], 7, place.far)
        else:
            for copy in (a_first, a_last, b_first, b_last):
                copy.wait_recv()
            own[top, :] = total[:half] + cut[2].astype(f) + cut[3].astype(f)
            own[low, :] = total[half:] + cut[4].astype(f) + cut[5].astype(f)
    finish(place, own, hid_ref, extra_ref, gain_ref, outs)
    gather_four(place, all_ref, sems, 10)
    for copy in copies:
        copy.wait_send()


def turn_back(place, own, hid_ref, grad_ref, gain_ref, outs):
    all_ref, hg_ref, gg_ref = outs
    two_grad = own[...]
    r, hhat = normalize(hid_ref[...])
    gg_ref[...] = jnp.sum(two_grad * hhat, axis=0, keepdims=True)
    m = two_grad * gain_ref[...]
    grad = grad_ref[...].astype(jnp.float32) + r * (m - hhat * jnp.mean(m * hhat, axis=1, keepdims=True))
    hg_ref[...] = grad
    all_ref[place.tp] = grad.astype(jnp.bfloat16)


def turn(gus, ws, logit_grad, router_w, hidden, grad_own, gain):
    shards, _, experts, part, ff = ws[0].shape
    own, width = hidden.shape
    count = len(gus)
    kinds = 2
    cols = gus[0].shape[1]
    anys = pl.BlockSpec(memory_space=pl.ANY)
    return pl.pallas_call(
        functools.partial(turn_body, count=count, kinds=kinds, first=0, finish=turn_back),
        grid=(1,),
        in_specs=[anys] * count
        + [
            pl.BlockSpec((shards, kinds, experts, part, ff), lambda i: (0, 0, 0, 0, 0), pipeline_mode=pl.Buffered(1))
            for _ in ws
        ]
        + [WHOLE] * 5,
        out_specs=[WHOLE] * 3,
        out_shape=[
            jax.ShapeDtypeStruct((4, own, width), jnp.bfloat16),
            jax.ShapeDtypeStruct((own, width), jnp.float32),
            jax.ShapeDtypeStruct((1, width), jnp.float32),
        ],
        scratch_shapes=[
            pltpu.VMEM((2, count, own, cols), jnp.bfloat16),
            pltpu.SemaphoreType.DMA((2, count)),
            pltpu.VMEM((4, own, width), jnp.bfloat16),
            pltpu.VMEM((4, own, width), jnp.bfloat16),
            pltpu.VMEM((4, own, width), jnp.bfloat16),
            pltpu.VMEM((6, own // 2, width), jnp.bfloat16),
            pltpu.VMEM((own, width), jnp.float32),
            pltpu.SemaphoreType.DMA((2, 13)),
        ],
        compiler_params=pltpu.CompilerParams(vmem_limit_bytes=VL, collective_id=2, has_side_effects=True),
        cost_estimate=busy(75),
        name="turn",
    )(*gus, *ws, logit_grad, router_w, hidden, grad_own, gain)


from jax.sharding import PartitionSpec as P

rope_base = 10000.0
CHUNKS = 4
bf16 = jnp.bfloat16
f32 = jnp.float32


def rope_tables(positions):
    half = HD // 2
    frequency = rope_base ** (-2.0 * jnp.arange(half, dtype=f32) / HD)
    angles = positions.astype(f32)[:, None] * frequency[None, :]
    return jnp.cos(angles)[:, None, :], jnp.sin(angles)[:, None, :]


def busy(us):
    return pl.CostEstimate(flops=int(us * 1e9), bytes_accessed=1 << 20, transcendentals=0)


def swap(x):
    return lax.ppermute(x, "ctx", [(0, 1), (1, 0)])


def after(x, *done):
    return lax.optimization_barrier((x, *done))


def rotate(values, cosine, sine):
    shaped = values.reshape(values.shape[0], -1, HD)
    a, b = shaped[:, :, : HD // 2], shaped[:, :, HD // 2 :]
    return jnp.concatenate([a * cosine - b * sine, b * cosine + a * sine], axis=2)


def per_device(
    tokens, out_grad, doc_ids, block_ids, expert_ids, norm1_gain, w_query, w_key, w_value, w_out,
    norm2_gain, w_router, w_gate, w_up, w_down,
):
    shards = lax.axis_size("fsdp")
    ctx_size = lax.axis_size("ctx")
    tp_size = lax.axis_size("tp")
    ctx = lax.axis_index("ctx")
    tp = lax.axis_index("tp")
    rows, width = tokens.shape
    part = width // shards
    own = rows // tp_size
    length = doc_ids.shape[0]
    q_width, kv_width = w_query.shape[1], w_key.shape[1]
    heads, kv_heads = q_width // HD, kv_width // HD
    experts = w_gate.shape[0]
    mine = experts // ctx_size
    each = mine // CHUNKS
    ff = w_gate.shape[2]

    front = jnp.concatenate(
        [jnp.concatenate([w_query, w_key, w_value], axis=1),
         jnp.pad(norm1_gain[None], ((0, 7), (0, q_width + 2 * kv_width - part)))], axis=0
    )
    front = lax.all_gather(front, "fsdp", axis=0)
    packed = jnp.concatenate([w_out.T, w_router, norm2_gain[:, None]], axis=1)
    packed = jnp.pad(packed, ((0, 8), (0, 2 * q_width - packed.shape[1])))
    ordered = lambda here, there, axis=0: jnp.concatenate(
        [jnp.where(ctx == 0, here, there), jnp.where(ctx == 0, there, here)], axis=axis
    )
    shard_list = []
    for chunk in range(CHUNKS):
        first = ctx * mine + chunk * each
        pick = lambda w: lax.dynamic_slice_in_dim(w, first, each, 0)
        shard_list.append(jnp.stack([pick(w_gate), pick(w_up), pick(w_down).transpose(0, 2, 1)]))
    front, packed, *shard_list = after(front, packed, *shard_list)
    packed = lax.all_gather(packed, "fsdp", axis=0)[:, :part].reshape(width, 2 * q_width)
    qkv_w = front[:, :part].reshape(width, q_width + 2 * kv_width)
    gain_one = front[:, part, :part].reshape(width).astype(f32)
    out_w = packed[:, :q_width]
    router_w = packed[:, q_width : q_width + experts]
    gain_two = packed[:, q_width + experts].astype(f32)

    stacked = [lax.all_gather(shard, "fsdp", axis=0) for shard in shard_list]
    ids_all = ordered(expert_ids, swap(expert_ids))

    inputs = tokens.astype(f32)
    rms_one = lax.rsqrt(jnp.mean(inputs * inputs, axis=1, keepdims=True) + epsilon)
    normed = (inputs * rms_one * gain_one).astype(bf16)
    start = ctx * rows
    cosine, sine = rope_tables(start + jnp.arange(rows, dtype=jnp.int32))
    kv_lin = jnp.dot(normed, qkv_w[:, q_width:], preferred_element_type=f32)
    keys_values = jnp.concatenate(
        [rotate(kv_lin[:, :kv_width], cosine, sine).reshape(rows, kv_width), kv_lin[:, kv_width:]], axis=1
    ).astype(bf16)
    queries = rotate(jnp.dot(normed, qkv_w[:, :q_width], preferred_element_type=f32), cosine, sine)
    queries = queries.astype(bf16).transpose(1, 0, 2) * bf16(HD**-0.5)
    near = min(DOC, rows)
    apart = lambda x: jnp.where(
        ctx == 0, jnp.pad(x, ((0, rows - near), (0, 0))), jnp.pad(x, ((rows - near, 0), (0, 0)))
    )
    window = lax.dynamic_slice_in_dim(keys_values, jnp.where(ctx == 0, rows - near, 0), near)
    keys_values = ordered(keys_values, apart(swap(window)))
    grad_here, keys_values = after(out_grad, keys_values)
    grad_all = ordered(grad_here, swap(grad_here))
    keys_values = keys_values.reshape(length, 2 * kv_heads, HD).transpose(1, 0, 2)
    keys, values = keys_values[:kv_heads], keys_values[kv_heads:]
    query_doc = lax.dynamic_slice_in_dim(doc_ids, start, rows)
    query_block = lax.dynamic_slice_in_dim(block_ids, start, rows)
    base = start.astype(jnp.int32).reshape(1)
    tokens_own = lax.dynamic_slice_in_dim(tokens, tp * own, own)
    grad_own = lax.dynamic_slice_in_dim(out_grad, tp * own, own)
    attn_mix, hidden, normed_two = mid(
        tokens_own, queries, keys, values, query_doc[:, None], query_block[:, None], doc_ids[None],
        block_ids[None], out_w, gain_two[None],
    )
    normed_two = normed_two.reshape(ctx_size * rows, width)

    logits = jnp.dot(normed_two, router_w, preferred_element_type=f32)
    chosen = jnp.any(ids_all[:, :, None] == jnp.arange(experts, dtype=jnp.int32)[None, None, :], axis=1)
    masked = jnp.where(chosen, logits, masked_score)
    powers = jnp.exp(masked - jnp.max(masked, axis=1, keepdims=True))
    gates = powers / jnp.sum(powers, axis=1, keepdims=True)

    normed_t, grad_t = normed_two.T, grad_all.T
    inner_all, outer_all, shard_grads = [], [], []
    dots = jnp.zeros_like(gates)
    for chunk in range(CHUNKS):
        inner, outer, grads, dots = moe_main(
            (ctx * mine + chunk * each).astype(jnp.int32).reshape(1),
            normed_two, grad_all, normed_t, grad_t, gates, dots, stacked[chunk],
        )
        inner_all.append(inner)
        outer_all.append(outer)
        shard_grads.append(lax.psum_scatter(grads, "fsdp", scatter_dimension=0, tiled=False))
    combined = moe_back(inner_all, stacked, 2, 1)

    weighted = gates * dots
    dots_sum = jnp.sum(weighted, axis=1, keepdims=True)
    logit_grad = (weighted - gates * dots_sum).astype(bf16)
    router_grad = lax.dot_general(
        logit_grad, normed_two, (((0,), (0,)), ((), ())), preferred_element_type=f32
    )
    grad_own, shard_grads[0] = after(grad_own, shard_grads[0])
    branch_grad, hidden_grad, gain_two_grad = turn(
        outer_all, stacked, logit_grad, router_w, hidden, grad_own, gain_two[None]
    )
    branch_grad, *first = after(branch_grad, *shard_grads[:3])
    there = [swap(piece) for piece in first]
    branch_grad = branch_grad.reshape(rows, width)

    out_w_grad = lax.dot_general(
        branch_grad, attn_mix, (((0,), (0,)), ((), ())), preferred_element_type=f32
    )
    mix_grad = jnp.dot(branch_grad, out_w, preferred_element_type=f32).astype(bf16)
    query_grad, key_grad, value_grad = flash_bwd(
        base, queries, mix_grad.reshape(rows, heads, HD).transpose(1, 0, 2), keys, values,
        query_doc[None], query_block[None], doc_ids[:, None], block_ids[:, None],
    )
    query_grad, key_grad, value_grad, *there = after(query_grad, key_grad, value_grad, *there)
    kv_grad = jnp.concatenate([key_grad, value_grad], axis=0).transpose(1, 0, 2).reshape(length, 2 * kv_width)
    kv_grad = kv_grad.astype(bf16)
    kept = lax.dynamic_slice_in_dim(kv_grad, start, rows)
    given = lax.dynamic_slice_in_dim(kv_grad, jnp.where(ctx == 0, rows, rows - near), near)
    got = swap(given)
    got = jnp.where(
        ctx == 0, jnp.pad(got, ((rows - near, 0), (0, 0))), jnp.pad(got, ((0, rows - near), (0, 0)))
    )
    kv_grad = kept.astype(f32) + got.astype(f32)
    kv_grad, last = after(kv_grad, shard_grads[3])
    there.append(swap(last))
    query_grad = (query_grad * HD**-0.5).transpose(1, 0, 2).reshape(rows, q_width)
    turned_grad = rotate(
        jnp.concatenate([query_grad, kv_grad[:, :kv_width]], axis=1), cosine, -sine
    ).reshape(rows, q_width + kv_width)
    lin_grad = jnp.concatenate([turned_grad, kv_grad[:, kv_width:]], axis=1).astype(bf16)
    qkv_grad = lax.dot_general(normed, lin_grad, (((0,), (0,)), ((), ())), preferred_element_type=f32)

    small_grads = jnp.concatenate(
        [router_grad, gain_two_grad, jnp.zeros((8 - (experts + 1) % 8, width), f32)], axis=0
    )
    input_grad, small_grads = tail(
        tokens_own, hidden_grad, lin_grad, qkv_w, gain_one[None], small_grads, shards
    )
    input_grad = input_grad.reshape(rows, width)
    hidden, small_grads, there[-1] = after(hidden, small_grads, there[-1])
    mixed = lax.psum_scatter(combined, ("ctx", "tp"), scatter_dimension=0, tiled=True)
    block_out = lax.all_gather((hidden + mixed.astype(f32)).astype(bf16), "tp", axis=0, tiled=True)

    big = jnp.concatenate([qkv_grad, out_w_grad], axis=1).astype(bf16)
    big = lax.psum_scatter(big, "fsdp", scatter_dimension=0, tiled=True)
    big = big.astype(f32) + swap(big).astype(f32)
    gate_s, up_s, down_s = [
        ordered(
            jnp.concatenate([piece[kind] for piece in shard_grads]),
            jnp.concatenate([piece[kind] for piece in there]),
        ).astype(f32)
        for kind in range(3)
    ]
    at = q_width + 2 * kv_width
    return (
        block_out,
        input_grad,
        small_grads[-1],
        big[:, :q_width],
        big[:, q_width : q_width + kv_width],
        big[:, q_width + kv_width : at],
        big[:, at : at + q_width].T,
        small_grads[experts],
        small_grads[:experts].T,
        gate_s,
        up_s,
        down_s.transpose(0, 2, 1),
    )


def solution(mesh):
    rows = P(("fsdp", "ctx"), None)
    return jax.shard_map(
        per_device,
        mesh=mesh,
        in_specs=(
            rows, rows, P("fsdp"), P("fsdp"), rows, P("fsdp"), P("fsdp", "tp"), P("fsdp", "tp"),
            P("fsdp", "tp"), P("tp", "fsdp"), P("fsdp"), P("fsdp", None), P(None, "fsdp", "tp"),
            P(None, "fsdp", "tp"), P(None, "tp", "fsdp"),
        ),
        out_specs=(
            rows, rows, P("fsdp"), P("fsdp", "tp"), P("fsdp", "tp"), P("fsdp", "tp"), P("tp", "fsdp"),
            P("fsdp"), P("fsdp", None), P(None, "fsdp", "tp"), P(None, "fsdp", "tp"), P(None, "tp", "fsdp"),
        ),
        check_vma=False,
    )
```

```python
import functools
import jax
import jax.numpy as jnp
from jax import lax
from jax.experimental import pallas as pl
from jax.experimental.pallas import tpu as pltpu

HD = 64
DOC = 1024
BLK = 256
QB = 256
BAND = DOC + 2 * BLK
masked_score = -1e30
epsilon = 1e-06
VL = 60 * 1024 * 1024

def nt(a, b):
    return lax.dot_general(a, b, (((1,), (1,)), ((), ())), preferred_element_type=jnp.float32)

def tn(a, b):
    return lax.dot_general(a, b, (((0,), (0,)), ((), ())), preferred_element_type=jnp.float32)

def nn(a, b):
    return jnp.dot(a, b, preferred_element_type=jnp.float32)

def band_start(row, length):
    return pl.multiple_of(jnp.clip(row - DOC, 0, length - BAND), QB)

def flash_fwd_body(base_ref, q_ref, k_ref, v_ref, docq_ref, blkq_ref, dock_ref, blkk_ref, o_ref, *, share, length):
    step = pl.program_id(0)
    start = band_start(base_ref[0] + step * QB, length)
    keys = pl.ds(start, BAND)
    dock = dock_ref[:, keys]
    blkk = blkk_ref[:, keys]
    ok = (docq_ref[...] == dock) & (blkk <= blkq_ref[...])
    bias = jnp.where(ok, 0.0, masked_score)
    for head in range(q_ref.shape[0]):
        s = nt(q_ref[head], k_ref[head // share, keys, :]) + bias
        top = jnp.max(s, axis=1, keepdims=True)
        e = jnp.exp(s - top)
        p = e * (1.0 / jnp.sum(e, axis=1, keepdims=True))
        o_ref[head] = nn(p.astype(jnp.bfloat16), v_ref[head // share, keys, :]).astype(jnp.bfloat16)

def flash_fwd(base, q, k, v, docq, blkq, dock, blkk):
    heads, rows, _ = q.shape
    kv, length, _ = k.shape
    full = lambda shape: pl.BlockSpec(shape, lambda i, b: (0,) * len(shape))
    return pl.pallas_call(
        functools.partial(flash_fwd_body, share=heads // kv, length=length),
        grid_spec=pltpu.PrefetchScalarGridSpec(
            num_scalar_prefetch=1, grid=(rows // QB,),
            in_specs=[
                pl.BlockSpec((heads, QB, HD), lambda i, b: (0, i, 0)),
                full(k.shape), full(v.shape),
                pl.BlockSpec((QB, 1), lambda i, b: (i, 0)),
                pl.BlockSpec((QB, 1), lambda i, b: (i, 0)),
                full((1, length)), full((1, length)),
            ],
            out_specs=pl.BlockSpec((heads, QB, HD), lambda i, b: (0, i, 0)),
        ),
        out_shape=jax.ShapeDtypeStruct(q.shape, jnp.bfloat16),
        compiler_params=pltpu.CompilerParams(vmem_limit_bytes=VL),
        name="flash_fwd",
    )(base, q, k, v, docq, blkq, dock, blkk)

def flash_bwd_body(base_ref, q_ref, g_ref, k_ref, v_ref, docq_ref, blkq_ref, dock_ref, blkk_ref, dq_ref, dk_ref, dv_ref, *, share, length):
    step = pl.program_id(0)
    start = band_start(base_ref[0] + step * QB, length)
    keys = pl.ds(start, BAND)

    @pl.when(step == 0)
    def _():
        dk_ref[...] = jnp.zeros_like(dk_ref)
        dv_ref[...] = jnp.zeros_like(dv_ref)

    ok = (docq_ref[...] == dock_ref[keys, :]) & (blkk_ref[keys, :] <= blkq_ref[...])
    bias = jnp.where(ok, 0.0, masked_score)
    for head in range(q_ref.shape[0]):
        kvh = head // share
        q = q_ref[head]
        g = g_ref[head]
        k = k_ref[kvh, keys, :]
        s = nt(k, q) + bias
        e = jnp.exp(s - jnp.max(s, axis=0, keepdims=True))
        p = e * (1.0 / jnp.sum(e, axis=0, keepdims=True))
        dp = nt(v_ref[kvh, keys, :], g)
        delta = jnp.sum(dp * p, axis=0, keepdims=True)
        ds = (p * (dp - delta)).astype(jnp.bfloat16)
        dq_ref[head] = tn(ds, k)
        dk_ref[kvh, keys, :] += nn(ds, q)
        dv_ref[kvh, keys, :] += nn(p.astype(jnp.bfloat16), g)

def flash_bwd(base, q, g, k, v, docq, blkq, dock, blkk):
    heads, rows, _ = q.shape
    kv, length, _ = k.shape
    full = lambda shape: pl.BlockSpec(shape, lambda i, b: (0,) * len(shape))
    return pl.pallas_call(
        functools.partial(flash_bwd_body, share=heads // kv, length=length),
        grid_spec=pltpu.PrefetchScalarGridSpec(
            num_scalar_prefetch=1, grid=(rows // QB,),
            in_specs=[
                pl.BlockSpec((heads, QB, HD), lambda i, b: (0, i, 0)),
                pl.BlockSpec((heads, QB, HD), lambda i, b: (0, i, 0)),
                full(k.shape), full(v.shape),
                pl.BlockSpec((1, QB), lambda i, b: (0, i)),
                pl.BlockSpec((1, QB), lambda i, b: (0, i)),
                full((length, 1)), full((length, 1)),
            ],
            out_specs=[
                pl.BlockSpec((heads, QB, HD), lambda i, b: (0, i, 0)),
                full(k.shape), full(v.shape),
            ],
        ),
        out_shape=[
            jax.ShapeDtypeStruct(q.shape, jnp.float32),
            jax.ShapeDtypeStruct(k.shape, jnp.float32),
            jax.ShapeDtypeStruct(v.shape, jnp.float32),
        ],
        compiler_params=pltpu.CompilerParams(vmem_limit_bytes=VL),
        cost_estimate=busy(55),
        name="flash_bwd",
    )(base, q, g, k, v, docq, blkq, dock, blkk)

PAIR = 2
TM = 512

def moe_body(base_ref, x_ref, g_ref, xt_ref, gt_ref, gates_ref, prev_ref, w_ref, a_ref, gu_ref, grads_ref, dots_ref):
    rows, width = x_ref.shape
    shards, _, pair, part, ff = w_ref.shape
    step = pl.program_id(0)

    def weights(which):
        return jnp.concatenate(
            [jnp.concatenate([w_ref[z, which, e] for z in range(shards)], axis=0) for e in range(pair)], axis=1
        )

    gate_w = weights(0)
    up_w = weights(1)
    down_w = weights(2)
    experts = gates_ref.shape[1]
    lane = base_ref[0] + step * pair

    def tile(i, carry):
        here = pl.ds(pl.multiple_of(i * TM, TM), TM)
        x = x_ref[here, :]
        gate_val = nn(x, gate_w)
        up_val = nn(x, up_w)
        back = nn(g_ref[here, :], down_w)
        lanes = lax.broadcasted_iota(jnp.int32, (TM, experts), 1)
        gates = gates_ref[here, :]
        gate = jnp.concatenate(
            [
                jnp.broadcast_to(
                    jnp.sum(jnp.where(lanes == lane + e, gates, 0.0), axis=1, keepdims=True), (TM, ff)
                )
                for e in range(pair)
            ],
            axis=1,
        )
        sig = 1.0 / (1.0 + jnp.exp(-gate_val))
        silu = gate_val * sig
        inner = silu * up_val
        a_ref[here, :] = (inner * gate).astype(jnp.bfloat16)
        prod = inner * back
        dots = jnp.where(step == 0, prev_ref[here, :], dots_ref[here, :])
        for e in range(pair):
            total = jnp.sum(prod[:, e * ff : (e + 1) * ff], axis=1, keepdims=True)
            dots = jnp.where(lanes == lane + e, total, dots)
        dots_ref[here, :] = dots
        back = back * gate
        gu_ref[here, : pair * ff] = (back * up_val * sig * (1.0 + gate_val * (1.0 - sig))).astype(jnp.bfloat16)
        gu_ref[here, pair * ff :] = (back * silu).astype(jnp.bfloat16)
        return carry

    lax.fori_loop(0, rows // TM, tile, 0)
    for z in range(shards):
        part_rows = pl.ds(z * part, part)
        both = nn(xt_ref[part_rows, :], gu_ref[...])
        down = nn(gt_ref[part_rows, :], a_ref[...])
        for e in range(pair):
            grads_ref[z, 0, e] = both[:, e * ff : (e + 1) * ff].astype(jnp.bfloat16)
            grads_ref[z, 1, e] = both[:, (pair + e) * ff : (pair + e + 1) * ff].astype(jnp.bfloat16)
            grads_ref[z, 2, e] = down[:, e * ff : (e + 1) * ff].astype(jnp.bfloat16)

def moe_main(base, x, g, xt, gt, gates, dots, w):
    rows, width = x.shape
    shards, three, count, part, ff = w.shape
    one = lambda shape: pl.BlockSpec(shape, lambda i: (0,) * len(shape), pipeline_mode=pl.Buffered(1))
    return pl.pallas_call(
        moe_body,
        grid=(count // PAIR,),
        in_specs=[
            SMEMS, one(x.shape), one(g.shape), one(xt.shape), one(gt.shape), one(gates.shape), one(dots.shape),
            pl.BlockSpec((shards, 3, PAIR, part, ff), lambda i: (0, 0, i, 0, 0)),
        ],
        out_specs=[
            pl.BlockSpec((rows, PAIR * ff), lambda i: (0, i)),
            pl.BlockSpec((rows, 2 * PAIR * ff), lambda i: (0, i)),
            pl.BlockSpec((shards, 3, PAIR, part, ff), lambda i: (0, 0, i, 0, 0)),
            one(dots.shape),
        ],
        out_shape=[
            jax.ShapeDtypeStruct((rows, count * ff), jnp.bfloat16),
            jax.ShapeDtypeStruct((rows, 2 * count * ff), jnp.bfloat16),
            jax.ShapeDtypeStruct(w.shape, jnp.bfloat16),
            jax.ShapeDtypeStruct(dots.shape, jnp.float32),
        ],
        compiler_params=pltpu.CompilerParams(vmem_limit_bytes=VL),
        cost_estimate=pl.CostEstimate(flops=2 * rows * width * count * ff * 6, bytes_accessed=8 * rows * width + 12 * count * ff * width, transcendentals=0),
        name="moe_main",
        input_output_aliases={6: 3},
    )(base, x, g, xt, gt, gates, dots, w)

def back_body(*refs, count, first, kinds):
    gu_refs, w_refs, o_ref = refs[:count], refs[count : 2 * count], refs[2 * count]
    shards, _, experts, part, ff = w_refs[0].shape
    for z in range(shards):
        total = None
        for gu_ref, w_ref in zip(gu_refs, w_refs):
            w = jnp.concatenate(
                [
                    w_ref[z, kind, p * PAIR + e]
                    for p in range(experts // PAIR)
                    for kind in range(kinds)
                    for e in range(PAIR)
                ],
                axis=1,
            )
            piece = nt(gu_ref[...], w)
            total = piece if total is None else total + piece
        o_ref[:, z * part : (z + 1) * part] = total.astype(o_ref.dtype)


def moe_back(gus, ws, first, kinds):
    shards, three, experts, part, ff = ws[0].shape
    rows = gus[0].shape[0]
    width = shards * part
    count = len(gus)
    return pl.pallas_call(
        functools.partial(back_body, count=count, first=first, kinds=kinds),
        grid=(rows // TM,),
        in_specs=[pl.BlockSpec((TM, kinds * experts * ff), lambda i: (i, 0)) for _ in gus]
        + [
            pl.BlockSpec(
                (shards, kinds, experts, part, ff),
                lambda i: (0, first // kinds, 0, 0, 0),
                pipeline_mode=pl.Buffered(1),
            )
            for _ in ws
        ],
        out_specs=pl.BlockSpec((TM, width), lambda i: (i, 0)),
        out_shape=jax.ShapeDtypeStruct((rows, width), jnp.bfloat16),
        compiler_params=pltpu.CompilerParams(vmem_limit_bytes=VL),
        cost_estimate=pl.CostEstimate(
            flops=2 * rows * width * count * experts * ff * kinds,
            bytes_accessed=2 * rows * kinds * count * experts * ff,
            transcendentals=0,
        ),
        name="moe_back" if kinds == 2 else "moe_out",
    )(*gus, *ws)


MESH = pl.DeviceIdType.MESH


class Place:
    def __init__(self):
        self.ctx = lax.axis_index("ctx")
        self.tp = lax.axis_index("tp")
        self.core = lax.rem(self.tp, 2)
        self.high = self.tp // 2
        self.pair_tp = self.high * 2 + 1 - self.core
        self.far_tp = (1 - self.high) * 2 + self.core
        self.cross_tp = (1 - self.high) * 2 + 1 - self.core
        self.pair = {"tp": self.pair_tp}
        self.far = {"tp": self.far_tp}
        self.side = {"ctx": 1 - self.ctx}

    def meet(self, who):
        barrier = pltpu.get_barrier_semaphore()
        for device in who:
            pl.semaphore_signal(barrier, inc=1, device_id=device, device_id_type=MESH)
        pl.semaphore_wait(barrier, len(who))


def push(src, dst, sems, slot, device):
    return pltpu.make_async_remote_copy(
        src_ref=src, dst_ref=dst, send_sem=sems.at[0, slot], recv_sem=sems.at[1, slot],
        device_id=device, device_id_type=MESH,
    )


def gather_four(place, all_ref, sems, at):
    here, far = all_ref.at[place.tp], all_ref.at[place.far_tp]
    to_far = push(here, here, sems, at, place.far)
    to_pair = push(here, here, sems, at + 1, place.pair)
    to_far.start()
    to_pair.start()
    to_far.wait_recv()
    on = push(far, far, sems, at + 2, place.pair)
    on.start()
    to_pair.wait_recv()
    on.wait_recv()
    to_far.wait_send()
    to_pair.wait_send()
    on.wait_send()


def gather_eight(place, all_ref, sems, at):
    rows = all_ref.shape[1]
    top, low = pl.ds(0, rows // 2), pl.ds(rows // 2, rows // 2)
    part = lambda ctx, tp: all_ref.at[ctx * 4 + tp]
    other = 1 - place.ctx
    here = part(place.ctx, place.tp)
    side = part(other, place.tp)
    far = part(place.ctx, place.far_tp)
    cross = part(other, place.far_tp)
    side_top, far_low = side.at[top], far.at[low]
    cross_top, cross_low = cross.at[top], cross.at[low]
    to_side = push(here, here, sems, at, place.side)
    to_far = push(here, here, sems, at + 1, place.far)
    to_pair = push(here, here, sems, at + 2, place.pair)
    for copy in (to_side, to_far, to_pair):
        copy.start()
    to_side.wait_recv()
    turn_far = push(side_top, side_top, sems, at + 3, place.far)
    pair_side = push(side, side, sems, at + 5, place.pair)
    turn_far.start()
    pair_side.start()
    to_far.wait_recv()
    turn_side = push(far_low, far_low, sems, at + 4, place.side)
    pair_far = push(far, far, sems, at + 6, place.pair)
    turn_side.start()
    pair_far.start()
    turn_far.wait_recv()
    pair_top = push(cross_top, cross_top, sems, at + 7, place.pair)
    pair_top.start()
    turn_side.wait_recv()
    pair_low = push(cross_low, cross_low, sems, at + 8, place.pair)
    pair_low.start()
    for copy in (to_pair, pair_side, pair_far, pair_top, pair_low):
        copy.wait_recv()
    for copy in (to_side, to_far, to_pair, turn_far, turn_side, pair_side, pair_far, pair_top, pair_low):
        copy.wait_send()


def reduce_four(place, produce, send_ref, pair_in, far_in, own_ref, sems, at):
    def fold(j):
        slot = j // 2

        @pl.when(lax.rem(j, 2) == place.core)
        def _():
            push(send_ref.at[j], pair_in.at[slot], sems, at + slot, place.pair).wait_recv()
            total = send_ref[j].astype(jnp.float32) + pair_in[slot].astype(jnp.float32)

            @pl.when(slot == place.high)
            def _():
                own_ref[...] = total

            @pl.when(slot != place.high)
            def _():
                send_ref[j] = total.astype(jnp.bfloat16)
                push(send_ref.at[j], far_in, sems, at + 2, place.far).start()

    def step(j, carry):
        produce(j)

        @pl.when(lax.rem(j, 2) != place.core)
        def _():
            slot = j // 2
            push(send_ref.at[j], pair_in.at[slot], sems, at + slot, place.pair).start()

        @pl.when(j > 0)
        def _():
            fold(j - 1)

        return carry

    lax.fori_loop(0, 4, step, 0)
    fold(3)
    last = push(send_ref.at[place.far_tp], far_in, sems, at + 2, place.far)
    last.wait_recv()
    own_ref[...] += far_in[...].astype(jnp.float32)
    last.wait_send()
    for slot in range(2):
        push(send_ref.at[place.pair_tp], pair_in.at[slot], sems, at + slot, place.pair).wait_send()


SMEMS = pl.BlockSpec(memory_space=pltpu.SMEM)
WHOLE = pl.BlockSpec(memory_space=pltpu.VMEM)


def normalize(x):
    r = lax.rsqrt(jnp.mean(x * x, axis=1, keepdims=True) + epsilon)
    return r, x * r


def mid_body(tok_ref, q_ref, k_ref, v_ref, docq_ref, blkq_ref, dock_ref, blkk_ref, w_ref, gain_ref,
             mix_ref, hid_ref, all_ref, whole_ref, send, pair_in, far_in, own, sems, w_sems, *, share, length):
    place = Place()
    shards, part, _ = whole_ref.shape
    z = lax.axis_index("fsdp")
    others = [{"fsdp": lax.rem(z + d, shards)} for d in range(1, shards)]
    place.meet((place.pair, place.far, place.side, *others))
    spread = [push(w_ref, whole_ref.at[z], w_sems, d, device) for d, device in enumerate(others)]
    for copy in spread:
        copy.start()
    whole_ref[z] = w_ref[...]
    heads, rows, _ = q_ref.shape
    block = rows // 4
    band = min(DOC + block + BLK, length)

    def produce(j):
        at = pl.multiple_of(j * block, block)
        here = pl.ds(at, block)
        start = pl.multiple_of(jnp.clip(place.ctx * rows + at - DOC, 0, length - band), 128)
        keys = pl.ds(start, band)
        ok = (docq_ref[here, :] == dock_ref[:, keys]) & (blkk_ref[:, keys] <= blkq_ref[here, :])
        bias = jnp.where(ok, 0.0, masked_score)
        outs = []
        for head in range(heads):
            s = nt(q_ref[head, here, :], k_ref[head // share, keys, :]) + bias
            e = jnp.exp(s - jnp.max(s, axis=1, keepdims=True))
            p = e * (1.0 / jnp.sum(e, axis=1, keepdims=True))
            outs.append(nn(p.astype(jnp.bfloat16), v_ref[head // share, keys, :]).astype(jnp.bfloat16))
        mix = jnp.concatenate(outs, axis=1)
        mix_ref[here, :] = mix

        @pl.when(j == 0)
        def _():
            for copy in spread:
                copy.wait_recv()

        for n in range(shards):
            send[j, :, n * part : (n + 1) * part] = nt(mix, whole_ref[n]).astype(jnp.bfloat16)

    reduce_four(place, produce, send, pair_in, far_in, own, sems, 0)
    hidden = tok_ref[...].astype(jnp.float32) + own[...]
    hid_ref[...] = hidden
    all_ref[place.ctx * 4 + place.tp] = (normalize(hidden)[1] * gain_ref[...]).astype(jnp.bfloat16)
    gather_eight(place, all_ref, sems, 3)
    for copy in spread:
        copy.wait_send()


def mid(tok, q, k, v, docq, blkq, dock, blkk, out_w, gain):
    heads, rows, _ = q.shape
    kv, length, _ = k.shape
    own, width = tok.shape
    part = out_w.shape[0]
    shards = width // part
    return pl.pallas_call(
        functools.partial(mid_body, share=heads // kv, length=length),
        in_specs=[WHOLE] * 10,
        out_specs=[WHOLE] * 4,
        out_shape=[
            jax.ShapeDtypeStruct((rows, heads * HD), jnp.bfloat16),
            jax.ShapeDtypeStruct((own, width), jnp.float32),
            jax.ShapeDtypeStruct((8, own, width), jnp.bfloat16),
            jax.ShapeDtypeStruct((shards, *out_w.shape), jnp.bfloat16),
        ],
        scratch_shapes=[
            pltpu.VMEM((4, own, width), jnp.bfloat16),
            pltpu.VMEM((2, own, width), jnp.bfloat16),
            pltpu.VMEM((own, width), jnp.bfloat16),
            pltpu.VMEM((own, width), jnp.float32),
            pltpu.SemaphoreType.DMA((2, 12)),
            pltpu.SemaphoreType.DMA((2, shards - 1)),
        ],
        compiler_params=pltpu.CompilerParams(vmem_limit_bytes=VL, collective_id=0, has_side_effects=True),
        cost_estimate=busy(100),
        name="mid",
    )(tok, q, k, v, docq, blkq, dock, blkk, out_w, gain)


def tail_body(tok_ref, hg_ref, lin_ref, w_ref, gain_ref, small_ref, all_ref, sum_ref,
              send, pair_in, far_in, own, mine, theirs, split, split_in, sems, small_sems, *, shards):
    place = Place()
    z = lax.axis_index("fsdp")
    others = [{"fsdp": lax.rem(z + d, shards)} for d in range(1, shards)]
    place.meet((place.pair, place.far, place.side, *others))
    block = lin_ref.shape[0] // 4
    part = sum_ref.shape[1]

    def produce(j):
        here = pl.ds(pl.multiple_of(j * block, block), block)
        send[j] = nt(lin_ref[here, :], w_ref[...]).astype(jnp.bfloat16)

    reduce_four(place, produce, send, pair_in, far_in, own, sems, 0)
    one_grad = own[...]
    r, xhat = normalize(tok_ref[...].astype(jnp.float32))
    n = one_grad * gain_ref[...]
    grad = hg_ref[...] + r * (n - xhat * jnp.mean(n * xhat, axis=1, keepdims=True))
    all_ref[place.tp] = grad.astype(jnp.bfloat16)
    row = lax.broadcasted_iota(jnp.int32, small_ref.shape, 0)
    mine[0] = jnp.where(
        row == small_ref.shape[0] - 1, jnp.sum(one_grad * xhat, axis=0, keepdims=True), small_ref[...]
    )
    hops = [
        push(mine.at[i], theirs.at[i], small_sems, i, device)
        for i, device in enumerate((place.pair, place.side, place.far))
    ]
    hops[0].start()
    here, far = all_ref.at[place.tp], all_ref.at[place.far_tp]
    to_far = push(here, here, sems, 3, place.far)
    to_pair = push(here, here, sems, 4, place.pair)
    to_far.start()
    to_pair.start()
    for i in range(2):
        hops[i].wait_recv()
        mine[i + 1] = mine[i] + theirs[i]
        hops[i + 1].start()
    to_far.wait_recv()
    on = push(far, far, sems, 5, place.pair)
    on.start()
    hops[2].wait_recv()
    total = mine[2] + theirs[2]
    for j in range(shards):
        split[j] = total[:, j * part : (j + 1) * part]
    spread = [
        push(split.at[lax.rem(z + d, shards)], split_in.at[d - 1], small_sems, 2 + d, others[d - 1])
        for d in range(1, shards)
    ]
    for copy in spread:
        copy.start()
    to_pair.wait_recv()
    on.wait_recv()
    result = split[z]
    for d in range(1, shards):
        spread[d - 1].wait_recv()
        result = result + split_in[d - 1]
    sum_ref[...] = result
    for copy in (to_far, to_pair, on, *hops, *spread):
        copy.wait_send()


def tail(tok, hidden_grad, lin_grad, qkv_w, gain, small, shards):
    own, width = tok.shape
    count = small.shape[0]
    part = width // shards
    return pl.pallas_call(
        functools.partial(tail_body, shards=shards),
        in_specs=[WHOLE] * 6,
        out_specs=[WHOLE] * 2,
        out_shape=[
            jax.ShapeDtypeStruct((4, own, width), jnp.bfloat16),
            jax.ShapeDtypeStruct((count, part), jnp.float32),
        ],
        scratch_shapes=[
            pltpu.VMEM((4, own, width), jnp.bfloat16),
            pltpu.VMEM((2, own, width), jnp.bfloat16),
            pltpu.VMEM((own, width), jnp.bfloat16),
            pltpu.VMEM((own, width), jnp.float32),
            pltpu.VMEM((3, count, width), jnp.float32),
            pltpu.VMEM((3, count, width), jnp.float32),
            pltpu.VMEM((shards, count, part), jnp.float32),
            pltpu.VMEM((shards - 1, count, part), jnp.float32),
            pltpu.SemaphoreType.DMA((2, 6)),
            pltpu.SemaphoreType.DMA((2, 2 + shards)),
        ],
        compiler_params=pltpu.CompilerParams(vmem_limit_bytes=VL, collective_id=1, has_side_effects=True),
        cost_estimate=busy(50),
        name="tail",
    )(tok, hidden_grad, lin_grad, qkv_w, gain, small)


def turn_body(*refs, count, kinds, first, finish):
    gu_refs, w_refs = refs[:count], refs[count : 2 * count]
    lg_ref, router_ref, hid_ref, extra_ref, gain_ref = refs[2 * count : 2 * count + 5]
    outs = refs[2 * count + 5 : 2 * count + 8]
    gu_buf, gu_sem, give, keep, pair_in, cut, own, sems = refs[2 * count + 8 :]
    all_ref = outs[0]
    place = Place()
    place.meet((place.pair, place.far, place.side))
    block = hid_ref.shape[0]
    shards, _, experts, part, ff = w_refs[0].shape
    half = block // 2
    top, low = pl.ds(0, half), pl.ds(half, half)
    bf = jnp.bfloat16
    f = jnp.float32
    order = [(1, 1), (1, 0), (0, 1), (0, 0)]

    def tile_of(step):
        dx, dy = order[step // 2]
        ctx = place.ctx + dx * (1 - 2 * place.ctx)
        high = place.high + dy * (1 - 2 * place.high)
        core = 1 - place.core if step % 2 == 0 else place.core
        return ctx * 4 + high * 2 + core

    def fetch(step):
        at = pl.ds(pl.multiple_of(tile_of(step) * block, block), block)
        return [
            pltpu.make_async_copy(gu.at[at, :], gu_buf.at[step % 2, n], gu_sem.at[step % 2, n])
            for n, gu in enumerate(gu_refs)
        ]

    for copy in fetch(0):
        copy.start()

    def compute(step, dst):
        for copy in fetch(step):
            copy.wait()
        if step + 1 < 8:
            for copy in fetch(step + 1):
                copy.start()
        at = pl.ds(pl.multiple_of(tile_of(step) * block, block), block)
        for z in range(shards):
            cols = slice(z * part, (z + 1) * part)
            total = None
            if lg_ref is not None:
                total = nt(lg_ref[at, :], router_ref[cols, :])
            for n, w_ref in enumerate(w_refs):
                w = jnp.concatenate(
                    [
                        w_ref[z, kind, p * PAIR + e]
                        for p in range(experts // PAIR)
                        for kind in range(kinds)
                        for e in range(PAIR)
                    ],
                    axis=1,
                )
                piece = nt(gu_buf[step % 2, n], w)
                total = piece if total is None else total + piece
            dst[:, cols] = total.astype(bf)

    copies = []

    def send(src, dst, slot, device):
        copy = push(src, dst, sems, slot, device)
        copy.start()
        copies.append(copy)
        return copy

    for k in range(4):
        compute(2 * k, give.at[k])
        got = send(give.at[k], pair_in.at[k], k, place.pair)
        compute(2 * k + 1, keep.at[k])
        got.wait_recv()
        total = keep[k].astype(f) + pair_in[k].astype(f)
        if k == 0:
            keep[k] = total.astype(bf)
            a_cross = send(keep.at[k, top], cut.at[0], 4, place.side)
            b_cross = send(keep.at[k, low], cut.at[1], 5, place.far)
        elif k == 1:
            b_cross.wait_recv()
            keep[k, top] = total[:half].astype(bf)
            keep[k, low] = (total[half:] + cut[1].astype(f)).astype(bf)
            a_first = send(keep.at[k, top], cut.at[2], 6, place.side)
            b_last = send(keep.at[k, low], cut.at[5], 9, place.side)
        elif k == 2:
            a_cross.wait_recv()
            keep[k, low] = total[half:].astype(bf)
            keep[k, top] = (total[:half] + cut[0].astype(f)).astype(bf)
            b_first = send(keep.at[k, low], cut.at[4], 8, place.far)
            a_last = send(keep.at[k, top], cut.at[3], 7, place.far)
        else:
            for copy in (a_first, a_last, b_first, b_last):
                copy.wait_recv()
            own[top, :] = total[:half] + cut[2].astype(f) + cut[3].astype(f)
            own[low, :] = total[half:] + cut[4].astype(f) + cut[5].astype(f)
    finish(place, own, hid_ref, extra_ref, gain_ref, outs)
    gather_four(place, all_ref, sems, 10)
    for copy in copies:
        copy.wait_send()


def turn_back(place, own, hid_ref, grad_ref, gain_ref, outs):
    all_ref, hg_ref, gg_ref = outs
    two_grad = own[...]
    r, hhat = normalize(hid_ref[...])
    gg_ref[...] = jnp.sum(two_grad * hhat, axis=0, keepdims=True)
    m = two_grad * gain_ref[...]
    grad = grad_ref[...].astype(jnp.float32) + r * (m - hhat * jnp.mean(m * hhat, axis=1, keepdims=True))
    hg_ref[...] = grad
    all_ref[place.tp] = grad.astype(jnp.bfloat16)


def turn(gus, ws, logit_grad, router_w, hidden, grad_own, gain):
    shards, _, experts, part, ff = ws[0].shape
    own, width = hidden.shape
    count = len(gus)
    kinds = 2
    cols = gus[0].shape[1]
    anys = pl.BlockSpec(memory_space=pl.ANY)
    return pl.pallas_call(
        functools.partial(turn_body, count=count, kinds=kinds, first=0, finish=turn_back),
        grid=(1,),
        in_specs=[anys] * count
        + [
            pl.BlockSpec((shards, kinds, experts, part, ff), lambda i: (0, 0, 0, 0, 0), pipeline_mode=pl.Buffered(1))
            for _ in ws
        ]
        + [WHOLE] * 5,
        out_specs=[WHOLE] * 3,
        out_shape=[
            jax.ShapeDtypeStruct((4, own, width), jnp.bfloat16),
            jax.ShapeDtypeStruct((own, width), jnp.float32),
            jax.ShapeDtypeStruct((1, width), jnp.float32),
        ],
        scratch_shapes=[
            pltpu.VMEM((2, count, own, cols), jnp.bfloat16),
            pltpu.SemaphoreType.DMA((2, count)),
            pltpu.VMEM((4, own, width), jnp.bfloat16),
            pltpu.VMEM((4, own, width), jnp.bfloat16),
            pltpu.VMEM((4, own, width), jnp.bfloat16),
            pltpu.VMEM((6, own // 2, width), jnp.bfloat16),
            pltpu.VMEM((own, width), jnp.float32),
            pltpu.SemaphoreType.DMA((2, 13)),
        ],
        compiler_params=pltpu.CompilerParams(vmem_limit_bytes=VL, collective_id=2, has_side_effects=True),
        cost_estimate=busy(75),
        name="turn",
    )(*gus, *ws, logit_grad, router_w, hidden, grad_own, gain)


from jax.sharding import PartitionSpec as P

rope_base = 10000.0
CHUNKS = 4
bf16 = jnp.bfloat16
f32 = jnp.float32


def rope_tables(positions):
    half = HD // 2
    frequency = rope_base ** (-2.0 * jnp.arange(half, dtype=f32) / HD)
    angles = positions.astype(f32)[:, None] * frequency[None, :]
    return jnp.cos(angles)[:, None, :], jnp.sin(angles)[:, None, :]


def busy(us):
    return pl.CostEstimate(flops=int(us * 1e9), bytes_accessed=1 << 20, transcendentals=0)


def swap(x):
    return lax.ppermute(x, "ctx", [(0, 1), (1, 0)])


def after(x, *done):
    return lax.optimization_barrier((x, *done))


def rotate(values, cosine, sine):
    shaped = values.reshape(values.shape[0], -1, HD)
    a, b = shaped[:, :, : HD // 2], shaped[:, :, HD // 2 :]
    return jnp.concatenate([a * cosine - b * sine, b * cosine + a * sine], axis=2)


def per_device(
    tokens, out_grad, doc_ids, block_ids, expert_ids, norm1_gain, w_query, w_key, w_value, w_out,
    norm2_gain, w_router, w_gate, w_up, w_down,
):
    shards = lax.axis_size("fsdp")
    ctx_size = lax.axis_size("ctx")
    tp_size = lax.axis_size("tp")
    ctx = lax.axis_index("ctx")
    tp = lax.axis_index("tp")
    rows, width = tokens.shape
    part = width // shards
    own = rows // tp_size
    length = doc_ids.shape[0]
    q_width, kv_width = w_query.shape[1], w_key.shape[1]
    heads, kv_heads = q_width // HD, kv_width // HD
    experts = w_gate.shape[0]
    mine = experts // ctx_size
    each = mine // CHUNKS
    ff = w_gate.shape[2]

    columns = q_width + 2 * kv_width
    extra = jnp.concatenate([norm1_gain, norm2_gain, w_router.reshape(-1)])
    extra_rows = -(-extra.shape[0] // (8 * columns)) * 8
    extra = jnp.pad(extra, (0, extra_rows * columns - extra.shape[0])).reshape(extra_rows, columns)
    front = jnp.concatenate([jnp.concatenate([w_query, w_key, w_value], axis=1), extra], axis=0)
    front = lax.all_gather(front, "fsdp", axis=0)
    ordered = lambda here, there, axis=0: jnp.concatenate(
        [jnp.where(ctx == 0, here, there), jnp.where(ctx == 0, there, here)], axis=axis
    )
    shard_list = []
    for chunk in range(CHUNKS):
        first = ctx * mine + chunk * each
        pick = lambda w: lax.dynamic_slice_in_dim(w, first, each, 0)
        shard_list.append(jnp.stack([pick(w_gate), pick(w_up), pick(w_down).transpose(0, 2, 1)]))
    front, *shard_list = after(front, *shard_list)
    qkv_w = front[:, :part].reshape(width, columns)
    extra = front[:, part:].reshape(shards, extra_rows * columns)
    gain_one = extra[:, :part].reshape(width).astype(f32)
    gain_two = extra[:, part : 2 * part].reshape(width).astype(f32)
    router_w = extra[:, 2 * part : (2 + experts) * part].reshape(width, experts)

    stacked = [lax.all_gather(shard, "fsdp", axis=0) for shard in shard_list]
    ids_all = ordered(expert_ids, swap(expert_ids))

    inputs = tokens.astype(f32)
    rms_one = lax.rsqrt(jnp.mean(inputs * inputs, axis=1, keepdims=True) + epsilon)
    normed = (inputs * rms_one * gain_one).astype(bf16)
    start = ctx * rows
    cosine, sine = rope_tables(start + jnp.arange(rows, dtype=jnp.int32))
    kv_lin = jnp.dot(normed, qkv_w[:, q_width:], preferred_element_type=f32)
    keys_values = jnp.concatenate(
        [rotate(kv_lin[:, :kv_width], cosine, sine).reshape(rows, kv_width), kv_lin[:, kv_width:]], axis=1
    ).astype(bf16)
    queries = rotate(jnp.dot(normed, qkv_w[:, :q_width], preferred_element_type=f32), cosine, sine)
    queries = queries.astype(bf16).transpose(1, 0, 2) * bf16(HD**-0.5)
    near = min(DOC, rows)
    apart = lambda x: jnp.where(
        ctx == 0, jnp.pad(x, ((0, rows - near), (0, 0))), jnp.pad(x, ((rows - near, 0), (0, 0)))
    )
    window = lax.dynamic_slice_in_dim(keys_values, jnp.where(ctx == 0, rows - near, 0), near)
    keys_values = ordered(keys_values, apart(swap(window)))
    grad_here, keys_values = after(out_grad, keys_values)
    grad_all = ordered(grad_here, swap(grad_here))
    keys_values = keys_values.reshape(length, 2 * kv_heads, HD).transpose(1, 0, 2)
    keys, values = keys_values[:kv_heads], keys_values[kv_heads:]
    query_doc = lax.dynamic_slice_in_dim(doc_ids, start, rows)
    query_block = lax.dynamic_slice_in_dim(block_ids, start, rows)
    base = start.astype(jnp.int32).reshape(1)
    tokens_own = lax.dynamic_slice_in_dim(tokens, tp * own, own)
    grad_own = lax.dynamic_slice_in_dim(out_grad, tp * own, own)
    attn_mix, hidden, normed_two, out_w = mid(
        tokens_own, queries, keys, values, query_doc[:, None], query_block[:, None], doc_ids[None],
        block_ids[None], w_out.T, gain_two[None],
    )
    out_w = out_w.reshape(width, q_width)
    normed_two = normed_two.reshape(ctx_size * rows, width)

    logits = jnp.dot(normed_two, router_w, preferred_element_type=f32)
    chosen = jnp.any(ids_all[:, :, None] == jnp.arange(experts, dtype=jnp.int32)[None, None, :], axis=1)
    masked = jnp.where(chosen, logits, masked_score)
    powers = jnp.exp(masked - jnp.max(masked, axis=1, keepdims=True))
    gates = powers / jnp.sum(powers, axis=1, keepdims=True)

    normed_t, grad_t = normed_two.T, grad_all.T
    inner_all, outer_all, shard_grads = [], [], []
    dots = jnp.zeros_like(gates)
    for chunk in range(CHUNKS):
        inner, outer, grads, dots = moe_main(
            (ctx * mine + chunk * each).astype(jnp.int32).reshape(1),
            normed_two, grad_all, normed_t, grad_t, gates, dots, stacked[chunk],
        )
        inner_all.append(inner)
        outer_all.append(outer)
        shard_grads.append(lax.psum_scatter(grads, "fsdp", scatter_dimension=0, tiled=False))
    combined = moe_back(inner_all, stacked, 2, 1)

    weighted = gates * dots
    dots_sum = jnp.sum(weighted, axis=1, keepdims=True)
    logit_grad = (weighted - gates * dots_sum).astype(bf16)
    router_grad = lax.dot_general(
        logit_grad, normed_two, (((0,), (0,)), ((), ())), preferred_element_type=f32
    )
    grad_own, shard_grads[0] = after(grad_own, shard_grads[0])
    branch_grad, hidden_grad, gain_two_grad = turn(
        outer_all, stacked, logit_grad, router_w, hidden, grad_own, gain_two[None]
    )
    branch_grad, *first = after(branch_grad, *shard_grads[:3])
    there = [swap(piece) for piece in first]
    branch_grad = branch_grad.reshape(rows, width)

    out_w_grad = lax.dot_general(
        branch_grad, attn_mix, (((0,), (0,)), ((), ())), preferred_element_type=f32
    )
    mix_grad = jnp.dot(branch_grad, out_w, preferred_element_type=f32).astype(bf16)
    query_grad, key_grad, value_grad = flash_bwd(
        base, queries, mix_grad.reshape(rows, heads, HD).transpose(1, 0, 2), keys, values,
        query_doc[None], query_block[None], doc_ids[:, None], block_ids[:, None],
    )
    query_grad, key_grad, value_grad, *there = after(query_grad, key_grad, value_grad, *there)
    kv_grad = jnp.concatenate([key_grad, value_grad], axis=0).transpose(1, 0, 2).reshape(length, 2 * kv_width)
    kv_grad = kv_grad.astype(bf16)
    kept = lax.dynamic_slice_in_dim(kv_grad, start, rows)
    given = lax.dynamic_slice_in_dim(kv_grad, jnp.where(ctx == 0, rows, rows - near), near)
    got = swap(given)
    got = jnp.where(
        ctx == 0, jnp.pad(got, ((rows - near, 0), (0, 0))), jnp.pad(got, ((0, rows - near), (0, 0)))
    )
    kv_grad = kept.astype(f32) + got.astype(f32)
    kv_grad, last = after(kv_grad, shard_grads[3])
    there.append(swap(last))
    query_grad = (query_grad * HD**-0.5).transpose(1, 0, 2).reshape(rows, q_width)
    turned_grad = rotate(
        jnp.concatenate([query_grad, kv_grad[:, :kv_width]], axis=1), cosine, -sine
    ).reshape(rows, q_width + kv_width)
    lin_grad = jnp.concatenate([turned_grad, kv_grad[:, kv_width:]], axis=1).astype(bf16)
    qkv_grad = lax.dot_general(normed, lin_grad, (((0,), (0,)), ((), ())), preferred_element_type=f32)

    small_grads = jnp.concatenate(
        [router_grad, gain_two_grad, jnp.zeros((8 - (experts + 1) % 8, width), f32)], axis=0
    )
    input_grad, small_grads = tail(
        tokens_own, hidden_grad, lin_grad, qkv_w, gain_one[None], small_grads, shards
    )
    input_grad = input_grad.reshape(rows, width)
    hidden, small_grads, there[-1] = after(hidden, small_grads, there[-1])
    mixed = lax.psum_scatter(combined, ("ctx", "tp"), scatter_dimension=0, tiled=True)
    block_out = lax.all_gather((hidden + mixed.astype(f32)).astype(bf16), "tp", axis=0, tiled=True)

    big = jnp.concatenate([qkv_grad, out_w_grad], axis=1).astype(bf16)
    big = lax.psum_scatter(big, "fsdp", scatter_dimension=0, tiled=True)
    big = big.astype(f32) + swap(big).astype(f32)
    gate_s, up_s, down_s = [
        ordered(
            jnp.concatenate([piece[kind] for piece in shard_grads]),
            jnp.concatenate([piece[kind] for piece in there]),
        ).astype(f32)
        for kind in range(3)
    ]
    at = q_width + 2 * kv_width
    return (
        block_out,
        input_grad,
        small_grads[-1],
        big[:, :q_width],
        big[:, q_width : q_width + kv_width],
        big[:, q_width + kv_width : at],
        big[:, at : at + q_width].T,
        small_grads[experts],
        small_grads[:experts].T,
        gate_s,
        up_s,
        down_s.transpose(0, 2, 1),
    )


def solution(mesh):
    rows = P(("fsdp", "ctx"), None)
    return jax.shard_map(
        per_device,
        mesh=mesh,
        in_specs=(
            rows, rows, P("fsdp"), P("fsdp"), rows, P("fsdp"), P("fsdp", "tp"), P("fsdp", "tp"),
            P("fsdp", "tp"), P("tp", "fsdp"), P("fsdp"), P("fsdp", None), P(None, "fsdp", "tp"),
            P(None, "fsdp", "tp"), P(None, "tp", "fsdp"),
        ),
        out_specs=(
            rows, rows, P("fsdp"), P("fsdp", "tp"), P("fsdp", "tp"), P("fsdp", "tp"), P("tp", "fsdp"),
            P("fsdp"), P("fsdp", None), P(None, "fsdp", "tp"), P(None, "fsdp", "tp"), P(None, "tp", "fsdp"),
        ),
        check_vma=False,
    )
```

```python
import functools
import jax
import jax.numpy as jnp
from jax import lax
from jax.experimental import pallas as pl
from jax.experimental.pallas import tpu as pltpu

HD = 64
DOC = 1024
BLK = 256
QB = 256
BAND = DOC + 2 * BLK
masked_score = -1e30
epsilon = 1e-06
VL = 60 * 1024 * 1024

def nt(a, b):
    return lax.dot_general(a, b, (((1,), (1,)), ((), ())), preferred_element_type=jnp.float32)

def tn(a, b):
    return lax.dot_general(a, b, (((0,), (0,)), ((), ())), preferred_element_type=jnp.float32)

def nn(a, b):
    return jnp.dot(a, b, preferred_element_type=jnp.float32)

def band_start(row, length):
    return pl.multiple_of(jnp.clip(row - DOC, 0, length - BAND), QB)

def flash_fwd_body(base_ref, q_ref, k_ref, v_ref, docq_ref, blkq_ref, dock_ref, blkk_ref, o_ref, *, share, length):
    step = pl.program_id(0)
    start = band_start(base_ref[0] + step * QB, length)
    keys = pl.ds(start, BAND)
    dock = dock_ref[:, keys]
    blkk = blkk_ref[:, keys]
    ok = (docq_ref[...] == dock) & (blkk <= blkq_ref[...])
    bias = jnp.where(ok, 0.0, masked_score)
    for head in range(q_ref.shape[0]):
        s = nt(q_ref[head], k_ref[head // share, keys, :]) + bias
        top = jnp.max(s, axis=1, keepdims=True)
        e = jnp.exp(s - top)
        p = e * (1.0 / jnp.sum(e, axis=1, keepdims=True))
        o_ref[head] = nn(p.astype(jnp.bfloat16), v_ref[head // share, keys, :]).astype(jnp.bfloat16)

def flash_fwd(base, q, k, v, docq, blkq, dock, blkk):
    heads, rows, _ = q.shape
    kv, length, _ = k.shape
    full = lambda shape: pl.BlockSpec(shape, lambda i, b: (0,) * len(shape))
    return pl.pallas_call(
        functools.partial(flash_fwd_body, share=heads // kv, length=length),
        grid_spec=pltpu.PrefetchScalarGridSpec(
            num_scalar_prefetch=1, grid=(rows // QB,),
            in_specs=[
                pl.BlockSpec((heads, QB, HD), lambda i, b: (0, i, 0)),
                full(k.shape), full(v.shape),
                pl.BlockSpec((QB, 1), lambda i, b: (i, 0)),
                pl.BlockSpec((QB, 1), lambda i, b: (i, 0)),
                full((1, length)), full((1, length)),
            ],
            out_specs=pl.BlockSpec((heads, QB, HD), lambda i, b: (0, i, 0)),
        ),
        out_shape=jax.ShapeDtypeStruct(q.shape, jnp.bfloat16),
        compiler_params=pltpu.CompilerParams(vmem_limit_bytes=VL),
        name="flash_fwd",
    )(base, q, k, v, docq, blkq, dock, blkk)

def flash_bwd_body(base_ref, q_ref, g_ref, k_ref, v_ref, docq_ref, blkq_ref, dock_ref, blkk_ref, dq_ref, dk_ref, dv_ref, *, share, length):
    step = pl.program_id(0)
    start = band_start(base_ref[0] + step * QB, length)
    keys = pl.ds(start, BAND)

    @pl.when(step == 0)
    def _():
        dk_ref[...] = jnp.zeros_like(dk_ref)
        dv_ref[...] = jnp.zeros_like(dv_ref)

    ok = (docq_ref[...] == dock_ref[keys, :]) & (blkk_ref[keys, :] <= blkq_ref[...])
    bias = jnp.where(ok, 0.0, masked_score)
    for head in range(q_ref.shape[0]):
        kvh = head // share
        q = q_ref[head]
        g = g_ref[head]
        k = k_ref[kvh, keys, :]
        s = nt(k, q) + bias
        e = jnp.exp(s - jnp.max(s, axis=0, keepdims=True))
        p = e * (1.0 / jnp.sum(e, axis=0, keepdims=True))
        dp = nt(v_ref[kvh, keys, :], g)
        delta = jnp.sum(dp * p, axis=0, keepdims=True)
        ds = (p * (dp - delta)).astype(jnp.bfloat16)
        dq_ref[head] = tn(ds, k)
        dk_ref[kvh, keys, :] += nn(ds, q)
        dv_ref[kvh, keys, :] += nn(p.astype(jnp.bfloat16), g)

def flash_bwd(base, q, g, k, v, docq, blkq, dock, blkk):
    heads, rows, _ = q.shape
    kv, length, _ = k.shape
    full = lambda shape: pl.BlockSpec(shape, lambda i, b: (0,) * len(shape))
    return pl.pallas_call(
        functools.partial(flash_bwd_body, share=heads // kv, length=length),
        grid_spec=pltpu.PrefetchScalarGridSpec(
            num_scalar_prefetch=1, grid=(rows // QB,),
            in_specs=[
                pl.BlockSpec((heads, QB, HD), lambda i, b: (0, i, 0)),
                pl.BlockSpec((heads, QB, HD), lambda i, b: (0, i, 0)),
                full(k.shape), full(v.shape),
                pl.BlockSpec((1, QB), lambda i, b: (0, i)),
                pl.BlockSpec((1, QB), lambda i, b: (0, i)),
                full((length, 1)), full((length, 1)),
            ],
            out_specs=[
                pl.BlockSpec((heads, QB, HD), lambda i, b: (0, i, 0)),
                full(k.shape), full(v.shape),
            ],
        ),
        out_shape=[
            jax.ShapeDtypeStruct(q.shape, jnp.float32),
            jax.ShapeDtypeStruct(k.shape, jnp.float32),
            jax.ShapeDtypeStruct(v.shape, jnp.float32),
        ],
        compiler_params=pltpu.CompilerParams(vmem_limit_bytes=VL),
        cost_estimate=busy(55),
        name="flash_bwd",
    )(base, q, g, k, v, docq, blkq, dock, blkk)

PAIR = 2
TM = 512

def moe_body(base_ref, x_ref, g_ref, xt_ref, gt_ref, gates_ref, prev_ref, w_ref, a_ref, gu_ref, grads_ref, dots_ref):
    rows, width = x_ref.shape
    shards, _, pair, part, ff = w_ref.shape
    step = pl.program_id(0)

    def weights(which):
        return jnp.concatenate(
            [jnp.concatenate([w_ref[z, which, e] for z in range(shards)], axis=0) for e in range(pair)], axis=1
        )

    gate_w = weights(0)
    up_w = weights(1)
    down_w = weights(2)
    experts = gates_ref.shape[1]
    lane = base_ref[0] + step * pair

    def tile(i, carry):
        here = pl.ds(pl.multiple_of(i * TM, TM), TM)
        x = x_ref[here, :]
        gate_val = nn(x, gate_w)
        up_val = nn(x, up_w)
        back = nn(g_ref[here, :], down_w)
        lanes = lax.broadcasted_iota(jnp.int32, (TM, experts), 1)
        gates = gates_ref[here, :]
        gate = jnp.concatenate(
            [
                jnp.broadcast_to(
                    jnp.sum(jnp.where(lanes == lane + e, gates, 0.0), axis=1, keepdims=True), (TM, ff)
                )
                for e in range(pair)
            ],
            axis=1,
        )
        sig = 1.0 / (1.0 + jnp.exp(-gate_val))
        silu = gate_val * sig
        inner = silu * up_val
        a_ref[here, :] = (inner * gate).astype(jnp.bfloat16)
        prod = inner * back
        dots = jnp.where(step == 0, prev_ref[here, :], dots_ref[here, :])
        for e in range(pair):
            total = jnp.sum(prod[:, e * ff : (e + 1) * ff], axis=1, keepdims=True)
            dots = jnp.where(lanes == lane + e, total, dots)
        dots_ref[here, :] = dots
        back = back * gate
        gu_ref[here, : pair * ff] = (back * up_val * sig * (1.0 + gate_val * (1.0 - sig))).astype(jnp.bfloat16)
        gu_ref[here, pair * ff :] = (back * silu).astype(jnp.bfloat16)
        return carry

    lax.fori_loop(0, rows // TM, tile, 0)
    for z in range(shards):
        part_rows = pl.ds(z * part, part)
        both = nn(xt_ref[part_rows, :], gu_ref[...])
        down = nn(gt_ref[part_rows, :], a_ref[...])
        for e in range(pair):
            grads_ref[z, 0, e] = both[:, e * ff : (e + 1) * ff].astype(jnp.bfloat16)
            grads_ref[z, 1, e] = both[:, (pair + e) * ff : (pair + e + 1) * ff].astype(jnp.bfloat16)
            grads_ref[z, 2, e] = down[:, e * ff : (e + 1) * ff].astype(jnp.bfloat16)

def moe_main(base, x, g, xt, gt, gates, dots, w):
    rows, width = x.shape
    shards, three, count, part, ff = w.shape
    one = lambda shape: pl.BlockSpec(shape, lambda i: (0,) * len(shape), pipeline_mode=pl.Buffered(1))
    return pl.pallas_call(
        moe_body,
        grid=(count // PAIR,),
        in_specs=[
            SMEMS, one(x.shape), one(g.shape), one(xt.shape), one(gt.shape), one(gates.shape), one(dots.shape),
            pl.BlockSpec((shards, 3, PAIR, part, ff), lambda i: (0, 0, i, 0, 0)),
        ],
        out_specs=[
            pl.BlockSpec((rows, PAIR * ff), lambda i: (0, i)),
            pl.BlockSpec((rows, 2 * PAIR * ff), lambda i: (0, i)),
            pl.BlockSpec((shards, 3, PAIR, part, ff), lambda i: (0, 0, i, 0, 0)),
            one(dots.shape),
        ],
        out_shape=[
            jax.ShapeDtypeStruct((rows, count * ff), jnp.bfloat16),
            jax.ShapeDtypeStruct((rows, 2 * count * ff), jnp.bfloat16),
            jax.ShapeDtypeStruct(w.shape, jnp.bfloat16),
            jax.ShapeDtypeStruct(dots.shape, jnp.float32),
        ],
        compiler_params=pltpu.CompilerParams(vmem_limit_bytes=VL),
        cost_estimate=pl.CostEstimate(flops=2 * rows * width * count * ff * 6, bytes_accessed=8 * rows * width + 12 * count * ff * width, transcendentals=0),
        name="moe_main",
        input_output_aliases={6: 3},
    )(base, x, g, xt, gt, gates, dots, w)

def back_body(*refs, count, first, kinds):
    gu_refs, w_refs, o_ref = refs[:count], refs[count : 2 * count], refs[2 * count]
    shards, _, experts, part, ff = w_refs[0].shape
    for z in range(shards):
        total = None
        for gu_ref, w_ref in zip(gu_refs, w_refs):
            w = jnp.concatenate(
                [
                    w_ref[z, kind, p * PAIR + e]
                    for p in range(experts // PAIR)
                    for kind in range(kinds)
                    for e in range(PAIR)
                ],
                axis=1,
            )
            piece = nt(gu_ref[...], w)
            total = piece if total is None else total + piece
        o_ref[:, z * part : (z + 1) * part] = total.astype(o_ref.dtype)


def moe_back(gus, ws, first, kinds):
    shards, three, experts, part, ff = ws[0].shape
    rows = gus[0].shape[0]
    width = shards * part
    count = len(gus)
    return pl.pallas_call(
        functools.partial(back_body, count=count, first=first, kinds=kinds),
        grid=(rows // TM,),
        in_specs=[pl.BlockSpec((TM, kinds * experts * ff), lambda i: (i, 0)) for _ in gus]
        + [
            pl.BlockSpec(
                (shards, kinds, experts, part, ff),
                lambda i: (0, first // kinds, 0, 0, 0),
                pipeline_mode=pl.Buffered(1),
            )
            for _ in ws
        ],
        out_specs=pl.BlockSpec((TM, width), lambda i: (i, 0)),
        out_shape=jax.ShapeDtypeStruct((rows, width), jnp.bfloat16),
        compiler_params=pltpu.CompilerParams(vmem_limit_bytes=VL),
        cost_estimate=pl.CostEstimate(
            flops=2 * rows * width * count * experts * ff * kinds,
            bytes_accessed=2 * rows * kinds * count * experts * ff,
            transcendentals=0,
        ),
        name="moe_back" if kinds == 2 else "moe_out",
    )(*gus, *ws)


MESH = pl.DeviceIdType.MESH


class Place:
    def __init__(self):
        self.ctx = lax.axis_index("ctx")
        self.tp = lax.axis_index("tp")
        self.core = lax.rem(self.tp, 2)
        self.high = self.tp // 2
        self.pair_tp = self.high * 2 + 1 - self.core
        self.far_tp = (1 - self.high) * 2 + self.core
        self.cross_tp = (1 - self.high) * 2 + 1 - self.core
        self.pair = {"tp": self.pair_tp}
        self.far = {"tp": self.far_tp}
        self.side = {"ctx": 1 - self.ctx}

    def meet(self, who):
        barrier = pltpu.get_barrier_semaphore()
        for device in who:
            pl.semaphore_signal(barrier, inc=1, device_id=device, device_id_type=MESH)
        pl.semaphore_wait(barrier, len(who))


def push(src, dst, sems, slot, device):
    return pltpu.make_async_remote_copy(
        src_ref=src, dst_ref=dst, send_sem=sems.at[0, slot], recv_sem=sems.at[1, slot],
        device_id=device, device_id_type=MESH,
    )


def gather_four(place, all_ref, sems, at):
    here, far = all_ref.at[place.tp], all_ref.at[place.far_tp]
    to_far = push(here, here, sems, at, place.far)
    to_pair = push(here, here, sems, at + 1, place.pair)
    to_far.start()
    to_pair.start()
    to_far.wait_recv()
    on = push(far, far, sems, at + 2, place.pair)
    on.start()
    to_pair.wait_recv()
    on.wait_recv()
    to_far.wait_send()
    to_pair.wait_send()
    on.wait_send()


def gather_eight(place, all_ref, sems, at):
    rows = all_ref.shape[1]
    top, low = pl.ds(0, rows // 2), pl.ds(rows // 2, rows // 2)
    part = lambda ctx, tp: all_ref.at[ctx * 4 + tp]
    other = 1 - place.ctx
    here = part(place.ctx, place.tp)
    side = part(other, place.tp)
    far = part(place.ctx, place.far_tp)
    cross = part(other, place.far_tp)
    side_top, far_low = side.at[top], far.at[low]
    cross_top, cross_low = cross.at[top], cross.at[low]
    to_side = push(here, here, sems, at, place.side)
    to_far = push(here, here, sems, at + 1, place.far)
    to_pair = push(here, here, sems, at + 2, place.pair)
    for copy in (to_side, to_far, to_pair):
        copy.start()
    to_side.wait_recv()
    turn_far = push(side_top, side_top, sems, at + 3, place.far)
    pair_side = push(side, side, sems, at + 5, place.pair)
    turn_far.start()
    pair_side.start()
    to_far.wait_recv()
    turn_side = push(far_low, far_low, sems, at + 4, place.side)
    pair_far = push(far, far, sems, at + 6, place.pair)
    turn_side.start()
    pair_far.start()
    turn_far.wait_recv()
    pair_top = push(cross_top, cross_top, sems, at + 7, place.pair)
    pair_top.start()
    turn_side.wait_recv()
    pair_low = push(cross_low, cross_low, sems, at + 8, place.pair)
    pair_low.start()
    for copy in (to_pair, pair_side, pair_far, pair_top, pair_low):
        copy.wait_recv()
    for copy in (to_side, to_far, to_pair, turn_far, turn_side, pair_side, pair_far, pair_top, pair_low):
        copy.wait_send()


def reduce_four(place, produce, send_ref, pair_in, far_in, own_ref, sems, at):
    def fold(j):
        slot = j // 2

        @pl.when(lax.rem(j, 2) == place.core)
        def _():
            push(send_ref.at[j], pair_in.at[slot], sems, at + slot, place.pair).wait_recv()
            total = send_ref[j].astype(jnp.float32) + pair_in[slot].astype(jnp.float32)

            @pl.when(slot == place.high)
            def _():
                own_ref[...] = total

            @pl.when(slot != place.high)
            def _():
                send_ref[j] = total.astype(jnp.bfloat16)
                push(send_ref.at[j], far_in, sems, at + 2, place.far).start()

    def step(j, carry):
        produce(j)

        @pl.when(lax.rem(j, 2) != place.core)
        def _():
            slot = j // 2
            push(send_ref.at[j], pair_in.at[slot], sems, at + slot, place.pair).start()

        @pl.when(j > 0)
        def _():
            fold(j - 1)

        return carry

    lax.fori_loop(0, 4, step, 0)
    fold(3)
    last = push(send_ref.at[place.far_tp], far_in, sems, at + 2, place.far)
    last.wait_recv()
    own_ref[...] += far_in[...].astype(jnp.float32)
    last.wait_send()
    for slot in range(2):
        push(send_ref.at[place.pair_tp], pair_in.at[slot], sems, at + slot, place.pair).wait_send()


SMEMS = pl.BlockSpec(memory_space=pltpu.SMEM)
WHOLE = pl.BlockSpec(memory_space=pltpu.VMEM)


def normalize(x):
    r = lax.rsqrt(jnp.mean(x * x, axis=1, keepdims=True) + epsilon)
    return r, x * r


def mid_body(tok_ref, q_ref, k_ref, v_ref, docq_ref, blkq_ref, dock_ref, blkk_ref, w_ref, gain_ref,
             mix_ref, hid_ref, all_ref, whole_ref, send, pair_in, far_in, own, sems, w_sems, *, share, length):
    place = Place()
    shards, part, _ = whole_ref.shape
    z = lax.axis_index("fsdp")
    others = [{"fsdp": lax.rem(z + d, shards)} for d in range(1, shards)]
    place.meet((place.pair, place.far, place.side, *others))
    spread = [push(w_ref, whole_ref.at[z], w_sems, d, device) for d, device in enumerate(others)]
    for copy in spread:
        copy.start()
    whole_ref[z] = w_ref[...]
    heads, rows, _ = q_ref.shape
    block = rows // 4
    band = min(DOC + block + BLK, length)

    def produce(j):
        at = pl.multiple_of(j * block, block)
        here = pl.ds(at, block)
        start = pl.multiple_of(jnp.clip(place.ctx * rows + at - DOC, 0, length - band), 128)
        keys = pl.ds(start, band)
        ok = (docq_ref[here, :] == dock_ref[:, keys]) & (blkk_ref[:, keys] <= blkq_ref[here, :])
        bias = jnp.where(ok, 0.0, masked_score)
        outs = []
        for head in range(heads):
            s = nt(q_ref[head, here, :], k_ref[head // share, keys, :]) + bias
            e = jnp.exp(s - jnp.max(s, axis=1, keepdims=True))
            p = e * (1.0 / jnp.sum(e, axis=1, keepdims=True))
            outs.append(nn(p.astype(jnp.bfloat16), v_ref[head // share, keys, :]).astype(jnp.bfloat16))
        mix = jnp.concatenate(outs, axis=1)
        mix_ref[here, :] = mix

        @pl.when(j == 0)
        def _():
            for copy in spread:
                copy.wait_recv()

        for n in range(shards):
            send[j, :, n * part : (n + 1) * part] = nt(mix, whole_ref[n]).astype(jnp.bfloat16)

    reduce_four(place, produce, send, pair_in, far_in, own, sems, 0)
    hidden = tok_ref[...].astype(jnp.float32) + own[...]
    hid_ref[...] = hidden
    all_ref[place.ctx * 4 + place.tp] = (normalize(hidden)[1] * gain_ref[...]).astype(jnp.bfloat16)
    gather_eight(place, all_ref, sems, 3)
    for copy in spread:
        copy.wait_send()


def mid(tok, q, k, v, docq, blkq, dock, blkk, out_w, gain):
    heads, rows, _ = q.shape
    kv, length, _ = k.shape
    own, width = tok.shape
    part = out_w.shape[0]
    shards = width // part
    return pl.pallas_call(
        functools.partial(mid_body, share=heads // kv, length=length),
        in_specs=[WHOLE] * 10,
        out_specs=[WHOLE] * 4,
        out_shape=[
            jax.ShapeDtypeStruct((rows, heads * HD), jnp.bfloat16),
            jax.ShapeDtypeStruct((own, width), jnp.float32),
            jax.ShapeDtypeStruct((8, own, width), jnp.bfloat16),
            jax.ShapeDtypeStruct((shards, *out_w.shape), jnp.bfloat16),
        ],
        scratch_shapes=[
            pltpu.VMEM((4, own, width), jnp.bfloat16),
            pltpu.VMEM((2, own, width), jnp.bfloat16),
            pltpu.VMEM((own, width), jnp.bfloat16),
            pltpu.VMEM((own, width), jnp.float32),
            pltpu.SemaphoreType.DMA((2, 12)),
            pltpu.SemaphoreType.DMA((2, shards - 1)),
        ],
        compiler_params=pltpu.CompilerParams(vmem_limit_bytes=VL, collective_id=0, has_side_effects=True),
        cost_estimate=busy(100),
        name="mid",
    )(tok, q, k, v, docq, blkq, dock, blkk, out_w, gain)


def tail_body(tok_ref, hg_ref, lin_ref, w_ref, gain_ref, small_ref, all_ref, sum_ref,
              send, pair_in, far_in, own, mine, theirs, split, split_in, sems, small_sems, *, shards):
    place = Place()
    z = lax.axis_index("fsdp")
    others = [{"fsdp": lax.rem(z + d, shards)} for d in range(1, shards)]
    place.meet((place.pair, place.far, place.side, *others))
    block = lin_ref.shape[0] // 4
    part = sum_ref.shape[1]

    def produce(j):
        here = pl.ds(pl.multiple_of(j * block, block), block)
        send[j] = nt(lin_ref[here, :], w_ref[...]).astype(jnp.bfloat16)

    reduce_four(place, produce, send, pair_in, far_in, own, sems, 0)
    one_grad = own[...]
    r, xhat = normalize(tok_ref[...].astype(jnp.float32))
    n = one_grad * gain_ref[...]
    grad = hg_ref[...] + r * (n - xhat * jnp.mean(n * xhat, axis=1, keepdims=True))
    all_ref[place.tp] = grad.astype(jnp.bfloat16)
    row = lax.broadcasted_iota(jnp.int32, small_ref.shape, 0)
    mine[0] = jnp.where(
        row == small_ref.shape[0] - 1, jnp.sum(one_grad * xhat, axis=0, keepdims=True), small_ref[...]
    )
    hops = [
        push(mine.at[i], theirs.at[i], small_sems, i, device)
        for i, device in enumerate((place.pair, place.side, place.far))
    ]
    hops[0].start()
    here, far = all_ref.at[place.tp], all_ref.at[place.far_tp]
    to_far = push(here, here, sems, 3, place.far)
    to_pair = push(here, here, sems, 4, place.pair)
    to_far.start()
    to_pair.start()
    for i in range(2):
        hops[i].wait_recv()
        mine[i + 1] = mine[i] + theirs[i]
        hops[i + 1].start()
    to_far.wait_recv()
    on = push(far, far, sems, 5, place.pair)
    on.start()
    hops[2].wait_recv()
    total = mine[2] + theirs[2]
    for j in range(shards):
        split[j] = total[:, j * part : (j + 1) * part]
    spread = [
        push(split.at[lax.rem(z + d, shards)], split_in.at[d - 1], small_sems, 2 + d, others[d - 1])
        for d in range(1, shards)
    ]
    for copy in spread:
        copy.start()
    to_pair.wait_recv()
    on.wait_recv()
    result = split[z]
    for d in range(1, shards):
        spread[d - 1].wait_recv()
        result = result + split_in[d - 1]
    sum_ref[...] = result
    for copy in (to_far, to_pair, on, *hops, *spread):
        copy.wait_send()


def tail(tok, hidden_grad, lin_grad, qkv_w, gain, small, shards):
    own, width = tok.shape
    count = small.shape[0]
    part = width // shards
    return pl.pallas_call(
        functools.partial(tail_body, shards=shards),
        in_specs=[WHOLE] * 6,
        out_specs=[WHOLE] * 2,
        out_shape=[
            jax.ShapeDtypeStruct((4, own, width), jnp.bfloat16),
            jax.ShapeDtypeStruct((count, part), jnp.float32),
        ],
        scratch_shapes=[
            pltpu.VMEM((4, own, width), jnp.bfloat16),
            pltpu.VMEM((2, own, width), jnp.bfloat16),
            pltpu.VMEM((own, width), jnp.bfloat16),
            pltpu.VMEM((own, width), jnp.float32),
            pltpu.VMEM((3, count, width), jnp.float32),
            pltpu.VMEM((3, count, width), jnp.float32),
            pltpu.VMEM((shards, count, part), jnp.float32),
            pltpu.VMEM((shards - 1, count, part), jnp.float32),
            pltpu.SemaphoreType.DMA((2, 6)),
            pltpu.SemaphoreType.DMA((2, 2 + shards)),
        ],
        compiler_params=pltpu.CompilerParams(vmem_limit_bytes=VL, collective_id=1, has_side_effects=True),
        cost_estimate=busy(50),
        name="tail",
    )(tok, hidden_grad, lin_grad, qkv_w, gain, small)


def turn_body(*refs, count, kinds, first, finish):
    gu_refs, w_refs = refs[:count], refs[count : 2 * count]
    lg_ref, router_ref, hid_ref, extra_ref, gain_ref = refs[2 * count : 2 * count + 5]
    outs = refs[2 * count + 5 : 2 * count + 8]
    gu_buf, gu_sem, give, keep, pair_in, cut, own, sems = refs[2 * count + 8 :]
    all_ref = outs[0]
    place = Place()
    place.meet((place.pair, place.far, place.side))
    block = hid_ref.shape[0]
    shards, _, experts, part, ff = w_refs[0].shape
    half = block // 2
    top, low = pl.ds(0, half), pl.ds(half, half)
    bf = jnp.bfloat16
    f = jnp.float32
    order = [(1, 1), (1, 0), (0, 1), (0, 0)]

    def tile_of(step):
        dx, dy = order[step // 2]
        ctx = place.ctx + dx * (1 - 2 * place.ctx)
        high = place.high + dy * (1 - 2 * place.high)
        core = 1 - place.core if step % 2 == 0 else place.core
        return ctx * 4 + high * 2 + core

    def fetch(step):
        at = pl.ds(pl.multiple_of(tile_of(step) * block, block), block)
        return [
            pltpu.make_async_copy(gu.at[at, :], gu_buf.at[step % 2, n], gu_sem.at[step % 2, n])
            for n, gu in enumerate(gu_refs)
        ]

    for copy in fetch(0):
        copy.start()

    def compute(step, dst):
        for copy in fetch(step):
            copy.wait()
        if step + 1 < 8:
            for copy in fetch(step + 1):
                copy.start()
        at = pl.ds(pl.multiple_of(tile_of(step) * block, block), block)
        for z in range(shards):
            cols = slice(z * part, (z + 1) * part)
            total = None
            if lg_ref is not None:
                total = nt(lg_ref[at, :], router_ref[cols, :])
            for n, w_ref in enumerate(w_refs):
                w = jnp.concatenate(
                    [
                        w_ref[z, kind, p * PAIR + e]
                        for p in range(experts // PAIR)
                        for kind in range(kinds)
                        for e in range(PAIR)
                    ],
                    axis=1,
                )
                piece = nt(gu_buf[step % 2, n], w)
                total = piece if total is None else total + piece
            dst[:, cols] = total.astype(bf)

    copies = []

    def send(src, dst, slot, device):
        copy = push(src, dst, sems, slot, device)
        copy.start()
        copies.append(copy)
        return copy

    for k in range(4):
        compute(2 * k, give.at[k])
        got = send(give.at[k], pair_in.at[k], k, place.pair)
        compute(2 * k + 1, keep.at[k])
        got.wait_recv()
        total = keep[k].astype(f) + pair_in[k].astype(f)
        if k == 0:
            keep[k] = total.astype(bf)
            a_cross = send(keep.at[k, top], cut.at[0], 4, place.side)
            b_cross = send(keep.at[k, low], cut.at[1], 5, place.far)
        elif k == 1:
            b_cross.wait_recv()
            keep[k, top] = total[:half].astype(bf)
            keep[k, low] = (total[half:] + cut[1].astype(f)).astype(bf)
            a_first = send(keep.at[k, top], cut.at[2], 6, place.side)
            b_last = send(keep.at[k, low], cut.at[5], 9, place.side)
        elif k == 2:
            a_cross.wait_recv()
            keep[k, low] = total[half:].astype(bf)
            keep[k, top] = (total[:half] + cut[0].astype(f)).astype(bf)
            b_first = send(keep.at[k, low], cut.at[4], 8, place.far)
            a_last = send(keep.at[k, top], cut.at[3], 7, place.far)
        else:
            for copy in (a_first, a_last, b_first, b_last):
                copy.wait_recv()
            own[top, :] = total[:half] + cut[2].astype(f) + cut[3].astype(f)
            own[low, :] = total[half:] + cut[4].astype(f) + cut[5].astype(f)
    finish(place, own, hid_ref, extra_ref, gain_ref, outs)
    gather_four(place, all_ref, sems, 10)
    for copy in copies:
        copy.wait_send()


def turn_back(place, own, hid_ref, grad_ref, gain_ref, outs):
    all_ref, hg_ref, gg_ref = outs
    two_grad = own[...]
    r, hhat = normalize(hid_ref[...])
    gg_ref[...] = jnp.sum(two_grad * hhat, axis=0, keepdims=True)
    m = two_grad * gain_ref[...]
    grad = grad_ref[...].astype(jnp.float32) + r * (m - hhat * jnp.mean(m * hhat, axis=1, keepdims=True))
    hg_ref[...] = grad
    all_ref[place.tp] = grad.astype(jnp.bfloat16)


def turn(gus, ws, logit_grad, router_w, hidden, grad_own, gain):
    shards, _, experts, part, ff = ws[0].shape
    own, width = hidden.shape
    count = len(gus)
    kinds = 2
    cols = gus[0].shape[1]
    anys = pl.BlockSpec(memory_space=pl.ANY)
    return pl.pallas_call(
        functools.partial(turn_body, count=count, kinds=kinds, first=0, finish=turn_back),
        grid=(1,),
        in_specs=[anys] * count
        + [
            pl.BlockSpec((shards, kinds, experts, part, ff), lambda i: (0, 0, 0, 0, 0), pipeline_mode=pl.Buffered(1))
            for _ in ws
        ]
        + [WHOLE] * 5,
        out_specs=[WHOLE] * 3,
        out_shape=[
            jax.ShapeDtypeStruct((4, own, width), jnp.bfloat16),
            jax.ShapeDtypeStruct((own, width), jnp.float32),
            jax.ShapeDtypeStruct((1, width), jnp.float32),
        ],
        scratch_shapes=[
            pltpu.VMEM((2, count, own, cols), jnp.bfloat16),
            pltpu.SemaphoreType.DMA((2, count)),
            pltpu.VMEM((4, own, width), jnp.bfloat16),
            pltpu.VMEM((4, own, width), jnp.bfloat16),
            pltpu.VMEM((4, own, width), jnp.bfloat16),
            pltpu.VMEM((6, own // 2, width), jnp.bfloat16),
            pltpu.VMEM((own, width), jnp.float32),
            pltpu.SemaphoreType.DMA((2, 13)),
        ],
        compiler_params=pltpu.CompilerParams(vmem_limit_bytes=VL, collective_id=2, has_side_effects=True),
        cost_estimate=busy(75),
        name="turn",
    )(*gus, *ws, logit_grad, router_w, hidden, grad_own, gain)


def place_body(ctx_ref, *refs, chunks, turned):
    own_refs, other_refs, outs = refs[:chunks], refs[chunks : 2 * chunks], refs[2 * chunks :]
    ctx = ctx_ref[0]
    for chunk in range(chunks):
        for half, piece in ((ctx, own_refs[chunk]), (1 - ctx, other_refs[chunk])):
            for kind in range(3):
                value = piece[kind, 0].astype(jnp.float32)
                outs[kind][half, chunk, 0] = value.T if kind == 2 and turned else value


def place_shards(ctx, own, other):
    _, each, part, ff = own[0].shape
    chunks = len(own)
    turned = part % 128 == 0
    shapes = [(part, ff), (part, ff), (ff, part) if turned else (part, ff)]
    outs = pl.pallas_call(
        functools.partial(place_body, chunks=chunks, turned=turned),
        grid=(each,),
        in_specs=[SMEMS] + [pl.BlockSpec((3, 1, part, ff), lambda e: (0, e, 0, 0))] * (2 * chunks),
        out_specs=[pl.BlockSpec((2, chunks, 1, *shape), lambda e: (0, 0, e, 0, 0)) for shape in shapes],
        out_shape=[jax.ShapeDtypeStruct((2, chunks, each, *shape), jnp.float32) for shape in shapes],
        compiler_params=pltpu.CompilerParams(vmem_limit_bytes=VL),
        cost_estimate=busy(8),
        name="place_shards",
    )(ctx.astype(jnp.int32).reshape(1), *own, *other)
    gate, up, down = [out.reshape(2 * chunks * each, *out.shape[3:]) for out in outs]
    return gate, up, down if turned else down.transpose(0, 2, 1)


from jax.sharding import PartitionSpec as P

rope_base = 10000.0
CHUNKS = 4
bf16 = jnp.bfloat16
f32 = jnp.float32


def rope_tables(positions):
    half = HD // 2
    frequency = rope_base ** (-2.0 * jnp.arange(half, dtype=f32) / HD)
    angles = positions.astype(f32)[:, None] * frequency[None, :]
    return jnp.cos(angles)[:, None, :], jnp.sin(angles)[:, None, :]


def busy(us):
    return pl.CostEstimate(flops=int(us * 1e9), bytes_accessed=1 << 20, transcendentals=0)


def swap(x):
    return lax.ppermute(x, "ctx", [(0, 1), (1, 0)])


def after(x, *done):
    return lax.optimization_barrier((x, *done))


def rotate(values, cosine, sine):
    shaped = values.reshape(values.shape[0], -1, HD)
    a, b = shaped[:, :, : HD // 2], shaped[:, :, HD // 2 :]
    return jnp.concatenate([a * cosine - b * sine, b * cosine + a * sine], axis=2)


def per_device(
    tokens, out_grad, doc_ids, block_ids, expert_ids, norm1_gain, w_query, w_key, w_value, w_out,
    norm2_gain, w_router, w_gate, w_up, w_down,
):
    shards = lax.axis_size("fsdp")
    ctx_size = lax.axis_size("ctx")
    tp_size = lax.axis_size("tp")
    ctx = lax.axis_index("ctx")
    tp = lax.axis_index("tp")
    rows, width = tokens.shape
    part = width // shards
    own = rows // tp_size
    length = doc_ids.shape[0]
    q_width, kv_width = w_query.shape[1], w_key.shape[1]
    heads, kv_heads = q_width // HD, kv_width // HD
    experts = w_gate.shape[0]
    mine = experts // ctx_size
    each = mine // CHUNKS
    ff = w_gate.shape[2]

    columns = q_width + 2 * kv_width
    extra = jnp.concatenate([norm1_gain, norm2_gain, w_router.reshape(-1)])
    extra_rows = -(-extra.shape[0] // (8 * columns)) * 8
    extra = jnp.pad(extra, (0, extra_rows * columns - extra.shape[0])).reshape(extra_rows, columns)
    front = jnp.concatenate([jnp.concatenate([w_query, w_key, w_value], axis=1), extra], axis=0)
    front = lax.all_gather(front, "fsdp", axis=0)
    ordered = lambda here, there, axis=0: jnp.concatenate(
        [jnp.where(ctx == 0, here, there), jnp.where(ctx == 0, there, here)], axis=axis
    )
    shard_list = []
    for chunk in range(CHUNKS):
        first = ctx * mine + chunk * each
        pick = lambda w: lax.dynamic_slice_in_dim(w, first, each, 0)
        shard_list.append(jnp.stack([pick(w_gate), pick(w_up), pick(w_down).transpose(0, 2, 1)]))
    front, *shard_list = after(front, *shard_list)
    qkv_w = front[:, :part].reshape(width, columns)
    extra = front[:, part:].reshape(shards, extra_rows * columns)
    gain_one = extra[:, :part].reshape(width).astype(f32)
    gain_two = extra[:, part : 2 * part].reshape(width).astype(f32)
    router_w = extra[:, 2 * part : (2 + experts) * part].reshape(width, experts)

    stacked = [lax.all_gather(shard, "fsdp", axis=0) for shard in shard_list]
    ids_all = ordered(expert_ids, swap(expert_ids))

    inputs = tokens.astype(f32)
    rms_one = lax.rsqrt(jnp.mean(inputs * inputs, axis=1, keepdims=True) + epsilon)
    normed = (inputs * rms_one * gain_one).astype(bf16)
    start = ctx * rows
    cosine, sine = rope_tables(start + jnp.arange(rows, dtype=jnp.int32))
    kv_lin = jnp.dot(normed, qkv_w[:, q_width:], preferred_element_type=f32)
    keys_values = jnp.concatenate(
        [rotate(kv_lin[:, :kv_width], cosine, sine).reshape(rows, kv_width), kv_lin[:, kv_width:]], axis=1
    ).astype(bf16)
    queries = rotate(jnp.dot(normed, qkv_w[:, :q_width], preferred_element_type=f32), cosine, sine)
    queries = queries.astype(bf16).transpose(1, 0, 2) * bf16(HD**-0.5)
    near = min(DOC, rows)
    apart = lambda x: jnp.where(
        ctx == 0, jnp.pad(x, ((0, rows - near), (0, 0))), jnp.pad(x, ((rows - near, 0), (0, 0)))
    )
    window = lax.dynamic_slice_in_dim(keys_values, jnp.where(ctx == 0, rows - near, 0), near)
    keys_values = ordered(keys_values, apart(swap(window)))
    grad_here, keys_values = after(out_grad, keys_values)
    grad_all = ordered(grad_here, swap(grad_here))
    keys_values = keys_values.reshape(length, 2 * kv_heads, HD).transpose(1, 0, 2)
    keys, values = keys_values[:kv_heads], keys_values[kv_heads:]
    query_doc = lax.dynamic_slice_in_dim(doc_ids, start, rows)
    query_block = lax.dynamic_slice_in_dim(block_ids, start, rows)
    base = start.astype(jnp.int32).reshape(1)
    tokens_own = lax.dynamic_slice_in_dim(tokens, tp * own, own)
    grad_own = lax.dynamic_slice_in_dim(out_grad, tp * own, own)
    attn_mix, hidden, normed_two, out_w = mid(
        tokens_own, queries, keys, values, query_doc[:, None], query_block[:, None], doc_ids[None],
        block_ids[None], w_out.T, gain_two[None],
    )
    out_w = out_w.reshape(width, q_width)
    normed_two = normed_two.reshape(ctx_size * rows, width)

    logits = jnp.dot(normed_two, router_w, preferred_element_type=f32)
    chosen = jnp.any(ids_all[:, :, None] == jnp.arange(experts, dtype=jnp.int32)[None, None, :], axis=1)
    masked = jnp.where(chosen, logits, masked_score)
    powers = jnp.exp(masked - jnp.max(masked, axis=1, keepdims=True))
    gates = powers / jnp.sum(powers, axis=1, keepdims=True)

    normed_t, grad_t = normed_two.T, grad_all.T
    inner_all, outer_all, shard_grads = [], [], []
    dots = jnp.zeros_like(gates)
    for chunk in range(CHUNKS):
        inner, outer, grads, dots = moe_main(
            (ctx * mine + chunk * each).astype(jnp.int32).reshape(1),
            normed_two, grad_all, normed_t, grad_t, gates, dots, stacked[chunk],
        )
        inner_all.append(inner)
        outer_all.append(outer)
        shard_grads.append(lax.psum_scatter(grads, "fsdp", scatter_dimension=0, tiled=False))
    combined = moe_back(inner_all, stacked, 2, 1)

    weighted = gates * dots
    dots_sum = jnp.sum(weighted, axis=1, keepdims=True)
    logit_grad = (weighted - gates * dots_sum).astype(bf16)
    router_grad = lax.dot_general(
        logit_grad, normed_two, (((0,), (0,)), ((), ())), preferred_element_type=f32
    )
    grad_own, shard_grads[0] = after(grad_own, shard_grads[0])
    branch_grad, hidden_grad, gain_two_grad = turn(
        outer_all, stacked, logit_grad, router_w, hidden, grad_own, gain_two[None]
    )
    branch_grad, *first = after(branch_grad, *shard_grads[:3])
    there = [swap(piece) for piece in first]
    branch_grad = branch_grad.reshape(rows, width)

    out_w_grad = lax.dot_general(
        branch_grad, attn_mix, (((0,), (0,)), ((), ())), preferred_element_type=f32
    )
    mix_grad = jnp.dot(branch_grad, out_w, preferred_element_type=f32).astype(bf16)
    query_grad, key_grad, value_grad = flash_bwd(
        base, queries, mix_grad.reshape(rows, heads, HD).transpose(1, 0, 2), keys, values,
        query_doc[None], query_block[None], doc_ids[:, None], block_ids[:, None],
    )
    query_grad, key_grad, value_grad, *there = after(query_grad, key_grad, value_grad, *there)
    kv_grad = jnp.concatenate([key_grad, value_grad], axis=0).transpose(1, 0, 2).reshape(length, 2 * kv_width)
    kv_grad = kv_grad.astype(bf16)
    kept = lax.dynamic_slice_in_dim(kv_grad, start, rows)
    given = lax.dynamic_slice_in_dim(kv_grad, jnp.where(ctx == 0, rows, rows - near), near)
    got = swap(given)
    got = jnp.where(
        ctx == 0, jnp.pad(got, ((rows - near, 0), (0, 0))), jnp.pad(got, ((0, rows - near), (0, 0)))
    )
    kv_grad = kept.astype(f32) + got.astype(f32)
    kv_grad, last = after(kv_grad, shard_grads[3])
    there.append(swap(last))
    query_grad = (query_grad * HD**-0.5).transpose(1, 0, 2).reshape(rows, q_width)
    turned_grad = rotate(
        jnp.concatenate([query_grad, kv_grad[:, :kv_width]], axis=1), cosine, -sine
    ).reshape(rows, q_width + kv_width)
    lin_grad = jnp.concatenate([turned_grad, kv_grad[:, kv_width:]], axis=1).astype(bf16)
    qkv_grad = lax.dot_general(normed, lin_grad, (((0,), (0,)), ((), ())), preferred_element_type=f32)

    small_grads = jnp.concatenate(
        [router_grad, gain_two_grad, jnp.zeros((8 - (experts + 1) % 8, width), f32)], axis=0
    )
    input_grad, small_grads = tail(
        tokens_own, hidden_grad, lin_grad, qkv_w, gain_one[None], small_grads, shards
    )
    input_grad = input_grad.reshape(rows, width)
    hidden, small_grads, there[-1] = after(hidden, small_grads, there[-1])
    mixed = lax.psum_scatter(combined, ("ctx", "tp"), scatter_dimension=0, tiled=True)
    block_out = lax.all_gather((hidden + mixed.astype(f32)).astype(bf16), "tp", axis=0, tiled=True)

    big = jnp.concatenate([qkv_grad, out_w_grad], axis=1).astype(bf16)
    big = lax.psum_scatter(big, "fsdp", scatter_dimension=0, tiled=True)
    big = big.astype(f32) + swap(big).astype(f32)
    gate_s, up_s, down_s = place_shards(ctx, shard_grads, there)
    at = q_width + 2 * kv_width
    return (
        block_out,
        input_grad,
        small_grads[-1],
        big[:, :q_width],
        big[:, q_width : q_width + kv_width],
        big[:, q_width + kv_width : at],
        big[:, at : at + q_width].T,
        small_grads[experts],
        small_grads[:experts].T,
        gate_s,
        up_s,
        down_s,
    )


def solution(mesh):
    rows = P(("fsdp", "ctx"), None)
    return jax.shard_map(
        per_device,
        mesh=mesh,
        in_specs=(
            rows, rows, P("fsdp"), P("fsdp"), rows, P("fsdp"), P("fsdp", "tp"), P("fsdp", "tp"),
            P("fsdp", "tp"), P("tp", "fsdp"), P("fsdp"), P("fsdp", None), P(None, "fsdp", "tp"),
            P(None, "fsdp", "tp"), P(None, "tp", "fsdp"),
        ),
        out_specs=(
            rows, rows, P("fsdp"), P("fsdp", "tp"), P("fsdp", "tp"), P("fsdp", "tp"), P("tp", "fsdp"),
            P("fsdp"), P("fsdp", None), P(None, "fsdp", "tp"), P(None, "fsdp", "tp"), P(None, "tp", "fsdp"),
        ),
        check_vma=False,
    )
```
